32 devices in a mesh: row: 8 (over z, y), rep: 4 (over x, core).
Axes of the slice: x: 2, y: 2, z: 4, core: 2. Of those that a mesh axis runs over, the one named last changes fastest.
Arguments:
- params: float32 [59, 32768], P(None, 'row'), may hold values from -6 to 6, as said below
- first_moment: float32 [59, 32768], P(None, 'row'), may hold values from -6 to 6
- second_moment: float32 [59, 32768], P(None, 'row'), may hold values from 0.01 to 1
- camera: float32 [2, 4, 11], P(None, 'rep'), may hold values from -200 to 200, as said below
- tile_corner: float32 [2, 4, 32, 2], P(None, 'rep', 'row'), may hold values from 0 to 240
- tile_owner: int32 [2, 4, 32, 4], P(None, 'rep', 'row'), may hold values from 0 to 7, all different within a row; in each aligned block of 4 rows (0 to 3, 4 to 7, ..., all dimensions but the last counted through in order) at most 4 rows name the same one
- tile_block: int32 [2, 4, 32, 4], P(None, 'rep', 'row'), may hold values from 0 to 31
- depth_order: int32 [2, 4, 32, 512], P(None, 'rep', 'row'), may hold values from 0 to 511, each once within a row
- targets: float32 [2, 4, 32, 3, 256], P(None, 'rep', 'row'), may hold values from 0 to 1
- migration: int32 [8, 2, 2], P('row'), may hold values from 0 to 31, as said below
Outputs:
- new_params: float32 [59, 32768], P(None, 'row')
- new_first: float32 [59, 32768], P(None, 'row')
- new_second: float32 [59, 32768], P(None, 'row')
- rendered: float32 [2, 4, 32, 3, 256], P(None, 'rep', 'row')
The draws below stay inside these ranges and needn't reach their ends.
Inputs may be any that keep to these rules, and one draw needn't show every extreme that they name: `tile_owner`: each tile names 4 different owners; among the tiles of one device no owner is named more than 4 times. `depth_order`: each tile's row is a permutation. `migration`: the (4) entries of one owner are different blocks. `params`: row 6 lies in [1, 2]; rows 3 to 5 in [-1.9, -0.7]; row 10 in [2, 4]. `camera`: entries 8 to 10 form a unit vector.
All inputs are finite; a program needn't handle non-finite values.
Results may differ from the reference program's by a relative error of at most 0.0003.
Values sent between devices are 32-bit elements; how exact they have to be, the bound alone decides.
No kernel may reach another device: no remote copies, remote signals or barrier semaphores. Data moves between devices by JAX's collectives and lax.ppermute only.
A program may use at most 64 MiB of HBM per device.

```python
import math
import jax
import jax.numpy as jnp
import numpy as np
from jax import lax

P_SIZE = 59
BLOCK = 128
LISTB = 4
PIX = 256
ITERS = 2
MIGH = 2
TILES_DEV = 4
BLK_DEV = 32
DEPTH = 512
OWNERS = 8
REPLICAS = 4
TILES = 32
GAUSS = 32768
CAP = 4


def draw_params(key, part):
    subkeys = jax.random.split(jax.random.fold_in(key, 101), 7)
    gauss_count = GAUSS
    means = jax.random.uniform(subkeys[0], (3, gauss_count), jnp.float32, -1.0, 1.0)
    log_scales = jax.random.uniform(subkeys[1], (3, gauss_count), jnp.float32, -1.9, -0.7)
    quat_real = jax.random.uniform(subkeys[2], (1, gauss_count), jnp.float32, 1.0, 2.0)
    quat_rest = jax.random.uniform(subkeys[3], (3, gauss_count), jnp.float32, -1.0, 1.0)
    logits = jax.random.uniform(subkeys[4], (1, gauss_count), jnp.float32, 2.0, 4.0)
    base_colour = jax.random.normal(subkeys[5], (3, gauss_count), jnp.float32)
    higher = 0.5 * jax.random.normal(subkeys[6], (45, gauss_count), jnp.float32)
    colour_rows = jnp.clip(jnp.concatenate([base_colour, higher], axis=0), -6.0, 6.0)
    return jnp.concatenate([means, log_scales, quat_real, quat_rest, logits, colour_rows], axis=0)


def draw_camera(key, part):
    subkeys = jax.random.split(jax.random.fold_in(key, 202), 4)
    affine = jnp.clip(50.0 * jax.random.normal(subkeys[0], (ITERS, REPLICAS, 6), jnp.float32), -200.0, 200.0)
    centre = 128.0 + jnp.clip(20.0 * jax.random.normal(subkeys[1], (ITERS, REPLICAS, 2), jnp.float32), -60.0, 60.0)
    height = jax.random.uniform(subkeys[2], (ITERS, REPLICAS, 1), jnp.float32, -1.0, 1.0)
    turning = jax.random.uniform(subkeys[3], (ITERS, REPLICAS, 1), jnp.float32, -jnp.pi, jnp.pi)
    radial = jnp.sqrt(1.0 - height * height)
    facing = jnp.concatenate([radial * jnp.cos(turning), radial * jnp.sin(turning), height], axis=-1)
    return jnp.concatenate([affine, centre, facing], axis=-1)


def draw_migration(key, part):
    subkeys = jax.random.split(jax.random.fold_in(key, 303), OWNERS)
    picks = jax.vmap(lambda k: jax.random.permutation(k, BLK_DEV)[:2 * MIGH])(subkeys)
    return picks.reshape(OWNERS, 2, MIGH).astype(jnp.int32)


def place_ends(result, rng, least, top_value):
    place = [jax.random.randint(jax.random.fold_in(rng, axis), (), 0, length) for axis, length in enumerate(result.shape)]
    main_axis = result.shape.index(max(result.shape))
    beside = place[:main_axis] + [(place[main_axis] + 1) % result.shape[main_axis]] + place[main_axis + 1:]
    return result.at[tuple(place)].set(least).at[tuple(beside)].set(top_value)


def level_of(key, dims, cuts, least, high):
    level, own = 1.0, jax.random.fold_in(key, 6)
    for dim, parts in cuts:
        steps = jnp.exp(jax.random.uniform(jax.random.fold_in(own, dim), (parts,), jnp.float32, least / len(cuts), high / len(cuts)))
        level = level * jnp.repeat(steps, dims[dim] // parts).reshape([-1 if axis == dim else 1 for axis in range(len(dims))])
    return level


def routed_block(stream_key, own, number, rows, count, top, limit, lean):
    order = jax.random.permutation(stream_key, count)
    heavy_load, common = load_shares(count, rows * top, limit, lean, True), load_shares(count, rows * top, limit, lean, False)
    places = jnp.arange(count)

    def named(lengths, turn):
        used = int((lengths > 0).sum())
        fixed = max(1, used // 4)
        passed = fixed + (places - fixed + turn * (used - fixed)) % max(1, count - fixed)
        return jnp.zeros((count,), jnp.int32).at[order[jnp.where(places < fixed, places, passed)]].set(jnp.asarray(lengths, jnp.int32))

    lengths = jnp.where(number % 4 == 0, named(heavy_load, number // 4), named(common, number - number // 4 - 1))
    mixed = jax.random.permutation(jax.random.fold_in(own, 3), count)
    giver, sink = mixed[0:count // 2 * 2:2], mixed[1:count // 2 * 2:2]
    room = jnp.minimum(lengths[giver] - 1, limit - lengths[sink]) // 2
    room = jnp.where((giver == order[0]) | (sink == order[0]) | (lengths[sink] == 0), 0, jnp.maximum(room, 0))
    passed = jax.random.randint(jax.random.fold_in(own, 4), (count // 2,), 0, 1 << 20) % (room + 1)
    lengths = lengths.at[giver].add(-passed).at[sink].add(passed)
    items = jnp.searchsorted(jnp.cumsum(lengths), jnp.arange(rows * top), side="right").astype(jnp.int32)
    listing = items.reshape(top, rows).T
    listing = listing[jax.random.permutation(jax.random.fold_in(own, 1), rows)]
    turn = jax.random.randint(jax.random.fold_in(own, 2), (rows, 1), 0, top)
    return jnp.take_along_axis(listing, (jnp.arange(top)[None, :] + turn) % top, axis=1)


def load_shares(number_of, total, most, lean, full):
    loads = [(1 << 20) // math.isqrt(standing ** lean) + 1 for standing in range(1, number_of + 1)]
    largest = most if full else min(most, max(-(-total // number_of), total * loads[0] // sum(loads)))
    least = 1 if total - largest >= number_of - 1 else 0
    counts, rest = [largest] + [least] * (number_of - 1), total - largest - least * (number_of - 1)
    while rest > 0:
        candidates = [i for i in range(1, number_of) if counts[i] < largest] or [i for i in range(1, number_of) if counts[i] < most]
        pool, budget = sum([loads[i] for i in candidates]), rest
        for i in candidates:
            addition = min(most - counts[i], max(1, budget * loads[i] // pool), rest)
            counts[i] = counts[i] + addition
            rest = rest - addition
    return np.array(counts)


def bell_draw(rng, extent, width, limit, cuts=(), kind=jnp.bfloat16):
    result = width * jax.random.normal(rng, extent, jnp.float32)
    if cuts:
        result = result * level_of(rng, extent, cuts, -0.22, 0.18)
    return jnp.clip(result, -limit, limit).astype(kind)


def setup_inputs(seed: int = 0) -> dict:
    keys = jax.random.split(jax.random.key(seed), 11)
    params = draw_params(jax.random.fold_in(keys[10], 71), 0)
    first_moment = bell_draw(keys[1], (P_SIZE, GAUSS), 1.0, 6.0, ((1, 8),), jnp.float32)
    second_moment = jnp.clip(jnp.exp(math.log(1.0) - 4.6051702 * jax.random.uniform(keys[2], (P_SIZE, GAUSS), jnp.float32) ** level_of(keys[2], (P_SIZE, GAUSS), ((1, 8),), -0.2, 0.2)), 0.01, 1.0)
    camera = draw_camera(jax.random.fold_in(keys[10], 71), 0)
    tile_corner = jnp.clip(240.0 * jax.random.uniform(keys[4], (ITERS, REPLICAS, TILES, 2), jnp.float32) ** level_of(keys[4], (ITERS, REPLICAS, TILES, 2), ((1, 4), (2, 8)), -0.2, 0.2), 0.0, 240.0)
    tile_owner_keys = jax.random.split(jax.random.fold_in(keys[5], 1), ITERS * REPLICAS * TILES // TILES_DEV)
    tile_owner_turns = jax.random.permutation(jax.random.fold_in(keys[5], 3), ITERS * REPLICAS * TILES // TILES_DEV)
    tile_owner = jax.vmap(lambda own, number: routed_block(jax.random.fold_in(keys[5], 2), own, number, TILES_DEV, OWNERS, LISTB, CAP, 2))(tile_owner_keys, tile_owner_turns).reshape((ITERS, REPLICAS, TILES, LISTB))
    tile_block = place_ends(jax.random.randint(keys[6], (ITERS, REPLICAS, TILES, LISTB), 0, BLK_DEV), jax.random.fold_in(keys[6], 1), 0, BLK_DEV - 1).astype(jnp.int32)
    depth_order = jax.vmap(lambda own: jax.random.permutation(own, DEPTH))(jax.random.split(keys[7], ITERS * REPLICAS * TILES)).reshape((ITERS, REPLICAS, TILES, DEPTH)).astype(jnp.int32)
    targets = jnp.clip(1.0 * jax.random.uniform(keys[8], (ITERS, REPLICAS, TILES, 3, PIX), jnp.float32) ** level_of(keys[8], (ITERS, REPLICAS, TILES, 3, PIX), ((1, 4), (2, 8)), -0.2, 0.2), 0.0, 1.0)
    migration = draw_migration(jax.random.fold_in(keys[10], 71), 0)
    return {"params": params, "first_moment": first_moment, "second_moment": second_moment, "camera": camera, "tile_corner": tile_corner, "tile_owner": tile_owner, "tile_block": tile_block, "depth_order": depth_order, "targets": targets, "migration": migration}


harm_zero = 0.28209479177387814
harm_one = 0.4886025119029199
harm_two = (1.0925484305920792, -1.0925484305920792, 0.31539156525252005, -1.0925484305920792, 0.5462742152960396)
harm_three = (-0.5900435899266435, 2.890611442640554, -0.4570457994644658, 0.3731763325901154, -0.4570457994644658, 1.445305721320277, -0.5900435899266435)
learn_rate = 0.01
adam_epsilon = 1e-08

def harmonics(facing):
    face_x, face_y, face_z = (facing[0], facing[1], facing[2])
    face_xx, face_yy, face_zz = (face_x * face_x, face_y * face_y, face_z * face_z)
    terms = [harm_zero + 0.0 * face_x, -harm_one * face_y, harm_one * face_z, -harm_one * face_x, harm_two[0] * face_x * face_y, harm_two[1] * face_y * face_z, harm_two[2] * (2.0 * face_zz - face_xx - face_yy), harm_two[3] * face_x * face_z, harm_two[4] * (face_xx - face_yy), harm_three[0] * face_y * (3.0 * face_xx - face_yy), harm_three[1] * face_x * face_y * face_z, harm_three[2] * face_y * (4.0 * face_zz - face_xx - face_yy), harm_three[3] * face_z * (2.0 * face_zz - 3.0 * face_xx - 3.0 * face_yy), harm_three[4] * face_x * (4.0 * face_zz - face_xx - face_yy), harm_three[5] * face_z * (face_xx - face_yy), harm_three[6] * face_x * (face_xx - 3.0 * face_yy)]
    return jnp.stack(terms)

def project(params, camera_now):
    means = params[0:3]
    scales = jnp.exp(params[3:6])
    quats = params[6:10]
    quats = quats / jnp.sqrt(lax.optimization_barrier(jnp.sum(quats * quats, axis=0, keepdims=True)))
    quat_w, quat_x, quat_y, quat_z = (quats[0], quats[1], quats[2], quats[3])
    rotation = [[1.0 - 2.0 * (quat_y * quat_y + quat_z * quat_z), 2.0 * (quat_x * quat_y - quat_w * quat_z), 2.0 * (quat_x * quat_z + quat_w * quat_y)], [2.0 * (quat_x * quat_y + quat_w * quat_z), 1.0 - 2.0 * (quat_x * quat_x + quat_z * quat_z), 2.0 * (quat_y * quat_z - quat_w * quat_x)], [2.0 * (quat_x * quat_z - quat_w * quat_y), 2.0 * (quat_y * quat_z + quat_w * quat_x), 1.0 - 2.0 * (quat_x * quat_x + quat_y * quat_y)]]
    affine = [[camera_now[0], camera_now[1], camera_now[2]], [camera_now[3], camera_now[4], camera_now[5]]]
    spread = [[(affine[i][0] * rotation[0][k] + affine[i][1] * rotation[1][k] + affine[i][2] * rotation[2][k]) * scales[k] for k in range(3)] for i in range(2)]
    cov_xx = spread[0][0] * spread[0][0] + spread[0][1] * spread[0][1] + spread[0][2] * spread[0][2] + 0.3
    cov_yy = spread[1][0] * spread[1][0] + spread[1][1] * spread[1][1] + spread[1][2] * spread[1][2] + 0.3
    cov_xy = spread[0][0] * spread[1][0] + spread[0][1] * spread[1][1] + spread[0][2] * spread[1][2]
    determinant = cov_xx * cov_yy - cov_xy * cov_xy
    centre_x = affine[0][0] * means[0] + affine[0][1] * means[1] + affine[0][2] * means[2] + camera_now[6]
    centre_y = affine[1][0] * means[0] + affine[1][1] * means[1] + affine[1][2] * means[2] + camera_now[7]
    basis = harmonics(camera_now[8:11])
    colours = 0.5 + jnp.einsum('k,kcg->cg', basis, params[11:59].reshape(16, 3, -1), precision=lax.Precision.HIGHEST)
    opacity = jax.nn.sigmoid(params[10])
    geometry = jnp.stack([centre_x, centre_y, cov_yy / determinant, -cov_xy / determinant, cov_xx / determinant])
    return jnp.concatenate([geometry, colours, opacity[None]], axis=0)

def render(splat_rows, corner):
    side = math.isqrt(PIX)
    pixels = jnp.arange(PIX, dtype=jnp.int32)
    pos_x = corner[0] + (pixels % side).astype(jnp.float32) + 0.5
    pos_y = corner[1] + (pixels // side).astype(jnp.float32) + 0.5
    gap_x = pos_x[:, None] - splat_rows[0][None, :]
    gap_y = pos_y[:, None] - splat_rows[1][None, :]
    exponent = 0.5 * (splat_rows[2] * gap_x * gap_x + 2.0 * splat_rows[3] * gap_x * gap_y + splat_rows[4] * gap_y * gap_y)
    alphas = splat_rows[8] * jnp.exp(-exponent)
    log_keep = jnp.log1p(-alphas)
    transmit = jnp.exp(jnp.cumsum(log_keep, axis=1) - log_keep)
    return jnp.einsum('cn,pn->cp', splat_rows[5:8], alphas * transmit, precision=lax.Precision.HIGHEST)

def reference(params, first_moment, second_moment, camera, tile_corner, tile_owner, tile_block, depth_order, targets, migration):
    offsets = jnp.arange(BLOCK, dtype=jnp.int32)
    current = params
    moment_one = first_moment
    moment_two = second_moment
    pictures = []
    for step_index in range(ITERS):
        gradient = jnp.zeros_like(current)
        frames = []
        for replica in range(REPLICAS):
            camera_now = camera[step_index, replica]
            projected, pullback = jax.vjp(lambda p: project(p, camera_now), current)
            firsts = (tile_owner[step_index, replica] * BLK_DEV + tile_block[step_index, replica]) * BLOCK
            gauss_ids = (firsts[:, :, None] + offsets[None, None, :]).reshape(TILES, DEPTH).astype(jnp.int32)
            ordered = jnp.take_along_axis(gauss_ids, depth_order[step_index, replica], axis=1)

            def one_tile(pieces):
                tile_ids, corner, target = pieces
                splat_rows = jnp.take(projected, tile_ids, axis=1)
                picture, tile_back = jax.vjp(lambda r: render(r, corner), splat_rows)
                return (picture, tile_back(picture - target)[0])
            picture, tile_grads = lax.map(one_tile, (ordered, tile_corner[step_index, replica], targets[step_index, replica]))
            flat_grads = jnp.transpose(tile_grads, (1, 0, 2)).reshape(9, TILES * DEPTH)
            row_grads = jnp.zeros_like(projected).at[:, ordered.reshape(-1)].add(flat_grads)
            gradient = gradient + pullback(row_grads)[0]
            frames.append(picture)
        pictures.append(jnp.stack(frames))
        moment_one = 0.9 * moment_one + 0.1 * gradient
        moment_two = 0.999 * moment_two + 0.001 * gradient * gradient
        current = current - learn_rate * moment_one / (jnp.sqrt(moment_two) + adam_epsilon)
    stacked = jnp.stack([current, moment_one, moment_two]).reshape(3, P_SIZE, OWNERS, BLK_DEV, BLOCK)
    owner_ids = jnp.arange(OWNERS, dtype=jnp.int32)
    moved = stacked
    for column in range(MIGH):
        going_left = migration[:, 0, column]
        going_right = migration[:, 1, column]
        from_left = jnp.roll(stacked[:, :, owner_ids, going_right], 1, axis=2)
        from_right = jnp.roll(stacked[:, :, owner_ids, going_left], -1, axis=2)
        moved = moved.at[:, :, owner_ids, going_left].set(from_left)
        moved = moved.at[:, :, owner_ids, going_right].set(from_right)
    moved = moved.reshape(3, P_SIZE, GAUSS)
    return (moved[0], moved[1], moved[2], jnp.stack(pictures))
```

```python
import math

import jax
import jax.numpy as jnp
from jax import lax
from jax.experimental import pallas as pl
from jax.experimental.pallas import tpu as pltpu
from jax.sharding import PartitionSpec as P

P_SIZE = 59
BLOCK = 128
LISTB = 4
PIX = 256
ITERS = 2
MIGH = 2
DEPTH = 512
SIDE = 16
HALF = DEPTH // 2
MIG_LANE = 64
CAM_ROWS = 16
LOG2E = 1.4426950408889634

harm_zero = 0.28209479177387814
harm_one = 0.4886025119029199
harm_two = (
    1.0925484305920792,
    -1.0925484305920792,
    0.31539156525252005,
    -1.0925484305920792,
    0.5462742152960396,
)
harm_three = (
    -0.5900435899266435,
    2.890611442640554,
    -0.4570457994644658,
    0.3731763325901154,
    -0.4570457994644658,
    1.445305721320277,
    -0.5900435899266435,
)
learn_rate = 0.01
adam_epsilon = 1e-08

f32 = jnp.float32
bf16 = jnp.bfloat16
VM = pl.BlockSpec(memory_space=pltpu.VMEM)
SM = pl.BlockSpec(memory_space=pltpu.SMEM)


def up8(count):
    return -(-count // 8) * 8


def harmonics(x, y, z):
    xx, yy, zz = x * x, y * y, z * z
    return [
        harm_zero + 0.0 * x,
        -harm_one * y,
        harm_one * z,
        -harm_one * x,
        harm_two[0] * x * y,
        harm_two[1] * y * z,
        harm_two[2] * (2.0 * zz - xx - yy),
        harm_two[3] * x * z,
        harm_two[4] * (xx - yy),
        harm_three[0] * y * (3.0 * xx - yy),
        harm_three[1] * x * y * z,
        harm_three[2] * y * (4.0 * zz - xx - yy),
        harm_three[3] * z * (2.0 * zz - 3.0 * xx - 3.0 * yy),
        harm_three[4] * x * (4.0 * zz - xx - yy),
        harm_three[5] * z * (xx - yy),
        harm_three[6] * x * (xx - 3.0 * yy),
    ]


def split(value, pieces):
    out = []
    for piece in range(pieces):
        part = value.astype(bf16)
        out.append(part)
        if piece < pieces - 1:
            value = value - part.astype(f32)
    return out


def dot(left, right, dims=((1,), (0,))):
    return lax.dot_general(left, right, (dims, ((), ())), preferred_element_type=f32)


NT = ((1,), (1,))
TN = ((0,), (0,))


def rank_of(owners, index):
    rank = jnp.int32(0)
    for other in range(index):
        rank = rank + (owners[other] == owners[index]).astype(jnp.int32)
    return rank


def request_kernel(capacity, owner_ref, block_ref, migration_ref, out_ref):
    owners = out_ref.shape[0]
    tiles = owner_ref.shape[2]
    lane = lax.broadcasted_iota(jnp.int32, (owners, BLOCK), 1)
    row = lax.broadcasted_iota(jnp.int32, (owners, BLOCK), 0)
    place = row * BLOCK + lane
    message = jnp.full((owners, BLOCK), -1, jnp.int32)
    for step in range(ITERS):
        names = [owner_ref[step, 0, t, j] for t in range(tiles) for j in range(LISTB)]
        for index in range(tiles * LISTB):
            target = names[index] * BLOCK + step * capacity + rank_of(names, index)
            block = block_ref[step, 0, index // LISTB, index % LISTB]
            message = jnp.where(place == target, block, message)
    for side in range(2):
        for j in range(MIGH):
            message = jnp.where(
                lane == MIG_LANE + side * MIGH + j, migration_ref[0, side, j], message
            )
    for owner in range(owners):
        out_ref[owner] = message[owner : owner + 1]


def geometry(row):
    scales = [jnp.exp(row(3 + k)) for k in range(3)]
    quats = [row(6 + k) for k in range(4)]
    norm = lax.rsqrt(
        quats[0] * quats[0] + quats[1] * quats[1] + quats[2] * quats[2] + quats[3] * quats[3]
    )
    w, x, y, z = [part * norm for part in quats]
    rotation = [
        [1.0 - 2.0 * (y * y + z * z), 2.0 * (x * y - w * z), 2.0 * (x * z + w * y)],
        [2.0 * (x * y + w * z), 1.0 - 2.0 * (x * x + z * z), 2.0 * (y * z - w * x)],
        [2.0 * (x * z - w * y), 2.0 * (y * z + w * x), 1.0 - 2.0 * (x * x + y * y)],
    ]
    return scales, (w, x, y, z), norm, rotation


def conic_of(scales, rotation, affine):
    spread = [
        [
            (
                affine[3 * i] * rotation[0][k]
                + affine[3 * i + 1] * rotation[1][k]
                + affine[3 * i + 2] * rotation[2][k]
            )
            * scales[k]
            for k in range(3)
        ]
        for i in range(2)
    ]
    one, two = spread
    cov_xx = one[0] * one[0] + one[1] * one[1] + one[2] * one[2] + 0.3
    cov_yy = two[0] * two[0] + two[1] * two[1] + two[2] * two[2] + 0.3
    cov_xy = one[0] * two[0] + one[1] * two[1] + one[2] * two[2]
    inverse = 1.0 / (cov_xx * cov_yy - cov_xy * cov_xy)
    return cov_yy * inverse, -cov_xy * inverse, cov_xx * inverse


def serve(step, capacity, blocks, camera_ref, asked_ref, dense, table, faint, out_ref):
    cam = [camera_ref[step, 0, k] for k in range(11)]
    basis = harmonics(cam[8], cam[9], cam[10])
    for group in range(blocks // 8):

        def row(p):
            return dense[p * blocks + 8 * group : p * blocks + 8 * group + 8, :]

        scales, _, _, rotation = geometry(row)
        conic = conic_of(scales, rotation, cam)
        means = [row(k) for k in range(3)]
        rows = [
            cam[0] * means[0] + cam[1] * means[1] + cam[2] * means[2] + cam[6],
            cam[3] * means[0] + cam[4] * means[1] + cam[5] * means[2] + cam[7],
            conic[0],
            conic[1],
            conic[2],
        ]
        for k in range(3):
            colour = basis[0] * row(11 + k)
            for j in range(1, 16):
                colour = colour + basis[j] * row(11 + 3 * j + k)
            rows.append(0.5 + colour)
        for k in range(8):
            table[pl.ds(64 * group + k, 8, stride=8), :] = rows[k]
        faint[8 * group : 8 * group + 8, :] = -LOG2E * jnp.log(1.0 + jnp.exp(-row(10)))
    owners = out_ref.shape[0]
    for peer in range(owners):
        for slot in range(capacity):
            block = jnp.maximum(asked_ref[peer, 0, step * capacity + slot], 0)
            out_ref[peer, 8 * slot : 8 * slot + 8, :] = table[
                pl.ds(pl.multiple_of(block * 8, 8), 8), :
            ]
            out_ref[peer, 8 * capacity + slot : 8 * capacity + slot + 1, :] = faint[
                pl.ds(block, 1), :
            ]


def row_groups():
    return [(first, min(8, P_SIZE - first)) for first in range(0, P_SIZE, 8)]


def start_kernel(capacity, params_ref, camera_ref, asked_ref, out_ref, dense, table, faint):
    blocks = params_ref.shape[1] // BLOCK
    for block in range(blocks):
        for first, count in row_groups():
            dense[pl.ds(first * blocks + block, count, stride=blocks), :] = params_ref[
                first : first + count, block * BLOCK : (block + 1) * BLOCK
            ]
    serve(0, capacity, blocks, camera_ref, asked_ref, dense, table, faint, out_ref)


def render_kernel(step, capacity, slots, final, *refs):
    if final:
        (
            arrived, corner_ref, owner_ref, block_ref, asked_ref, order_ref, target_ref, earlier_ref,
            picture_ref, out_ref, onehot, upper, lower, features, flat, coeffs,
        ) = refs
        for other in range(ITERS - 1):
            picture_ref[other] = earlier_ref[other]
    else:
        (
            arrived, corner_ref, owner_ref, order_ref, target_ref,
            picture_ref, out_ref, onehot, upper, lower, features, flat, coeffs,
        ) = refs
    owners = arrived.shape[0]
    tiles = owner_ref.shape[2]
    out_ref[...] = jnp.zeros_like(out_ref)

    first = lax.broadcasted_iota(jnp.int32, (HALF, HALF), 0)
    second = lax.broadcasted_iota(jnp.int32, (HALF, HALF), 1)
    upper[...] = jnp.where(first < second, 1.0, 0.0).astype(bf16)
    lower[...] = jnp.where(first > second, 1.0, 0.0).astype(bf16)
    pixel = lax.broadcasted_iota(jnp.int32, (PIX, BLOCK), 0)
    which = lax.broadcasted_iota(jnp.int32, (PIX, BLOCK), 1) // 3
    px = (pixel % SIDE).astype(f32) - (SIDE / 2 - 0.5)
    py = (pixel // SIDE).astype(f32) - (SIDE / 2 - 0.5)
    chosen = jnp.where(which == 0, 1.0, 0.0)
    for index, value in enumerate((px, py, px * px, px * py, py * py)):
        chosen = jnp.where(which == index + 1, value, chosen)
    features[...] = chosen.astype(bf16)
    pixel = lax.broadcasted_iota(jnp.int32, (16, PIX), 1)
    which = lax.broadcasted_iota(jnp.int32, (16, PIX), 0)
    px = (pixel % SIDE).astype(f32) - (SIDE / 2 - 0.5)
    py = (pixel // SIDE).astype(f32) - (SIDE / 2 - 0.5)
    chosen = jnp.where(which == 0, 1.0, 0.0)
    for index, value in enumerate((px, py, px * px, px * py, py * py)):
        chosen = jnp.where(which == index + 1, value, chosen)
    flat[...] = chosen.astype(bf16)
    coeffs[...] = jnp.zeros_like(coeffs)

    names = [owner_ref[step, 0, t, j] for t in range(tiles) for j in range(LISTB)]
    ranks = [rank_of(names, index) for index in range(tiles * LISTB)]

    for tile in range(tiles):
        order = order_ref[step, 0, tile : tile + 1, :]
        for piece in range(DEPTH // BLOCK):
            ids = lax.broadcasted_iota(jnp.int32, (BLOCK, DEPTH), 0) + piece * BLOCK
            onehot[piece * BLOCK : (piece + 1) * BLOCK, :] = jnp.where(
                ids == order, 1.0, 0.0
            ).astype(bf16)
        pieces, dims = [], []
        for j in range(LISTB):
            name, rank = names[tile * LISTB + j], ranks[tile * LISTB + j]
            pieces.append(arrived[name, pl.ds(pl.multiple_of(rank * 8, 8), 8), :])
            dims.append(
                jnp.broadcast_to(arrived[name, pl.ds(8 * capacity + rank, 1), :], (8, BLOCK))
            )
        sorted_rows, sorted_dim = [], []
        for piece in range(DEPTH // BLOCK):
            ids = jnp.broadcast_to(order[:, piece * BLOCK : (piece + 1) * BLOCK], (8, BLOCK))
            within, source = ids & (BLOCK - 1), ids // BLOCK
            got = jnp.take_along_axis(pieces[0], within, axis=1)
            dim = jnp.take_along_axis(dims[0], within, axis=1)
            for j in range(1, LISTB):
                got = jnp.where(source == j, jnp.take_along_axis(pieces[j], within, axis=1), got)
                dim = jnp.where(source == j, jnp.take_along_axis(dims[j], within, axis=1), dim)
            sorted_rows.append(got)
            sorted_dim.append(dim)
        rows = jnp.concatenate(sorted_rows, axis=1)
        faint = jnp.concatenate(sorted_dim, axis=1)[0:1]
        u = rows[0:1] - (corner_ref[step, 0, tile, 0] + SIDE / 2)
        v = rows[1:2] - (corner_ref[step, 0, tile, 1] + SIDE / 2)
        a, b, c = rows[2:3], rows[3:4], rows[4:5]
        colours = rows[5:8]
        half_a, half_b, half_c = (-0.5 * LOG2E) * a, -LOG2E * b, (-0.5 * LOG2E) * c
        values = (
            half_a * u * u + half_b * u * v + half_c * v * v + faint,
            -(2.0 * half_a * u + half_b * v),
            -(2.0 * half_c * v + half_b * u),
            half_a,
            half_b,
            half_c,
        )
        for index, value in enumerate(values):
            for piece, part in enumerate(split(value, 3)):
                coeffs[3 * index + piece : 3 * index + piece + 1, :] = part.astype(f32)
        form = coeffs[...].astype(bf16)
        col_h, col_m, col_l = [part.astype(f32) for part in split(colours, 3)]
        col_left = jnp.concatenate([col_h, col_m, col_l], axis=0).astype(bf16)
        col_right = jnp.concatenate(
            [col_h, col_m, col_h, col_m, col_l, col_h], axis=0
        ).astype(bf16)

        step_rows = 128
        moments = jnp.zeros((16, DEPTH), f32)
        col_grads = jnp.zeros((9, DEPTH), f32)
        for at in range(0, PIX, step_rows):
            feats = features[at : at + step_rows, 0:32]
            power = dot(feats, form)
            alpha = jnp.exp2(power)
            keep = jnp.log(1.0 - alpha)
            ratio = jnp.exp2(power - LOG2E * keep)
            keep_h, keep_m = split(keep, 2)
            tri = upper[...]
            near = dot(keep_h[:, :HALF], tri) + dot(keep_m[:, :HALF], tri)
            far = dot(keep_h[:, HALF:], tri) + dot(keep_m[:, HALF:], tri)
            far = far + (near[:, HALF - 1 : HALF] + keep[:, HALF - 1 : HALF])
            weight = alpha * jnp.exp(jnp.concatenate([near, far], axis=1))
            weight_h, weight_m = split(weight, 2)
            shades = dot(col_left, weight_h, NT) + dot(col_left, weight_m, NT)
            shades = shades[0:3] + shades[3:6] + shades[6:9]
            if final:
                picture_ref[step, 0, tile, :, at : at + step_rows] = shades
            else:
                picture_ref[step, 0, tile, :, at : at + step_rows] = shades
            error = shades - target_ref[step, 0, tile, :, at : at + step_rows]
            err_h, err_m, err_l = [part.astype(f32) for part in split(error, 3)]
            err_left = jnp.concatenate([err_h, err_m, err_l], axis=0).astype(bf16)
            err_right = jnp.concatenate(
                [err_h, err_h, err_m, err_m, err_h, err_l], axis=0
            ).astype(bf16)
            col_grads = col_grads + dot(err_left, weight_h) + dot(err_left, weight_m)
            flow = weight * dot(err_right, col_right, TN)
            flow_h, flow_m = split(flow, 2)
            tri = lower[...]
            far = dot(flow_h[:, HALF:], tri) + dot(flow_m[:, HALF:], tri)
            near = dot(flow_h[:, :HALF], tri) + dot(flow_m[:, :HALF], tri)
            near = near + (far[:, 0:1] + flow[:, HALF : HALF + 1])
            heat = flow - ratio * jnp.concatenate([near, far], axis=1)
            for part in split(heat, 3):
                moments = moments + dot(flat[:, at : at + step_rows], part)
        col_grads = col_grads[0:3] + col_grads[3:6] + col_grads[6:9]
        m00, m10, m01 = moments[0:1], moments[1:2], moments[2:3]
        m20, m11, m02 = moments[3:4], moments[4:5], moments[5:6]
        x1, y1 = m10 - u * m00, m01 - v * m00
        grads = [
            a * x1 + b * y1,
            b * x1 + c * y1,
            -0.5 * (m20 - 2.0 * u * m10 + u * u * m00),
            -(m11 - u * m01 - v * m10 + u * v * m00),
            -0.5 * (m02 - 2.0 * v * m01 + v * v * m00),
            col_grads,
            m00,
            jnp.zeros((7, DEPTH), f32),
        ]
        grads = jnp.concatenate(grads, axis=0)
        listed = jnp.zeros((16, DEPTH), f32)
        for part in split(grads, 3):
            listed = listed + dot(part, onehot[...], NT)
        for j in range(LISTB):
            name, rank = names[tile * LISTB + j], ranks[tile * LISTB + j]
            if final:
                block = block_ref[step, 0, tile, j]
                for k in range(MIGH):
                    goes_left = asked_ref[name, 0, MIG_LANE + k] == block
                    goes_right = asked_ref[name, 0, MIG_LANE + MIGH + k] == block
                    rank = jnp.where(goes_left, capacity + MIGH + k, rank)
                    rank = jnp.where(goes_right, capacity + k, rank)
                goes_left = jnp.bool_(False)
                goes_right = jnp.bool_(False)
                for k in range(MIGH):
                    goes_left |= asked_ref[name, 0, MIG_LANE + k] == block
                    goes_right |= asked_ref[name, 0, MIG_LANE + MIGH + k] == block
                below = jnp.where(name == 0, owners - 1, name - 1)
                above = jnp.where(name == owners - 1, 0, name + 1)
                name = jnp.where(goes_left, below, jnp.where(goes_right, above, name))
            lanes = slice(j * BLOCK, (j + 1) * BLOCK)
            main = pl.ds(pl.multiple_of(rank * 8, 8), 8)
            extra = pl.ds(8 * slots + rank, 1)
            if final:
                out_ref[name, main, :] = out_ref[name, main, :] + listed[0:8, lanes]
                out_ref[name, extra, :] = out_ref[name, extra, :] + listed[8:9, lanes]
            else:
                out_ref[name, main, :] = listed[0:8, lanes]
                out_ref[name, extra, :] = listed[8:9, lanes]


def gather_kernel(step, capacity, slots, returned, asked_ref, migration_ref, camera_ref, out_ref):
    owners = returned.shape[0]
    blocks = (out_ref.shape[0] - CAM_ROWS) // 9
    out_ref[...] = jnp.zeros_like(out_ref)

    def body(peer, carry):
        for slot in range(slots):
            if slot < capacity:
                block = jnp.maximum(asked_ref[peer, 0, step * capacity + slot], 0)
            else:
                block = migration_ref[0, (slot - capacity) // MIGH, (slot - capacity) % MIGH]
            main = pl.ds(pl.multiple_of(block * 8, 8), 8)
            extra = pl.ds(8 * blocks + block, 1)
            out_ref[main, :] = out_ref[main, :] + returned[peer, 8 * slot : 8 * slot + 8, :]
            out_ref[extra, :] = (
                out_ref[extra, :] + returned[peer, 8 * slots + slot : 8 * slots + slot + 1, :]
            )
        return carry

    lax.fori_loop(0, owners, body, 0)
    for index, k in enumerate((0, 1, 2, 3, 4, 5, 8, 9, 10)):
        at = 9 * blocks + index
        out_ref[at : at + 1, :] = jnp.full((1, BLOCK), camera_ref[step, 0, k], f32)


def collect(own_ref, others, scratch):
    mine = lax.axis_index("rep")
    scratch[mine] = own_ref[...]
    for offset, ref in others:
        scratch[mine ^ offset] = ref[...]


def pullback(blocks, cams, dense, grads):
    count = cams.shape[0]
    affine, basis = [], []
    for c in range(count):
        rows = [
            jnp.broadcast_to(cams[c, 9 * blocks + k : 9 * blocks + k + 1, :], (8, BLOCK))
            for k in range(9)
        ]
        affine.append(rows[0:6])
        basis.append(harmonics(rows[6], rows[7], rows[8]))
    for group in range(blocks // 8):

        def row(p):
            return dense[p * blocks + 8 * group : p * blocks + 8 * group + 8, :]

        def put(p, value):
            grads[p * blocks + 8 * group : p * blocks + 8 * group + 8, :] = value

        given = [
            [cams[c, pl.ds(64 * group + k, 8, stride=8), :] for k in range(8)] for c in range(count)
        ]
        scales, (w, x, y, z), norm, rotation = geometry(row)
        means = [0.0, 0.0, 0.0]
        sigma = [0.0] * 6
        for c in range(count):
            m = affine[c]
            a, b, d = conic_of(scales, rotation, m)
            g_x, g_y, g_a, g_b, g_d = given[c][0:5]
            for k in range(3):
                means[k] = means[k] + m[k] * g_x + m[3 + k] * g_y
            g_b = 0.5 * g_b
            t00, t01 = a * g_a + b * g_b, a * g_b + b * g_d
            t10, t11 = b * g_a + d * g_b, b * g_b + d * g_d
            h00 = -(t00 * a + t01 * b)
            h01 = -(t00 * b + t01 * d)
            h11 = -(t10 * b + t11 * d)
            top = [h00 * m[k] + h01 * m[3 + k] for k in range(3)]
            low = [h01 * m[k] + h11 * m[3 + k] for k in range(3)]
            for index, (i, k) in enumerate(((0, 0), (0, 1), (0, 2), (1, 1), (1, 2), (2, 2))):
                sigma[index] = sigma[index] + m[i] * top[k] + m[3 + i] * low[k]
        for k in range(3):
            put(k, means[k])
        full = [
            [sigma[0], sigma[1], sigma[2]],
            [sigma[1], sigma[3], sigma[4]],
            [sigma[2], sigma[4], sigma[5]],
        ]
        turn = [[None] * 3 for _ in range(3)]
        for k in range(3):
            column = [rotation[j][k] * scales[k] for j in range(3)]
            pulled = [
                2.0 * (full[j][0] * column[0] + full[j][1] * column[1] + full[j][2] * column[2])
                for j in range(3)
            ]
            put(
                3 + k, pulled[0] * column[0] + pulled[1] * column[1] + pulled[2] * column[2]
            )
            for j in range(3):
                turn[j][k] = pulled[j] * scales[k]
        g_w = 2.0 * (
            z * (turn[1][0] - turn[0][1])
            + y * (turn[0][2] - turn[2][0])
            + x * (turn[2][1] - turn[1][2])
        )
        g_x = 2.0 * (
            y * (turn[0][1] + turn[1][0])
            + z * (turn[0][2] + turn[2][0])
            - 2.0 * x * (turn[1][1] + turn[2][2])
            + w * (turn[2][1] - turn[1][2])
        )
        g_y = 2.0 * (
            x * (turn[0][1] + turn[1][0])
            + z * (turn[1][2] + turn[2][1])
            - 2.0 * y * (turn[0][0] + turn[2][2])
            + w * (turn[0][2] - turn[2][0])
        )
        g_z = 2.0 * (
            x * (turn[0][2] + turn[2][0])
            + y * (turn[1][2] + turn[2][1])
            - 2.0 * z * (turn[0][0] + turn[1][1])
            + w * (turn[1][0] - turn[0][1])
        )
        along = w * g_w + x * g_x + y * g_y + z * g_z
        for k, (part, pull) in enumerate(((w, g_w), (x, g_x), (y, g_y), (z, g_z))):
            put(6 + k, norm * (pull - part * along))
        faint = cams[0, 8 * blocks + 8 * group : 8 * blocks + 8 * group + 8, :]
        for c in range(1, count):
            faint = faint + cams[c, 8 * blocks + 8 * group : 8 * blocks + 8 * group + 8, :]
        put(10, faint / (1.0 + jnp.exp(row(10))))
        for j in range(16):
            for k in range(3):
                value = basis[0][j] * given[0][5 + k]
                for c in range(1, count):
                    value = value + basis[c][j] * given[c][5 + k]
                put(11 + 3 * j + k, value)


def adam(value, first, second, gradient):
    first = 0.9 * first + 0.1 * gradient
    second = 0.999 * second + 0.001 * gradient * gradient
    return value - learn_rate * first / (jnp.sqrt(second) + adam_epsilon), first, second


def update_kernel(capacity, *refs):
    (
        own_ref, near_ref, far_ref, cross_ref, params_ref, first_ref, second_ref, camera_ref,
        asked_ref, migration_ref, new_params, new_first, new_second, out_ref, left_ref, right_ref,
        cams, dense, grads, table, faint,
    ) = refs
    blocks = params_ref.shape[1] // BLOCK
    collect(own_ref, ((1, near_ref), (2, far_ref), (3, cross_ref)), cams)
    for block in range(blocks):
        for top, count in row_groups()[:2]:
            dense[pl.ds(top * blocks + block, count, stride=blocks), :] = params_ref[
                top : top + count, block * BLOCK : (block + 1) * BLOCK
            ]
    pullback(blocks, cams, dense, grads)
    for block in range(blocks):
        lanes = slice(block * BLOCK, (block + 1) * BLOCK)
        for top, count in row_groups():
            part = slice(top, top + count)
            where = pl.ds(top * blocks + block, count, stride=blocks)
            value, first, second = adam(
                params_ref[part, lanes], first_ref[part, lanes], second_ref[part, lanes],
                grads[where, :],
            )
            new_params[part, lanes] = value
            new_first[part, lanes] = first
            new_second[part, lanes] = second
            dense[where, :] = value
    serve(1, capacity, blocks, camera_ref, asked_ref, dense, table, faint, out_ref)
    for side, ref in ((0, left_ref), (1, right_ref)):
        for j in range(MIGH):
            lanes = pl.ds(pl.multiple_of(migration_ref[0, side, j] * BLOCK, BLOCK), BLOCK)
            for index, source in enumerate((new_params, new_first, new_second)):
                ref[index, :, j * BLOCK : (j + 1) * BLOCK] = source[:, lanes]


def final_kernel(*refs):
    (
        own_ref, near_ref, far_ref, cross_ref, params_ref, first_ref, second_ref, below_ref,
        above_ref, migration_ref, new_params, new_first, new_second, cams, dense, grads,
    ) = refs
    blocks = params_ref.shape[1] // BLOCK
    collect(own_ref, ((1, near_ref), (2, far_ref), (3, cross_ref)), cams)
    for block in range(blocks):
        for top, count in row_groups()[:2]:
            dense[pl.ds(top * blocks + block, count, stride=blocks), :] = params_ref[
                top : top + count, block * BLOCK : (block + 1) * BLOCK
            ]
    moved = [
        (migration_ref[0, side, j], ref, j)
        for side, ref in ((0, below_ref), (1, above_ref))
        for j in range(MIGH)
    ]
    for block, ref, j in moved:
        for top, count in row_groups()[:2]:
            dense[pl.ds(top * blocks + block, count, stride=blocks), :] = ref[
                0, top : top + count, j * BLOCK : (j + 1) * BLOCK
            ]
    pullback(blocks, cams, dense, grads)
    for block in range(blocks):
        lanes = slice(block * BLOCK, (block + 1) * BLOCK)
        for top, count in row_groups():
            part = slice(top, top + count)
            value, first, second = adam(
                params_ref[part, lanes], first_ref[part, lanes], second_ref[part, lanes],
                grads[pl.ds(top * blocks + block, count, stride=blocks), :],
            )
            new_params[part, lanes] = value
            new_first[part, lanes] = first
            new_second[part, lanes] = second
    for block, ref, j in moved:
        lanes = pl.ds(pl.multiple_of(block * BLOCK, BLOCK), BLOCK)
        source = slice(j * BLOCK, (j + 1) * BLOCK)
        for top, count in row_groups():
            part = slice(top, top + count)
            value, first, second = adam(
                ref[0, part, source], ref[1, part, source], ref[2, part, source],
                grads[pl.ds(top * blocks + block, count, stride=blocks), :],
            )
            new_params[part, lanes] = value
            new_first[part, lanes] = first
            new_second[part, lanes] = second


def shape(dims, dtype=f32):
    return jax.ShapeDtypeStruct(dims, dtype)


def bind(kernel, *static):
    def run(*refs):
        kernel(*static, *refs)

    return run


def swap(value, axis, offset):
    count = lax.axis_size(axis)
    return lax.ppermute(value, axis, [(i, i ^ offset) for i in range(count)])


def turn(value, axis, offset):
    count = lax.axis_size(axis)
    return lax.ppermute(value, axis, [(i, (i + offset) % count) for i in range(count)])


def exchange(value):
    far = swap(value, "rep", 2)
    near = swap(value, "rep", 1)
    cross = swap(far, "rep", 1)
    return near, far, cross


def row_exchange(value):
    return lax.all_to_all(value, "row", split_axis=0, concat_axis=0, tiled=True)


def local(
    params,
    first_moment,
    second_moment,
    camera,
    tile_corner,
    tile_owner,
    tile_block,
    depth_order,
    targets,
    migration,
):
    owners = lax.axis_size("row")
    replicas = lax.axis_size("rep")
    blocks = params.shape[1] // BLOCK
    tiles = tile_owner.shape[2]
    requests = tiles * LISTB
    capacity = max(2, 2 * ((requests + owners - 1) // owners))
    slots = capacity + 2 * MIGH
    dense = pltpu.VMEM((64 * blocks, BLOCK), f32)
    table = pltpu.VMEM((8 * blocks, BLOCK), f32)
    faint = pltpu.VMEM((blocks, BLOCK), f32)
    payload = 9 * blocks + CAM_ROWS
    cams = pltpu.VMEM((replicas, payload, BLOCK), f32)
    state = [shape(params.shape)] * 3

    lists = pl.pallas_call(
        bind(request_kernel, capacity),
        out_shape=shape((owners, 1, BLOCK), jnp.int32),
        in_specs=[SM, SM, SM],
        out_specs=VM,
    )(tile_owner, tile_block, migration)
    asked = row_exchange(lists)

    outgoing = pl.pallas_call(
        bind(start_kernel, capacity),
        out_shape=shape((owners, up8(9 * capacity), BLOCK)),
        in_specs=[VM, SM, SM],
        out_specs=VM,
        scratch_shapes=[dense, table, faint],
    )(params, camera, asked)

    render_scratch = [
        pltpu.VMEM((DEPTH, DEPTH), bf16),
        pltpu.VMEM((HALF, HALF), bf16),
        pltpu.VMEM((HALF, HALF), bf16),
        pltpu.VMEM((PIX, BLOCK), bf16),
        pltpu.VMEM((16, PIX), bf16),
        pltpu.VMEM((32, DEPTH), f32),
    ]
    pictures_shape = shape(targets.shape)

    def gather(step, count, returned):
        return pl.pallas_call(
            bind(gather_kernel, step, capacity, count),
            out_shape=shape((payload, BLOCK)),
            in_specs=[VM, SM, SM, SM],
            out_specs=VM,
        )(returned, asked, migration, camera)

    arrived = row_exchange(outgoing)
    pictures, back = pl.pallas_call(
        bind(render_kernel, 0, capacity, capacity, False),
        out_shape=[pictures_shape, shape((owners, up8(9 * capacity), BLOCK))],
        in_specs=[VM, SM, SM, VM, VM],
        out_specs=[VM, VM],
        scratch_shapes=render_scratch,
    )(arrived, tile_corner, tile_owner, depth_order, targets)
    own = gather(0, capacity, row_exchange(back))
    near, far, cross = exchange(own)
    leaving = shape((3, P_SIZE, MIGH * BLOCK))
    current, moment_one, moment_two, outgoing, left, right = pl.pallas_call(
        bind(update_kernel, capacity),
        out_shape=state + [shape((owners, up8(9 * capacity), BLOCK)), leaving, leaving],
        in_specs=[VM] * 7 + [SM] * 3,
        out_specs=[VM] * 6,
        scratch_shapes=[cams, dense, dense, table, faint],
    )(
        own, near, far, cross, params, first_moment, second_moment, camera, asked, migration
    )
    arrived = row_exchange(outgoing)
    below = turn(right, "row", 1)
    above = turn(left, "row", -1)
    pictures, back = pl.pallas_call(
        bind(render_kernel, 1, capacity, slots, True),
        out_shape=[pictures_shape, shape((owners, up8(9 * slots), BLOCK))],
        in_specs=[VM, SM, SM, SM, SM, VM, VM, VM],
        out_specs=[VM, VM],
        scratch_shapes=render_scratch,
    )(arrived, tile_corner, tile_owner, tile_block, asked, depth_order, targets, pictures)
    own = gather(1, slots, row_exchange(back))
    near, far, cross = exchange(own)
    current, moment_one, moment_two = pl.pallas_call(
        final_kernel,
        out_shape=state,
        in_specs=[VM] * 9 + [SM],
        out_specs=[VM] * 3,
        scratch_shapes=[cams, dense, dense],
    )(own, near, far, cross, current, moment_one, moment_two, below, above, migration)
    return current, moment_one, moment_two, pictures


def solution(mesh):
    return jax.shard_map(
        local,
        mesh=mesh,
        in_specs=(
            P(None, "row"),
            P(None, "row"),
            P(None, "row"),
            P(None, "rep", None),
            P(None, "rep", "row", None),
            P(None, "rep", "row", None),
            P(None, "rep", "row", None),
            P(None, "rep", "row", None),
            P(None, "rep", "row", None, None),
            P("row", None, None),
        ),
        out_specs=(
            P(None, "row"),
            P(None, "row"),
            P(None, "row"),
            P(None, "rep", "row", None, None),
        ),
        check_vma=False,
    )
```

```python
import math

import jax
import jax.numpy as jnp
from jax import lax
from jax.experimental import pallas as pl
from jax.experimental.pallas import tpu as pltpu
from jax.sharding import PartitionSpec as P

P_SIZE = 59
BLOCK = 128
LISTB = 4
PIX = 256
ITERS = 2
MIGH = 2
DEPTH = 512
SIDE = 16
MIG_LANE = 64
CAM_ROWS = 16
LOG2E = 1.4426950408889634

harm_zero = 0.28209479177387814
harm_one = 0.4886025119029199
harm_two = (
    1.0925484305920792,
    -1.0925484305920792,
    0.31539156525252005,
    -1.0925484305920792,
    0.5462742152960396,
)
harm_three = (
    -0.5900435899266435,
    2.890611442640554,
    -0.4570457994644658,
    0.3731763325901154,
    -0.4570457994644658,
    1.445305721320277,
    -0.5900435899266435,
)
learn_rate = 0.01
adam_epsilon = 1e-08

f32 = jnp.float32
bf16 = jnp.bfloat16
VM = pl.BlockSpec(memory_space=pltpu.VMEM)
SM = pl.BlockSpec(memory_space=pltpu.SMEM)


def up8(count):
    return -(-count // 8) * 8


def harmonics(x, y, z):
    xx, yy, zz = x * x, y * y, z * z
    return [
        harm_zero + 0.0 * x,
        -harm_one * y,
        harm_one * z,
        -harm_one * x,
        harm_two[0] * x * y,
        harm_two[1] * y * z,
        harm_two[2] * (2.0 * zz - xx - yy),
        harm_two[3] * x * z,
        harm_two[4] * (xx - yy),
        harm_three[0] * y * (3.0 * xx - yy),
        harm_three[1] * x * y * z,
        harm_three[2] * y * (4.0 * zz - xx - yy),
        harm_three[3] * z * (2.0 * zz - 3.0 * xx - 3.0 * yy),
        harm_three[4] * x * (4.0 * zz - xx - yy),
        harm_three[5] * z * (xx - yy),
        harm_three[6] * x * (xx - 3.0 * yy),
    ]


def split(value, pieces):
    out = []
    for piece in range(pieces):
        part = value.astype(bf16)
        out.append(part)
        if piece < pieces - 1:
            value = value - part.astype(f32)
    return out


def dot(left, right, dims=((1,), (0,))):
    return lax.dot_general(left, right, (dims, ((), ())), preferred_element_type=f32)


NT = ((1,), (1,))
TN = ((0,), (0,))


def rank_of(owners, index):
    rank = jnp.int32(0)
    for other in range(index):
        rank = rank + (owners[other] == owners[index]).astype(jnp.int32)
    return rank


def request_kernel(capacity, owner_ref, block_ref, migration_ref, out_ref):
    owners = out_ref.shape[0]
    tiles = owner_ref.shape[2]
    lane = lax.broadcasted_iota(jnp.int32, (owners, BLOCK), 1)
    row = lax.broadcasted_iota(jnp.int32, (owners, BLOCK), 0)
    place = row * BLOCK + lane
    message = jnp.full((owners, BLOCK), -1, jnp.int32)
    for step in range(ITERS):
        names = [owner_ref[step, 0, t, j] for t in range(tiles) for j in range(LISTB)]
        for index in range(tiles * LISTB):
            target = names[index] * BLOCK + step * capacity + rank_of(names, index)
            block = block_ref[step, 0, index // LISTB, index % LISTB]
            message = jnp.where(place == target, block, message)
    for side in range(2):
        for j in range(MIGH):
            message = jnp.where(
                lane == MIG_LANE + side * MIGH + j, migration_ref[0, side, j], message
            )
    for owner in range(owners):
        out_ref[owner] = message[owner : owner + 1]


def geometry(row):
    scales = [jnp.exp(row(3 + k)) for k in range(3)]
    quats = [row(6 + k) for k in range(4)]
    norm = lax.rsqrt(
        quats[0] * quats[0] + quats[1] * quats[1] + quats[2] * quats[2] + quats[3] * quats[3]
    )
    w, x, y, z = [part * norm for part in quats]
    rotation = [
        [1.0 - 2.0 * (y * y + z * z), 2.0 * (x * y - w * z), 2.0 * (x * z + w * y)],
        [2.0 * (x * y + w * z), 1.0 - 2.0 * (x * x + z * z), 2.0 * (y * z - w * x)],
        [2.0 * (x * z - w * y), 2.0 * (y * z + w * x), 1.0 - 2.0 * (x * x + y * y)],
    ]
    return scales, (w, x, y, z), norm, rotation


def conic_of(scales, rotation, affine):
    spread = [
        [
            (
                affine[3 * i] * rotation[0][k]
                + affine[3 * i + 1] * rotation[1][k]
                + affine[3 * i + 2] * rotation[2][k]
            )
            * scales[k]
            for k in range(3)
        ]
        for i in range(2)
    ]
    one, two = spread
    cov_xx = one[0] * one[0] + one[1] * one[1] + one[2] * one[2] + 0.3
    cov_yy = two[0] * two[0] + two[1] * two[1] + two[2] * two[2] + 0.3
    cov_xy = one[0] * two[0] + one[1] * two[1] + one[2] * two[2]
    inverse = 1.0 / (cov_xx * cov_yy - cov_xy * cov_xy)
    return cov_yy * inverse, -cov_xy * inverse, cov_xx * inverse


def serve(step, capacity, blocks, camera_ref, asked_ref, dense, table, faint, out_ref):
    cam = [camera_ref[step, 0, k] for k in range(11)]
    basis = harmonics(cam[8], cam[9], cam[10])
    for group in range(blocks // 8):

        def row(p):
            return dense[p * blocks + 8 * group : p * blocks + 8 * group + 8, :]

        scales, _, _, rotation = geometry(row)
        conic = conic_of(scales, rotation, cam)
        means = [row(k) for k in range(3)]
        rows = [
            cam[0] * means[0] + cam[1] * means[1] + cam[2] * means[2] + cam[6],
            cam[3] * means[0] + cam[4] * means[1] + cam[5] * means[2] + cam[7],
            conic[0],
            conic[1],
            conic[2],
        ]
        for k in range(3):
            colour = basis[0] * row(11 + k)
            for j in range(1, 16):
                colour = colour + basis[j] * row(11 + 3 * j + k)
            rows.append(0.5 + colour)
        for k in range(8):
            table[pl.ds(64 * group + k, 8, stride=8), :] = rows[k]
        faint[8 * group : 8 * group + 8, :] = -LOG2E * jnp.log(1.0 + jnp.exp(-row(10)))
    owners = out_ref.shape[0]
    for peer in range(owners):
        for slot in range(capacity):
            block = jnp.maximum(asked_ref[peer, 0, step * capacity + slot], 0)
            out_ref[peer, 8 * slot : 8 * slot + 8, :] = table[
                pl.ds(pl.multiple_of(block * 8, 8), 8), :
            ]
            out_ref[peer, 8 * capacity + slot : 8 * capacity + slot + 1, :] = faint[
                pl.ds(block, 1), :
            ]


def row_groups():
    return [(first, min(8, P_SIZE - first)) for first in range(0, P_SIZE, 8)]


def start_kernel(capacity, params_ref, camera_ref, asked_ref, out_ref, dense, table, faint):
    blocks = params_ref.shape[1] // BLOCK
    for block in range(blocks):
        for first, count in row_groups():
            dense[pl.ds(first * blocks + block, count, stride=blocks), :] = params_ref[
                first : first + count, block * BLOCK : (block + 1) * BLOCK
            ]
    serve(0, capacity, blocks, camera_ref, asked_ref, dense, table, faint, out_ref)


def pixel_features(rows, per):
    pixel = lax.broadcasted_iota(jnp.int32, (rows, PIX), 1)
    which = lax.broadcasted_iota(jnp.int32, (rows, PIX), 0) // per
    px = (pixel % SIDE).astype(f32) - (SIDE / 2 - 0.5)
    py = (pixel // SIDE).astype(f32) - (SIDE / 2 - 0.5)
    chosen = jnp.where(which == 0, 1.0, 0.0)
    for index, value in enumerate((px, py, px * px, px * py, py * py)):
        chosen = jnp.where(which == index + 1, value, chosen)
    return chosen.astype(bf16)


def lane_gather(pieces, within, source):
    got = jnp.take_along_axis(pieces[0], within, axis=1)
    for j in range(1, len(pieces)):
        got = jnp.where(source == j, jnp.take_along_axis(pieces[j], within, axis=1), got)
    return got


def render_kernel(step, capacity, slots, final, *refs):
    if final:
        (
            arrived, corner_ref, owner_ref, block_ref, asked_ref, order_ref, target_ref, earlier_ref,
            picture_ref, out_ref, onehot, coeffs, alphas, locals_, weights, weight_h, weight_m,
            flows, behind, heat_h, heat_m,
        ) = refs
        for other in range(ITERS - 1):
            picture_ref[other] = earlier_ref[other]
    else:
        (
            arrived, corner_ref, owner_ref, order_ref, target_ref,
            picture_ref, out_ref, onehot, coeffs, alphas, locals_, weights, weight_h, weight_m,
            flows, behind, heat_h, heat_m,
        ) = refs
    owners = arrived.shape[0]
    tiles = owner_ref.shape[2]
    lists = DEPTH // BLOCK
    segments = 8
    steps = DEPTH // segments
    out_ref[...] = jnp.zeros_like(out_ref)
    coeffs[...] = jnp.zeros_like(coeffs)
    features = pixel_features(32, 3)
    flat = pixel_features(16, 1)

    names = [owner_ref[step, 0, t, j] for t in range(tiles) for j in range(LISTB)]
    ranks = [rank_of(names, index) for index in range(tiles * LISTB)]

    order = order_ref[step, 0]
    order = jnp.concatenate([order, order], axis=0) if tiles == 4 else order
    order_pieces = [order[:, k * BLOCK : (k + 1) * BLOCK] for k in range(lists)]
    woven = []
    for k in range(lists):
        row = lax.broadcasted_iota(jnp.int32, order_pieces[0].shape, 1) + k * BLOCK
        nth = (row % segments) * steps + row // segments
        woven.append(lane_gather(order_pieces, nth & (BLOCK - 1), nth // BLOCK))
    all_within = [piece & (BLOCK - 1) for piece in woven]
    all_source = [piece // BLOCK for piece in woven]
    faint_pieces = []
    for j in range(LISTB):
        parts = [
            arrived[
                names[t * LISTB + j], pl.ds(8 * capacity + ranks[t * LISTB + j], 1), :
            ]
            for t in range(tiles)
        ]
        faint_pieces.append(jnp.concatenate(parts * (8 // tiles), axis=0))
    all_faint = [
        lane_gather(faint_pieces, all_within[k], all_source[k]) for k in range(lists)
    ]
    row_id = lax.broadcasted_iota(jnp.int32, (BLOCK, BLOCK), 0).astype(f32).astype(bf16)
    sub = lax.broadcasted_iota(jnp.int32, (segments, PIX), 0)

    for tile in range(tiles):
        one = slice(tile, tile + 1)
        pieces = [
            arrived[
                names[tile * LISTB + j],
                pl.ds(pl.multiple_of(ranks[tile * LISTB + j] * 8, 8), 8),
                :,
            ]
            for j in range(LISTB)
        ]
        sorted_rows = []
        for k in range(lists):
            within = jnp.broadcast_to(all_within[k][one], (8, BLOCK))
            source = jnp.broadcast_to(all_source[k][one], (8, BLOCK))
            sorted_rows.append(lane_gather(pieces, within, source))
            local = woven[k][one].astype(f32)
            for piece in range(lists):
                inside = jnp.where(all_source[k][one] == piece, local - piece * BLOCK, -1.0)
                onehot[
                    piece * BLOCK : (piece + 1) * BLOCK, k * BLOCK : (k + 1) * BLOCK
                ] = jnp.where(row_id == inside.astype(bf16), jnp.ones((), bf16), jnp.zeros((), bf16))
        rows = jnp.concatenate(sorted_rows, axis=1)
        faint = jnp.concatenate([part[one] for part in all_faint], axis=1)
        u = rows[0:1] - (corner_ref[step, 0, 0, tile] + SIDE / 2)
        v = rows[1:2] - (corner_ref[step, 0, 1, tile] + SIDE / 2)
        a, b, c = rows[2:3], rows[3:4], rows[4:5]
        colours = rows[5:8]
        half_a, half_b, half_c = (-0.5 * LOG2E) * a, -LOG2E * b, (-0.5 * LOG2E) * c
        values = (
            half_a * u * u + half_b * u * v + half_c * v * v + faint,
            -(2.0 * half_a * u + half_b * v),
            -(2.0 * half_c * v + half_b * u),
            half_a,
            half_b,
            half_c,
        )
        for index, value in enumerate(values):
            for piece, part in enumerate(split(value, 3)):
                coeffs[3 * index + piece : 3 * index + piece + 1, :] = part.astype(f32)
        form = coeffs[...].astype(bf16)
        col_h, col_m, col_l = [part.astype(f32) for part in split(colours, 3)]
        col_left = jnp.concatenate([col_h, col_m, col_l], axis=0).astype(bf16)
        col_right = jnp.concatenate(
            [col_h, col_m, col_h, col_m, col_l, col_h], axis=0
        ).astype(bf16)

        passed = jnp.ones((segments, PIX), f32)
        for k in range(lists):
            power = dot(form[:, k * BLOCK : (k + 1) * BLOCK], features, TN)
            for at in range(0, BLOCK, segments):
                here = slice(k * BLOCK + at, k * BLOCK + at + segments)
                alpha = jnp.exp2(power[at : at + segments])
                alphas[here, :] = alpha
                locals_[here, :] = passed
                passed = passed * (1.0 - alpha)
        for shift in (1, 2, 4):
            passed = passed * jnp.where(sub >= shift, pltpu.roll(passed, shift, 0), 1.0)
        passed = jnp.where(sub >= 1, pltpu.roll(passed, 1, 0), 1.0)
        passed = jnp.concatenate([passed, passed], axis=0)
        for at in range(0, DEPTH, 2 * segments):
            here = slice(at, at + 2 * segments)
            weight = alphas[here, :] * (locals_[here, :] * passed)
            weights[here, :] = weight
            weight_h[here, :], weight_m[here, :] = split(weight, 2)

        shades = dot(col_left, weight_h[...]) + dot(col_left, weight_m[...])
        shades = shades[0:3] + shades[3:6] + shades[6:9]
        for k in range(3):
            picture_ref[step, 0, k, one, :] = shades[k : k + 1]
        error = shades - jnp.concatenate(
            [target_ref[step, 0, k, one, :] for k in range(3)], axis=0
        )
        err_h, err_m, err_l = [part.astype(f32) for part in split(error, 3)]
        err_left = jnp.concatenate([err_h, err_m, err_l], axis=0).astype(bf16)
        err_right = jnp.concatenate(
            [err_h, err_h, err_m, err_m, err_h, err_l], axis=0
        ).astype(bf16)
        col_grads = dot(err_left, weight_h[...], NT) + dot(err_left, weight_m[...], NT)

        total = jnp.zeros((segments, PIX), f32)
        for k in reversed(range(lists)):
            seen = dot(col_right[:, k * BLOCK : (k + 1) * BLOCK], err_right, TN)
            for at in reversed(range(0, BLOCK, segments)):
                here = slice(k * BLOCK + at, k * BLOCK + at + segments)
                flow = weights[here, :] * seen[at : at + segments]
                flows[here, :] = flow
                behind[here, :] = total
                total = total + flow
        for shift in (1, 2, 4):
            total = total + jnp.where(
                sub < segments - shift, pltpu.roll(total, segments - shift, 0), 0.0
            )
        total = jnp.where(sub < segments - 1, pltpu.roll(total, segments - 1, 0), 0.0)
        total = jnp.concatenate([total, total], axis=0)
        for at in range(0, DEPTH, 2 * segments):
            here = slice(at, at + 2 * segments)
            alpha = alphas[here, :]
            heat = flows[here, :] - (alpha / (1.0 - alpha)) * (behind[here, :] + total)
            heat_h[here, :], heat_m[here, :] = split(heat, 2)
        moments = dot(flat, heat_h[...], NT) + dot(flat, heat_m[...], NT)

        col_grads = col_grads[0:3] + col_grads[3:6] + col_grads[6:9]
        m00, m10, m01 = moments[0:1], moments[1:2], moments[2:3]
        m20, m11, m02 = moments[3:4], moments[4:5], moments[5:6]
        x1, y1 = m10 - u * m00, m01 - v * m00
        grads = [
            a * x1 + b * y1,
            b * x1 + c * y1,
            -0.5 * (m20 - 2.0 * u * m10 + u * u * m00),
            -(m11 - u * m01 - v * m10 + u * v * m00),
            -0.5 * (m02 - 2.0 * v * m01 + v * v * m00),
            col_grads,
            m00,
            jnp.zeros((7, DEPTH), f32),
        ]
        grads = jnp.concatenate(grads, axis=0)
        listed = dot(jnp.concatenate(split(grads, 3), axis=0), onehot[...], NT)
        listed = listed[0:16] + listed[16:32] + listed[32:48]
        for j in range(LISTB):
            name, rank = names[tile * LISTB + j], ranks[tile * LISTB + j]
            if final:
                block = block_ref[step, 0, tile, j]
                hop = jnp.int32(0)
                for k in range(MIGH):
                    goes_left = asked_ref[name, 0, MIG_LANE + k] == block
                    goes_right = asked_ref[name, 0, MIG_LANE + MIGH + k] == block
                    rank = jnp.where(goes_left, capacity + MIGH + k, rank)
                    rank = jnp.where(goes_right, capacity + k, rank)
                    hop = hop - goes_left.astype(jnp.int32) + goes_right.astype(jnp.int32)
                name = name + hop
                name = jnp.where(name < 0, owners - 1, jnp.where(name >= owners, 0, name))
            lanes = slice(j * BLOCK, (j + 1) * BLOCK)
            main = pl.ds(pl.multiple_of(rank * 8, 8), 8)
            extra = pl.ds(8 * slots + rank, 1)
            if final:
                out_ref[name, main, :] = out_ref[name, main, :] + listed[0:8, lanes]
                out_ref[name, extra, :] = out_ref[name, extra, :] + listed[8:9, lanes]
            else:
                out_ref[name, main, :] = listed[0:8, lanes]
                out_ref[name, extra, :] = listed[8:9, lanes]


def gather_kernel(step, capacity, slots, returned, asked_ref, migration_ref, camera_ref, out_ref):
    owners = returned.shape[0]
    blocks = (out_ref.shape[0] - CAM_ROWS) // 9
    out_ref[...] = jnp.zeros_like(out_ref)

    def body(peer, carry):
        for slot in range(slots):
            if slot < capacity:
                block = jnp.maximum(asked_ref[peer, 0, step * capacity + slot], 0)
            else:
                block = migration_ref[0, (slot - capacity) // MIGH, (slot - capacity) % MIGH]
            main = pl.ds(pl.multiple_of(block * 8, 8), 8)
            extra = pl.ds(8 * blocks + block, 1)
            out_ref[main, :] = out_ref[main, :] + returned[peer, 8 * slot : 8 * slot + 8, :]
            out_ref[extra, :] = (
                out_ref[extra, :] + returned[peer, 8 * slots + slot : 8 * slots + slot + 1, :]
            )
        return carry

    lax.fori_loop(0, owners, body, 0)
    for index, k in enumerate((0, 1, 2, 3, 4, 5, 8, 9, 10)):
        at = 9 * blocks + index
        out_ref[at : at + 1, :] = jnp.full((1, BLOCK), camera_ref[step, 0, k], f32)


def collect(own_ref, others, scratch):
    mine = lax.axis_index("rep")
    scratch[mine] = own_ref[...]
    for offset, ref in others:
        scratch[mine ^ offset] = ref[...]


def pullback(blocks, cams, dense, grads):
    count = cams.shape[0]
    affine, basis = [], []
    for c in range(count):
        rows = [
            jnp.broadcast_to(cams[c, 9 * blocks + k : 9 * blocks + k + 1, :], (8, BLOCK))
            for k in range(9)
        ]
        affine.append(rows[0:6])
        basis.append(harmonics(rows[6], rows[7], rows[8]))
    for group in range(blocks // 8):

        def row(p):
            return dense[p * blocks + 8 * group : p * blocks + 8 * group + 8, :]

        def put(p, value):
            grads[p * blocks + 8 * group : p * blocks + 8 * group + 8, :] = value

        given = [
            [cams[c, pl.ds(64 * group + k, 8, stride=8), :] for k in range(8)] for c in range(count)
        ]
        scales, (w, x, y, z), norm, rotation = geometry(row)
        means = [0.0, 0.0, 0.0]
        sigma = [0.0] * 6
        for c in range(count):
            m = affine[c]
            a, b, d = conic_of(scales, rotation, m)
            g_x, g_y, g_a, g_b, g_d = given[c][0:5]
            for k in range(3):
                means[k] = means[k] + m[k] * g_x + m[3 + k] * g_y
            g_b = 0.5 * g_b
            t00, t01 = a * g_a + b * g_b, a * g_b + b * g_d
            t10, t11 = b * g_a + d * g_b, b * g_b + d * g_d
            h00 = -(t00 * a + t01 * b)
            h01 = -(t00 * b + t01 * d)
            h11 = -(t10 * b + t11 * d)
            top = [h00 * m[k] + h01 * m[3 + k] for k in range(3)]
            low = [h01 * m[k] + h11 * m[3 + k] for k in range(3)]
            for index, (i, k) in enumerate(((0, 0), (0, 1), (0, 2), (1, 1), (1, 2), (2, 2))):
                sigma[index] = sigma[index] + m[i] * top[k] + m[3 + i] * low[k]
        for k in range(3):
            put(k, means[k])
        full = [
            [sigma[0], sigma[1], sigma[2]],
            [sigma[1], sigma[3], sigma[4]],
            [sigma[2], sigma[4], sigma[5]],
        ]
        turn = [[None] * 3 for _ in range(3)]
        for k in range(3):
            column = [rotation[j][k] * scales[k] for j in range(3)]
            pulled = [
                2.0 * (full[j][0] * column[0] + full[j][1] * column[1] + full[j][2] * column[2])
                for j in range(3)
            ]
            put(
                3 + k, pulled[0] * column[0] + pulled[1] * column[1] + pulled[2] * column[2]
            )
            for j in range(3):
                turn[j][k] = pulled[j] * scales[k]
        g_w = 2.0 * (
            z * (turn[1][0] - turn[0][1])
            + y * (turn[0][2] - turn[2][0])
            + x * (turn[2][1] - turn[1][2])
        )
        g_x = 2.0 * (
            y * (turn[0][1] + turn[1][0])
            + z * (turn[0][2] + turn[2][0])
            - 2.0 * x * (turn[1][1] + turn[2][2])
            + w * (turn[2][1] - turn[1][2])
        )
        g_y = 2.0 * (
            x * (turn[0][1] + turn[1][0])
            + z * (turn[1][2] + turn[2][1])
            - 2.0 * y * (turn[0][0] + turn[2][2])
            + w * (turn[0][2] - turn[2][0])
        )
        g_z = 2.0 * (
            x * (turn[0][2] + turn[2][0])
            + y * (turn[1][2] + turn[2][1])
            - 2.0 * z * (turn[0][0] + turn[1][1])
            + w * (turn[1][0] - turn[0][1])
        )
        along = w * g_w + x * g_x + y * g_y + z * g_z
        for k, (part, pull) in enumerate(((w, g_w), (x, g_x), (y, g_y), (z, g_z))):
            put(6 + k, norm * (pull - part * along))
        faint = cams[0, 8 * blocks + 8 * group : 8 * blocks + 8 * group + 8, :]
        for c in range(1, count):
            faint = faint + cams[c, 8 * blocks + 8 * group : 8 * blocks + 8 * group + 8, :]
        put(10, faint / (1.0 + jnp.exp(row(10))))
        for j in range(16):
            for k in range(3):
                value = basis[0][j] * given[0][5 + k]
                for c in range(1, count):
                    value = value + basis[c][j] * given[c][5 + k]
                put(11 + 3 * j + k, value)


def adam(value, first, second, gradient):
    first = 0.9 * first + 0.1 * gradient
    second = 0.999 * second + 0.001 * gradient * gradient
    root = second * lax.rsqrt(second)
    return value - learn_rate * first / (root + adam_epsilon), first, second


def update_kernel(capacity, *refs):
    (
        own_ref, near_ref, far_ref, cross_ref, params_ref, first_ref, second_ref, camera_ref,
        asked_ref, migration_ref, new_params, new_first, new_second, out_ref, left_ref, right_ref,
        cams, dense, grads, table, faint,
    ) = refs
    blocks = params_ref.shape[1] // BLOCK
    collect(own_ref, ((1, near_ref), (2, far_ref), (3, cross_ref)), cams)
    for block in range(blocks):
        for top, count in row_groups()[:2]:
            dense[pl.ds(top * blocks + block, count, stride=blocks), :] = params_ref[
                top : top + count, block * BLOCK : (block + 1) * BLOCK
            ]
    pullback(blocks, cams, dense, grads)
    for block in range(blocks):
        lanes = slice(block * BLOCK, (block + 1) * BLOCK)
        for top, count in row_groups():
            part = slice(top, top + count)
            where = pl.ds(top * blocks + block, count, stride=blocks)
            value, first, second = adam(
                params_ref[part, lanes], first_ref[part, lanes], second_ref[part, lanes],
                grads[where, :],
            )
            new_params[part, lanes] = value
            new_first[part, lanes] = first
            new_second[part, lanes] = second
            dense[where, :] = value
    serve(1, capacity, blocks, camera_ref, asked_ref, dense, table, faint, out_ref)
    for side, ref in ((0, left_ref), (1, right_ref)):
        for j in range(MIGH):
            lanes = pl.ds(pl.multiple_of(migration_ref[0, side, j] * BLOCK, BLOCK), BLOCK)
            for index, source in enumerate((new_params, new_first, new_second)):
                ref[index, :, j * BLOCK : (j + 1) * BLOCK] = source[:, lanes]


def final_kernel(*refs):
    (
        own_ref, near_ref, far_ref, cross_ref, params_ref, first_ref, second_ref, below_ref,
        above_ref, migration_ref, new_params, new_first, new_second, cams, dense, grads,
    ) = refs
    blocks = params_ref.shape[1] // BLOCK
    collect(own_ref, ((1, near_ref), (2, far_ref), (3, cross_ref)), cams)
    for block in range(blocks):
        for top, count in row_groups()[:2]:
            dense[pl.ds(top * blocks + block, count, stride=blocks), :] = params_ref[
                top : top + count, block * BLOCK : (block + 1) * BLOCK
            ]
    moved = [
        (migration_ref[0, side, j], ref, j)
        for side, ref in ((0, below_ref), (1, above_ref))
        for j in range(MIGH)
    ]
    for block, ref, j in moved:
        for top, count in row_groups()[:2]:
            dense[pl.ds(top * blocks + block, count, stride=blocks), :] = ref[
                0, top : top + count, j * BLOCK : (j + 1) * BLOCK
            ]
    pullback(blocks, cams, dense, grads)
    for block in range(blocks):
        lanes = slice(block * BLOCK, (block + 1) * BLOCK)
        for top, count in row_groups():
            part = slice(top, top + count)
            value, first, second = adam(
                params_ref[part, lanes], first_ref[part, lanes], second_ref[part, lanes],
                grads[pl.ds(top * blocks + block, count, stride=blocks), :],
            )
            new_params[part, lanes] = value
            new_first[part, lanes] = first
            new_second[part, lanes] = second
    for block, ref, j in moved:
        lanes = pl.ds(pl.multiple_of(block * BLOCK, BLOCK), BLOCK)
        source = slice(j * BLOCK, (j + 1) * BLOCK)
        for top, count in row_groups():
            part = slice(top, top + count)
            value, first, second = adam(
                ref[0, part, source], ref[1, part, source], ref[2, part, source],
                grads[pl.ds(top * blocks + block, count, stride=blocks), :],
            )
            new_params[part, lanes] = value
            new_first[part, lanes] = first
            new_second[part, lanes] = second


def shape(dims, dtype=f32):
    return jax.ShapeDtypeStruct(dims, dtype)


def bind(kernel, *static):
    def run(*refs):
        kernel(*static, *refs)

    return run


def swap(value, axis, offset):
    count = lax.axis_size(axis)
    return lax.ppermute(value, axis, [(i, i ^ offset) for i in range(count)])


def turn(value, axis, offset):
    count = lax.axis_size(axis)
    return lax.ppermute(value, axis, [(i, (i + offset) % count) for i in range(count)])


def exchange(value):
    far = swap(value, "rep", 2)
    near = swap(value, "rep", 1)
    cross = swap(far, "rep", 1)
    return near, far, cross


def row_exchange(value):
    return lax.all_to_all(value, "row", split_axis=0, concat_axis=0, tiled=True)


def local(
    params,
    first_moment,
    second_moment,
    camera,
    tile_corner,
    tile_owner,
    tile_block,
    depth_order,
    targets,
    migration,
):
    owners = lax.axis_size("row")
    replicas = lax.axis_size("rep")
    blocks = params.shape[1] // BLOCK
    tiles = tile_owner.shape[2]
    requests = tiles * LISTB
    capacity = max(2, 2 * ((requests + owners - 1) // owners))
    slots = capacity + 2 * MIGH
    dense = pltpu.VMEM((64 * blocks, BLOCK), f32)
    table = pltpu.VMEM((8 * blocks, BLOCK), f32)
    faint = pltpu.VMEM((blocks, BLOCK), f32)
    payload = 9 * blocks + CAM_ROWS
    cams = pltpu.VMEM((replicas, payload, BLOCK), f32)
    state = [shape(params.shape)] * 3

    lists = pl.pallas_call(
        bind(request_kernel, capacity),
        out_shape=shape((owners, 1, BLOCK), jnp.int32),
        in_specs=[SM, SM, SM],
        out_specs=VM,
    )(tile_owner, tile_block, migration)
    asked = row_exchange(lists)

    outgoing = pl.pallas_call(
        bind(start_kernel, capacity),
        out_shape=shape((owners, up8(9 * capacity), BLOCK)),
        in_specs=[VM, SM, SM],
        out_specs=VM,
        scratch_shapes=[dense, table, faint],
    )(params, camera, asked)

    deep = pltpu.VMEM((DEPTH, PIX), f32)
    packed = pltpu.VMEM((DEPTH, PIX), bf16)
    render_scratch = [
        pltpu.VMEM((DEPTH, DEPTH), bf16),
        pltpu.VMEM((32, DEPTH), f32),
        deep, deep, deep, packed, packed, deep, deep, packed, packed,
    ]
    corners = jnp.swapaxes(tile_corner, 2, 3)
    photos = jnp.swapaxes(targets, 2, 3)
    pictures_shape = shape(photos.shape)

    def gather(step, count, returned):
        return pl.pallas_call(
            bind(gather_kernel, step, capacity, count),
            out_shape=shape((payload, BLOCK)),
            in_specs=[VM, SM, SM, SM],
            out_specs=VM,
        )(returned, asked, migration, camera)

    arrived = row_exchange(outgoing)
    pictures, back = pl.pallas_call(
        bind(render_kernel, 0, capacity, capacity, False),
        out_shape=[pictures_shape, shape((owners, up8(9 * capacity), BLOCK))],
        in_specs=[VM, SM, SM, VM, VM],
        out_specs=[VM, VM],
        scratch_shapes=render_scratch,
    )(arrived, corners, tile_owner, depth_order, photos)
    own = gather(0, capacity, row_exchange(back))
    near, far, cross = exchange(own)
    leaving = shape((3, P_SIZE, MIGH * BLOCK))
    current, moment_one, moment_two, outgoing, left, right = pl.pallas_call(
        bind(update_kernel, capacity),
        out_shape=state + [shape((owners, up8(9 * capacity), BLOCK)), leaving, leaving],
        in_specs=[VM] * 7 + [SM] * 3,
        out_specs=[VM] * 6,
        scratch_shapes=[cams, dense, dense, table, faint],
    )(
        own, near, far, cross, params, first_moment, second_moment, camera, asked, migration
    )
    arrived = row_exchange(outgoing)
    below = turn(right, "row", 1)
    above = turn(left, "row", -1)
    pictures, back = pl.pallas_call(
        bind(render_kernel, 1, capacity, slots, True),
        out_shape=[pictures_shape, shape((owners, up8(9 * slots), BLOCK))],
        in_specs=[VM, SM, SM, SM, SM, VM, VM, VM],
        out_specs=[VM, VM],
        scratch_shapes=render_scratch,
    )(arrived, corners, tile_owner, tile_block, asked, depth_order, photos, pictures)
    own = gather(1, slots, row_exchange(back))
    near, far, cross = exchange(own)
    current, moment_one, moment_two = pl.pallas_call(
        final_kernel,
        out_shape=state,
        in_specs=[VM] * 9 + [SM],
        out_specs=[VM] * 3,
        scratch_shapes=[cams, dense, dense],
    )(own, near, far, cross, current, moment_one, moment_two, below, above, migration)
    return current, moment_one, moment_two, jnp.swapaxes(pictures, 2, 3)


def solution(mesh):
    return jax.shard_map(
        local,
        mesh=mesh,
        in_specs=(
            P(None, "row"),
            P(None, "row"),
            P(None, "row"),
            P(None, "rep", None),
            P(None, "rep", "row", None),
            P(None, "rep", "row", None),
            P(None, "rep", "row", None),
            P(None, "rep", "row", None),
            P(None, "rep", "row", None, None),
            P("row", None, None),
        ),
        out_specs=(
            P(None, "row"),
            P(None, "row"),
            P(None, "row"),
            P(None, "rep", "row", None, None),
        ),
        check_vma=False,
    )
```

```python
import jax
import jax.numpy as jnp
from jax import lax
from jax.experimental import pallas as pl
from jax.experimental.pallas import tpu as pltpu
from jax.sharding import PartitionSpec as P


P_SIZE = 59
BLOCK = 128
LISTB = 4
PIX = 256
ITERS = 2
MIGH = 2
DEPTH = 512
SIDE = 16
MIG_LANE = 64
CAM_ROWS = 16
LOG2E = 1.4426950408889634

harm_zero = 0.28209479177387814
harm_one = 0.4886025119029199
harm_two = (
    1.0925484305920792,
    -1.0925484305920792,
    0.31539156525252005,
    -1.0925484305920792,
    0.5462742152960396,
)
harm_three = (
    -0.5900435899266435,
    2.890611442640554,
    -0.4570457994644658,
    0.3731763325901154,
    -0.4570457994644658,
    1.445305721320277,
    -0.5900435899266435,
)
learn_rate = 0.01
adam_epsilon = 1e-08

f32 = jnp.float32
bf16 = jnp.bfloat16
VM = pl.BlockSpec(memory_space=pltpu.VMEM)
SM = pl.BlockSpec(memory_space=pltpu.SMEM)


def pitch(blocks):
    return blocks + 1 - blocks % 2


def up8(count):
    return -(-count // 8) * 8


def harmonics(x, y, z):
    xx, yy, zz = x * x, y * y, z * z
    return [
        harm_zero + 0.0 * x,
        -harm_one * y,
        harm_one * z,
        -harm_one * x,
        harm_two[0] * x * y,
        harm_two[1] * y * z,
        harm_two[2] * (2.0 * zz - xx - yy),
        harm_two[3] * x * z,
        harm_two[4] * (xx - yy),
        harm_three[0] * y * (3.0 * xx - yy),
        harm_three[1] * x * y * z,
        harm_three[2] * y * (4.0 * zz - xx - yy),
        harm_three[3] * z * (2.0 * zz - 3.0 * xx - 3.0 * yy),
        harm_three[4] * x * (4.0 * zz - xx - yy),
        harm_three[5] * z * (xx - yy),
        harm_three[6] * x * (xx - 3.0 * yy),
    ]


def split(value, pieces):
    out = []
    for piece in range(pieces):
        part = value.astype(bf16)
        out.append(part)
        if piece < pieces - 1:
            value = value - part.astype(f32)
    return out


def dot(left, right, dims=((1,), (0,))):
    return lax.dot_general(left, right, (dims, ((), ())), preferred_element_type=f32)


NT = ((1,), (1,))
TN = ((0,), (0,))


def rank_of(owners, index):
    rank = jnp.int32(0)
    for other in range(index):
        rank = rank + (owners[other] == owners[index]).astype(jnp.int32)
    return rank


def request_kernel(capacity, owner_ref, block_ref, migration_ref, out_ref):
    owners = out_ref.shape[0]
    tiles = owner_ref.shape[2]
    lane = lax.broadcasted_iota(jnp.int32, (owners, BLOCK), 1)
    row = lax.broadcasted_iota(jnp.int32, (owners, BLOCK), 0)
    place = row * BLOCK + lane
    message = jnp.full((owners, BLOCK), -1, jnp.int32)
    for step in range(ITERS):
        names = [owner_ref[step, 0, t, j] for t in range(tiles) for j in range(LISTB)]
        for index in range(tiles * LISTB):
            target = names[index] * BLOCK + step * capacity + rank_of(names, index)
            block = block_ref[step, 0, index // LISTB, index % LISTB]
            message = jnp.where(place == target, block, message)
    for side in range(2):
        for j in range(MIGH):
            message = jnp.where(
                lane == MIG_LANE + side * MIGH + j, migration_ref[0, side, j], message
            )
    for owner in range(owners):
        out_ref[owner] = message[owner : owner + 1]


def geometry(row):
    scales = [jnp.exp(row(3 + k)) for k in range(3)]
    quats = [row(6 + k) for k in range(4)]
    norm = lax.rsqrt(
        quats[0] * quats[0] + quats[1] * quats[1] + quats[2] * quats[2] + quats[3] * quats[3]
    )
    w, x, y, z = [part * norm for part in quats]
    rotation = [
        [1.0 - 2.0 * (y * y + z * z), 2.0 * (x * y - w * z), 2.0 * (x * z + w * y)],
        [2.0 * (x * y + w * z), 1.0 - 2.0 * (x * x + z * z), 2.0 * (y * z - w * x)],
        [2.0 * (x * z - w * y), 2.0 * (y * z + w * x), 1.0 - 2.0 * (x * x + y * y)],
    ]
    return scales, (w, x, y, z), norm, rotation


def conic_of(scales, rotation, affine):
    spread = [
        [
            (
                affine[3 * i] * rotation[0][k]
                + affine[3 * i + 1] * rotation[1][k]
                + affine[3 * i + 2] * rotation[2][k]
            )
            * scales[k]
            for k in range(3)
        ]
        for i in range(2)
    ]
    one, two = spread
    cov_xx = one[0] * one[0] + one[1] * one[1] + one[2] * one[2] + 0.3
    cov_yy = two[0] * two[0] + two[1] * two[1] + two[2] * two[2] + 0.3
    cov_xy = one[0] * two[0] + one[1] * two[1] + one[2] * two[2]
    inverse = 1.0 / (cov_xx * cov_yy - cov_xy * cov_xy)
    return cov_yy * inverse, -cov_xy * inverse, cov_xx * inverse


def serve(step, capacity, blocks, camera_ref, asked_ref, dense, table, out_ref):
    wide = pitch(blocks)
    cam = [camera_ref[step, 0, k] for k in range(11)]
    basis = harmonics(cam[8], cam[9], cam[10])
    for group in range(blocks // 8):

        def row(p):
            return dense[p * wide + 8 * group : p * wide + 8 * group + 8, :]

        scales, _, _, rotation = geometry(row)
        conic = conic_of(scales, rotation, cam)
        means = [row(k) for k in range(3)]
        rows = [
            cam[0] * means[0] + cam[1] * means[1] + cam[2] * means[2] + cam[6],
            cam[3] * means[0] + cam[4] * means[1] + cam[5] * means[2] + cam[7],
            conic[0],
            conic[1],
            conic[2],
        ]
        for k in range(3):
            colour = basis[0] * row(11 + k)
            for j in range(1, 16):
                colour = colour + basis[j] * row(11 + 3 * j + k)
            rows.append(0.5 + colour)
        rows.append(-LOG2E * jnp.log(1.0 + jnp.exp(-row(10))))
        for k in range(9):
            table[pl.ds(72 * group + k, 8, stride=9), :] = rows[k]
    owners = out_ref.shape[0]
    for peer in range(owners):
        for slot in range(capacity):
            block = jnp.maximum(asked_ref[peer, 0, step * capacity + slot], 0)
            out_ref[peer, 8 * slot : 8 * slot + 8, :] = table[pl.ds(block * 9, 8), :]
            out_ref[peer, 8 * capacity + slot : 8 * capacity + slot + 1, :] = table[
                pl.ds(block * 9 + 8, 1), :
            ]


def row_groups():
    return [(first, min(8, P_SIZE - first)) for first in range(0, P_SIZE, 8)]


def start_kernel(capacity, params_ref, camera_ref, asked_ref, out_ref, dense, table):
    blocks = params_ref.shape[1] // BLOCK
    for block in range(blocks):
        for first, count in row_groups():
            dense[pl.ds(first * pitch(blocks) + block, count, stride=pitch(blocks)), :] = params_ref[
                first : first + count, block * BLOCK : (block + 1) * BLOCK
            ]
    serve(0, capacity, blocks, camera_ref, asked_ref, dense, table, out_ref)


def pixel_features(rows, per):
    pixel = lax.broadcasted_iota(jnp.int32, (rows, PIX), 1)
    which = lax.broadcasted_iota(jnp.int32, (rows, PIX), 0) // per
    px = (pixel % SIDE).astype(f32) - (SIDE / 2 - 0.5)
    py = (pixel // SIDE).astype(f32) - (SIDE / 2 - 0.5)
    chosen = jnp.where(which == 0, 1.0, 0.0)
    for index, value in enumerate((px, py, px * px, px * py, py * py)):
        chosen = jnp.where(which == index + 1, value, chosen)
    return chosen.astype(bf16)


def lane_gather(pieces, within, source):
    got = jnp.take_along_axis(pieces[0], within, axis=1)
    for j in range(1, len(pieces)):
        got = jnp.where(source == j, jnp.take_along_axis(pieces[j], within, axis=1), got)
    return got


HEAT_PIECES = 2


def put(ref, rows, value):
    for k in range(ref.shape[0]):
        ref[k, rows, :] = value[:, k * BLOCK : (k + 1) * BLOCK]


def get(ref, first, count):
    return jnp.concatenate([ref[k, first : first + count, :] for k in range(ref.shape[0])], axis=1)


COL_ROWS = {0: (0, 9, 15), 1: (3, 12), 2: (6,)}


def render_kernel(step, capacity, slots, final, *refs):
    if final:
        (
            arrived, corner_ref, owner_ref, block_ref, asked_ref, order_ref, target_ref, earlier_ref,
            picture_ref, out_ref, *scratch,
        ) = refs
        for other in range(ITERS - 1):
            picture_ref[other] = earlier_ref[other]
    else:
        arrived, corner_ref, owner_ref, order_ref, target_ref, picture_ref, out_ref, *scratch = refs
    onehots, sorted_ref, coeffs, shades_ref, sums_ref, grads_ref, *per_tile = scratch
    owners = arrived.shape[0]
    tiles = owner_ref.shape[2]
    lists = DEPTH // BLOCK
    segments = 8
    steps = DEPTH // segments
    out_ref[...] = jnp.zeros_like(out_ref)
    coeffs[...] = jnp.zeros_like(coeffs)
    features = pixel_features(32, 3)
    flat = pixel_features(16, 1)

    names = [owner_ref[step, 0, t, j] for t in range(tiles) for j in range(LISTB)]
    ranks = [rank_of(names, index) for index in range(tiles * LISTB)]

    order = order_ref[step, 0]
    order = jnp.concatenate([order] * (8 // tiles), axis=0)
    order_pieces = [order[:, k * BLOCK : (k + 1) * BLOCK] for k in range(lists)]
    woven = []
    for k in range(lists):
        row = lax.broadcasted_iota(jnp.int32, order_pieces[0].shape, 1) + k * BLOCK
        nth = (row % segments) * steps + row // segments
        woven.append(lane_gather(order_pieces, nth & (BLOCK - 1), nth // BLOCK))
    all_within = [piece & (BLOCK - 1) for piece in woven]
    all_source = [piece // BLOCK for piece in woven]
    faint_pieces = []
    for j in range(LISTB):
        parts = [
            arrived[
                names[t * LISTB + j], pl.ds(8 * capacity + ranks[t * LISTB + j], 1), :
            ]
            for t in range(tiles)
        ]
        faint_pieces.append(jnp.concatenate(parts * (8 // tiles), axis=0))
    faint = [lane_gather(faint_pieces, all_within[k], all_source[k]) for k in range(lists)]
    faint = jnp.concatenate(faint, axis=1)[0:tiles]
    row_id = lax.broadcasted_iota(jnp.int32, (BLOCK, BLOCK), 0).astype(f32).astype(bf16)
    sub = lax.broadcasted_iota(jnp.int32, (segments, PIX), 0)

    for tile in range(tiles):
        one = slice(tile, tile + 1)
        pieces = [
            arrived[
                names[tile * LISTB + j],
                pl.ds(pl.multiple_of(ranks[tile * LISTB + j] * 8, 8), 8),
                :,
            ]
            for j in range(LISTB)
        ]
        for k in range(lists):
            within = jnp.broadcast_to(all_within[k][one], (8, BLOCK))
            source = jnp.broadcast_to(all_source[k][one], (8, BLOCK))
            sorted_ref[k, pl.ds(tile, 8, stride=9), :] = lane_gather(
                pieces, within, source
            )

    def param(k):
        return get(sorted_ref, 9 * k, tiles)

    which = lax.broadcasted_iota(jnp.int32, (tiles, DEPTH), 0)
    corner_x = jnp.zeros((tiles, DEPTH), f32)
    corner_y = jnp.zeros((tiles, DEPTH), f32)
    for tile in range(tiles):
        corner_x = jnp.where(which == tile, corner_ref[step, 0, 0, tile], corner_x)
        corner_y = jnp.where(which == tile, corner_ref[step, 0, 1, tile], corner_y)
    all_u = u = param(0) - (corner_x + SIDE / 2)
    all_v = v = param(1) - (corner_y + SIDE / 2)
    half_a, half_b, half_c = (
        (-0.5 * LOG2E) * param(2), -LOG2E * param(3), (-0.5 * LOG2E) * param(4)
    )
    values = (
        half_a * u * u + half_b * u * v + half_c * v * v + faint,
        -(2.0 * half_a * u + half_b * v),
        -(2.0 * half_c * v + half_b * u),
        half_a,
        half_b,
        half_c,
    )
    for index, value in enumerate(values):
        for piece, part in enumerate(split(value, 3)):
            put(coeffs, pl.ds(3 * index + piece, tiles, stride=33), part.astype(f32))
    for k in range(3):
        for piece, part in enumerate(split(param(5 + k), 3)):
            for at in COL_ROWS[piece]:
                put(shades_ref, pl.ds(at + k, tiles, stride=19), part.astype(f32))

    def opening(tile, ratios, locals_, weight_h, weight_m, mixed, heats):
        form = get(coeffs, 33 * tile, 32).astype(bf16)
        passed = jnp.ones((segments, PIX), f32)
        for k in range(lists):
            power = dot(form[:, k * BLOCK : (k + 1) * BLOCK], features, TN)
            for at in range(0, BLOCK, segments):
                here = slice(k * BLOCK + at, k * BLOCK + at + segments)
                alpha = jnp.exp2(power[at : at + segments])
                keep = 1.0 - alpha
                ratios[here, :] = alpha / keep
                locals_[here, :] = alpha * passed
                passed = passed * keep
        for shift in (1, 2, 4):
            passed = passed * jnp.where(sub >= shift, pltpu.roll(passed, shift, 0), 1.0)
        return jnp.where(sub >= 1, pltpu.roll(passed, 1, 0), 1.0)

    def picture(tile, passed, ratios, locals_, weight_h, weight_m, mixed, heats):
        one = slice(tile, tile + 1)
        twice = jnp.concatenate([passed, passed], axis=0)
        for at in range(0, DEPTH, 2 * segments):
            here = slice(at, at + 2 * segments)
            weight_h[here, :], weight_m[here, :] = split(locals_[here, :] * twice, 2)
        col_left = get(shades_ref, 19 * tile, 9).astype(bf16)
        shades = dot(col_left, weight_h[...]) + dot(col_left, weight_m[...])
        shades = shades[0:3] + shades[3:6] + shades[6:9]
        for k in range(3):
            picture_ref[step, 0, k, one, :] = shades[k : k + 1]
        error = shades - jnp.concatenate(
            [target_ref[step, 0, k, one, :] for k in range(3)], axis=0
        )
        err_h, err_m, err_l = [part.astype(f32) for part in split(error, 3)]
        return jnp.concatenate([err_h, err_h, err_h, err_m, err_m, err_l], axis=0).astype(bf16)

    def closing(tile, passed, errors, ratios, locals_, weight_h, weight_m, mixed, heats):
        err_left = jnp.concatenate(
            [errors.astype(f32)[0:3], errors.astype(f32)[9:12], errors.astype(f32)[15:18]], axis=0
        ).astype(bf16)
        col_grads = dot(err_left, weight_h[...], NT) + dot(err_left, weight_m[...], NT)
        put(sums_ref, pl.ds(72 + tile, 8, stride=9), col_grads[0:8])
        put(sums_ref, slice(144 + tile, 145 + tile), col_grads[8:9])
        col_right = get(shades_ref, 19 * tile, 18).astype(bf16)
        total = jnp.zeros((segments, PIX), f32)
        for k in reversed(range(lists)):
            seen = dot(col_right[:, k * BLOCK : (k + 1) * BLOCK], errors, TN)
            for at in reversed(range(0, BLOCK, segments)):
                here = slice(k * BLOCK + at, k * BLOCK + at + segments)
                flow = locals_[here, :] * passed * seen[at : at + segments]
                mixed[here, :] = flow - ratios[here, :] * total
                total = total + flow
        for shift in (1, 2, 4):
            total = total + jnp.where(
                sub < segments - shift, pltpu.roll(total, segments - shift, 0), 0.0
            )
        total = jnp.where(sub < segments - 1, pltpu.roll(total, segments - 1, 0), 0.0)
        twice = jnp.concatenate([total, total], axis=0)
        for at in range(0, DEPTH, 2 * segments):
            here = slice(at, at + 2 * segments)
            parts = split(mixed[here, :] - ratios[here, :] * twice, HEAT_PIECES)
            for ref, part in zip(heats, parts):
                ref[here, :] = part
        moments = dot(flat, heats[0][...], NT)
        for ref in heats[1:]:
            moments = moments + dot(flat, ref[...], NT)
        put(sums_ref, pl.ds(tile, 8, stride=9), moments[0:8])

    def unsort_matrix(tile):
        one = slice(tile, tile + 1)
        for k in range(lists):
            local = woven[k][one].astype(f32)
            for piece in range(lists):
                inside = jnp.where(all_source[k][one] == piece, local - piece * BLOCK, -1.0)
                onehots[
                    tile, piece * BLOCK : (piece + 1) * BLOCK, k * BLOCK : (k + 1) * BLOCK
                ] = jnp.where(row_id == inside.astype(bf16), jnp.ones((), bf16), jnp.zeros((), bf16))

    def buffers(tile):
        each = len(per_tile) // tiles
        mine = per_tile[each * tile : each * tile + each]
        return (*mine[0:5], mine[5:])

    def finish(first, count):
        def summed(row):
            return get(sums_ref, 9 * row + first, count)

        group = slice(first, first + count)
        a, b, c = [get(sorted_ref, 9 * k + first, count) for k in (2, 3, 4)]
        u, v = all_u[group], all_v[group]
        m00, m10, m01, m20, m11, m02 = [summed(k) for k in range(6)]
        x1, y1 = m10 - u * m00, m01 - v * m00
        grads = [
            a * x1 + b * y1,
            b * x1 + c * y1,
            -0.5 * (m20 - 2.0 * u * m10 + u * u * m00),
            -(m11 - u * m01 - v * m10 + u * v * m00),
            -0.5 * (m02 - 2.0 * v * m01 + v * v * m00),
            *[summed(8 + k) + summed(11 + k) + summed(14 + k) for k in range(3)],
            m00,
        ]
        for k, value in enumerate(grads):
            for piece, part in enumerate(split(value, 3)):
                put(grads_ref, pl.ds(49 * first + 16 * piece + k, count, stride=49), part.astype(f32))
        for tile in range(first, first + count):
            unsort(tile)

    def unsort(tile):
        listed = dot(get(grads_ref, 49 * tile, 48).astype(bf16), onehots[tile], NT)
        listed = listed[0:16] + listed[16:32] + listed[32:48]
        for j in range(LISTB):
            name, rank = names[tile * LISTB + j], ranks[tile * LISTB + j]
            if final:
                block = block_ref[step, 0, tile, j]
                hop = jnp.int32(0)
                for k in range(MIGH):
                    goes_left = asked_ref[name, 0, MIG_LANE + k] == block
                    goes_right = asked_ref[name, 0, MIG_LANE + MIGH + k] == block
                    rank = jnp.where(goes_left, capacity + MIGH + k, rank)
                    rank = jnp.where(goes_right, capacity + k, rank)
                    hop = hop - goes_left.astype(jnp.int32) + goes_right.astype(jnp.int32)
                name = name + hop
                name = jnp.where(name < 0, owners - 1, jnp.where(name >= owners, 0, name))
            lanes = slice(j * BLOCK, (j + 1) * BLOCK)
            main = pl.ds(pl.multiple_of(rank * 8, 8), 8)
            extra = pl.ds(8 * slots + rank, 1)
            if final:
                out_ref[name, main, :] = out_ref[name, main, :] + listed[0:8, lanes]
                out_ref[name, extra, :] = out_ref[name, extra, :] + listed[8:9, lanes]
            else:
                out_ref[name, main, :] = listed[0:8, lanes]
                out_ref[name, extra, :] = listed[8:9, lanes]


    passes, errors = {}, {}
    for tile in range(tiles):
        passes[tile] = opening(tile, *buffers(tile))
    for tile in range(tiles):
        errors[tile] = picture(tile, passes[tile], *buffers(tile))
    for tile in range(tiles):
        unsort_matrix(tile)
    for tile in range(tiles):
        closing(tile, passes[tile], errors[tile], *buffers(tile))
        if tile % 2 == 1 or tile == tiles - 1:
            finish(tile - tile % 2, 1 + tile % 2)


def gather_kernel(step, capacity, slots, returned, asked_ref, migration_ref, camera_ref, out_ref):
    owners = returned.shape[0]
    blocks = (out_ref.shape[0] - CAM_ROWS) // 9
    out_ref[...] = jnp.zeros_like(out_ref)

    def body(peer, carry):
        for slot in range(slots):
            if slot < capacity:
                block = jnp.maximum(asked_ref[peer, 0, step * capacity + slot], 0)
            else:
                block = migration_ref[0, (slot - capacity) // MIGH, (slot - capacity) % MIGH]
            main = pl.ds(block * 9, 8)
            extra = pl.ds(block * 9 + 8, 1)
            out_ref[main, :] = out_ref[main, :] + returned[peer, 8 * slot : 8 * slot + 8, :]
            out_ref[extra, :] = (
                out_ref[extra, :] + returned[peer, 8 * slots + slot : 8 * slots + slot + 1, :]
            )
        return carry

    lax.fori_loop(0, owners, body, 0)
    for index, k in enumerate((0, 1, 2, 3, 4, 5, 8, 9, 10)):
        at = 9 * blocks + index
        out_ref[at : at + 1, :] = jnp.full((1, BLOCK), camera_ref[step, 0, k], f32)


def collect(own_ref, others, scratch):
    mine = lax.axis_index("rep")
    scratch[mine] = own_ref[...]
    for offset, ref in others:
        scratch[mine ^ offset] = ref[...]


def pullback(blocks, cams, dense, grads):
    count = cams.shape[0]
    wide = pitch(blocks)
    affine, basis = [], []
    for c in range(count):
        rows = [
            jnp.broadcast_to(cams[c, 9 * blocks + k : 9 * blocks + k + 1, :], (8, BLOCK))
            for k in range(9)
        ]
        affine.append(rows[0:6])
        basis.append(harmonics(rows[6], rows[7], rows[8]))
    for group in range(blocks // 8):

        def row(p):
            return dense[p * wide + 8 * group : p * wide + 8 * group + 8, :]

        def put(p, value):
            grads[p * wide + 8 * group : p * wide + 8 * group + 8, :] = value

        given = [
            [cams[c, pl.ds(72 * group + k, 8, stride=9), :] for k in range(9)] for c in range(count)
        ]
        scales, (w, x, y, z), norm, rotation = geometry(row)
        means = [0.0, 0.0, 0.0]
        sigma = [0.0] * 6
        for c in range(count):
            m = affine[c]
            a, b, d = conic_of(scales, rotation, m)
            g_x, g_y, g_a, g_b, g_d = given[c][0:5]
            for k in range(3):
                means[k] = means[k] + m[k] * g_x + m[3 + k] * g_y
            g_b = 0.5 * g_b
            t00, t01 = a * g_a + b * g_b, a * g_b + b * g_d
            t10, t11 = b * g_a + d * g_b, b * g_b + d * g_d
            h00 = -(t00 * a + t01 * b)
            h01 = -(t00 * b + t01 * d)
            h11 = -(t10 * b + t11 * d)
            top = [h00 * m[k] + h01 * m[3 + k] for k in range(3)]
            low = [h01 * m[k] + h11 * m[3 + k] for k in range(3)]
            for index, (i, k) in enumerate(((0, 0), (0, 1), (0, 2), (1, 1), (1, 2), (2, 2))):
                sigma[index] = sigma[index] + m[i] * top[k] + m[3 + i] * low[k]
        for k in range(3):
            put(k, means[k])
        full = [
            [sigma[0], sigma[1], sigma[2]],
            [sigma[1], sigma[3], sigma[4]],
            [sigma[2], sigma[4], sigma[5]],
        ]
        turn = [[None] * 3 for _ in range(3)]
        for k in range(3):
            column = [rotation[j][k] * scales[k] for j in range(3)]
            pulled = [
                2.0 * (full[j][0] * column[0] + full[j][1] * column[1] + full[j][2] * column[2])
                for j in range(3)
            ]
            put(
                3 + k, pulled[0] * column[0] + pulled[1] * column[1] + pulled[2] * column[2]
            )
            for j in range(3):
                turn[j][k] = pulled[j] * scales[k]
        g_w = 2.0 * (
            z * (turn[1][0] - turn[0][1])
            + y * (turn[0][2] - turn[2][0])
            + x * (turn[2][1] - turn[1][2])
        )
        g_x = 2.0 * (
            y * (turn[0][1] + turn[1][0])
            + z * (turn[0][2] + turn[2][0])
            - 2.0 * x * (turn[1][1] + turn[2][2])
            + w * (turn[2][1] - turn[1][2])
        )
        g_y = 2.0 * (
            x * (turn[0][1] + turn[1][0])
            + z * (turn[1][2] + turn[2][1])
            - 2.0 * y * (turn[0][0] + turn[2][2])
            + w * (turn[0][2] - turn[2][0])
        )
        g_z = 2.0 * (
            x * (turn[0][2] + turn[2][0])
            + y * (turn[1][2] + turn[2][1])
            - 2.0 * z * (turn[0][0] + turn[1][1])
            + w * (turn[1][0] - turn[0][1])
        )
        along = w * g_w + x * g_x + y * g_y + z * g_z
        for k, (part, pull) in enumerate(((w, g_w), (x, g_x), (y, g_y), (z, g_z))):
            put(6 + k, norm * (pull - part * along))
        faint = given[0][8]
        for c in range(1, count):
            faint = faint + given[c][8]
        put(10, faint / (1.0 + jnp.exp(row(10))))
        for j in range(16):
            for k in range(3):
                value = basis[0][j] * given[0][5 + k]
                for c in range(1, count):
                    value = value + basis[c][j] * given[c][5 + k]
                put(11 + 3 * j + k, value)


def adam(value, first, second, gradient):
    first = 0.9 * first + 0.1 * gradient
    second = 0.999 * second + 0.001 * gradient * gradient
    root = second * lax.rsqrt(second)
    return value - learn_rate * first / (root + adam_epsilon), first, second


def update_kernel(capacity, *refs):
    (
        own_ref, near_ref, far_ref, cross_ref, params_ref, first_ref, second_ref, camera_ref,
        asked_ref, migration_ref, new_params, new_first, new_second, out_ref, left_ref, right_ref,
        cams, dense, grads, table,
    ) = refs
    blocks = params_ref.shape[1] // BLOCK
    wide = pitch(blocks)
    collect(own_ref, ((1, near_ref), (2, far_ref), (3, cross_ref)), cams)
    for block in range(blocks):
        for top, count in row_groups()[:2]:
            dense[pl.ds(top * wide + block, count, stride=wide), :] = params_ref[
                top : top + count, block * BLOCK : (block + 1) * BLOCK
            ]
    pullback(blocks, cams, dense, grads)
    for block in range(blocks):
        lanes = slice(block * BLOCK, (block + 1) * BLOCK)
        for top, count in row_groups():
            part = slice(top, top + count)
            where = pl.ds(top * wide + block, count, stride=wide)
            value, first, second = adam(
                params_ref[part, lanes], first_ref[part, lanes], second_ref[part, lanes],
                grads[where, :],
            )
            new_params[part, lanes] = value
            new_first[part, lanes] = first
            new_second[part, lanes] = second
            dense[where, :] = value
    serve(1, capacity, blocks, camera_ref, asked_ref, dense, table, out_ref)
    for side, ref in ((0, left_ref), (1, right_ref)):
        for j in range(MIGH):
            lanes = pl.ds(pl.multiple_of(migration_ref[0, side, j] * BLOCK, BLOCK), BLOCK)
            for index, source in enumerate((new_params, new_first, new_second)):
                ref[index, :, j * BLOCK : (j + 1) * BLOCK] = source[:, lanes]


def final_kernel(*refs):
    (
        own_ref, near_ref, far_ref, cross_ref, params_ref, first_ref, second_ref, below_ref,
        above_ref, migration_ref, new_params, new_first, new_second, cams, dense, grads,
    ) = refs
    blocks = params_ref.shape[1] // BLOCK
    wide = pitch(blocks)
    collect(own_ref, ((1, near_ref), (2, far_ref), (3, cross_ref)), cams)
    for block in range(blocks):
        for top, count in row_groups()[:2]:
            dense[pl.ds(top * wide + block, count, stride=wide), :] = params_ref[
                top : top + count, block * BLOCK : (block + 1) * BLOCK
            ]
    moved = [
        (migration_ref[0, side, j], ref, j)
        for side, ref in ((0, below_ref), (1, above_ref))
        for j in range(MIGH)
    ]
    for block, ref, j in moved:
        for top, count in row_groups()[:2]:
            dense[pl.ds(top * wide + block, count, stride=wide), :] = ref[
                0, top : top + count, j * BLOCK : (j + 1) * BLOCK
            ]
    pullback(blocks, cams, dense, grads)
    for block in range(blocks):
        lanes = slice(block * BLOCK, (block + 1) * BLOCK)
        for top, count in row_groups():
            part = slice(top, top + count)
            value, first, second = adam(
                params_ref[part, lanes], first_ref[part, lanes], second_ref[part, lanes],
                grads[pl.ds(top * wide + block, count, stride=wide), :],
            )
            new_params[part, lanes] = value
            new_first[part, lanes] = first
            new_second[part, lanes] = second
    for block, ref, j in moved:
        lanes = pl.ds(pl.multiple_of(block * BLOCK, BLOCK), BLOCK)
        source = slice(j * BLOCK, (j + 1) * BLOCK)
        for top, count in row_groups():
            part = slice(top, top + count)
            value, first, second = adam(
                ref[0, part, source], ref[1, part, source], ref[2, part, source],
                grads[pl.ds(top * wide + block, count, stride=wide), :],
            )
            new_params[part, lanes] = value
            new_first[part, lanes] = first
            new_second[part, lanes] = second


def shape(dims, dtype=f32):
    return jax.ShapeDtypeStruct(dims, dtype)


def bind(kernel, *static):
    def run(*refs):
        kernel(*static, *refs)

    return run


def swap(value, axis, offset):
    count = lax.axis_size(axis)
    return lax.ppermute(value, axis, [(i, i ^ offset) for i in range(count)])


def turn(value, axis, offset):
    count = lax.axis_size(axis)
    return lax.ppermute(value, axis, [(i, (i + offset) % count) for i in range(count)])


def exchange(value):
    far = swap(value, "rep", 2)
    near = swap(value, "rep", 1)
    cross = swap(far, "rep", 1)
    return near, far, cross


def row_exchange(value):
    return lax.all_to_all(value, "row", split_axis=0, concat_axis=0, tiled=True)


def local(
    params,
    first_moment,
    second_moment,
    camera,
    tile_corner,
    tile_owner,
    tile_block,
    depth_order,
    targets,
    migration,
):
    owners = lax.axis_size("row")
    replicas = lax.axis_size("rep")
    blocks = params.shape[1] // BLOCK
    tiles = tile_owner.shape[2]
    requests = tiles * LISTB
    capacity = max(2, 2 * ((requests + owners - 1) // owners))
    slots = capacity + 2 * MIGH
    dense = pltpu.VMEM((64 * pitch(blocks), BLOCK), f32)
    table = pltpu.VMEM((9 * blocks, BLOCK), f32)
    payload = 9 * blocks + CAM_ROWS
    cams = pltpu.VMEM((replicas, payload, BLOCK), f32)
    state = [shape(params.shape)] * 3

    lists = pl.pallas_call(
        bind(request_kernel, capacity),
        out_shape=shape((owners, 1, BLOCK), jnp.int32),
        in_specs=[SM, SM, SM],
        out_specs=VM,
    )(tile_owner, tile_block, migration)
    asked = row_exchange(lists)

    outgoing = pl.pallas_call(
        bind(start_kernel, capacity),
        out_shape=shape((owners, up8(9 * capacity), BLOCK)),
        in_specs=[VM, SM, SM],
        out_specs=VM,
        scratch_shapes=[dense, table],
    )(params, camera, asked)

    deep = pltpu.VMEM((DEPTH, PIX), f32)
    packed = pltpu.VMEM((DEPTH, PIX), bf16)
    render_scratch = [
        pltpu.VMEM((tiles, DEPTH, DEPTH), bf16),
        pltpu.VMEM((DEPTH // BLOCK, 80, BLOCK), f32),
        pltpu.VMEM((DEPTH // BLOCK, 33 * tiles, BLOCK), f32),
        pltpu.VMEM((DEPTH // BLOCK, 19 * tiles, BLOCK), f32),
        pltpu.VMEM((DEPTH // BLOCK, 160, BLOCK), f32),
        pltpu.VMEM((DEPTH // BLOCK, 49 * tiles, BLOCK), f32),
    ] + [deep, deep, packed, packed, deep, *[packed] * HEAT_PIECES] * tiles
    corners = jnp.swapaxes(tile_corner, 2, 3)
    photos = jnp.swapaxes(targets, 2, 3)
    pictures_shape = shape(photos.shape)

    def gather(step, count, returned):
        return pl.pallas_call(
            bind(gather_kernel, step, capacity, count),
            out_shape=shape((payload, BLOCK)),
            in_specs=[VM, SM, SM, SM],
            out_specs=VM,
        )(returned, asked, migration, camera)

    def second(arrived, pictures):
        return pl.pallas_call(
            bind(render_kernel, 1, capacity, slots, True),
            out_shape=[pictures_shape, shape((owners, up8(9 * slots), BLOCK))],
            in_specs=[VM, SM, SM, SM, SM, VM, VM, VM],
            out_specs=[VM, VM],
            scratch_shapes=render_scratch,
        )(arrived, corners, tile_owner, tile_block, asked, depth_order, photos, pictures)

    arrived = row_exchange(outgoing)
    pictures, back = pl.pallas_call(
        bind(render_kernel, 0, capacity, capacity, False),
        out_shape=[pictures_shape, shape((owners, up8(9 * capacity), BLOCK))],
        in_specs=[VM, SM, SM, VM, VM],
        out_specs=[VM, VM],
        scratch_shapes=render_scratch,
    )(arrived, corners, tile_owner, depth_order, photos)
    own = gather(0, capacity, row_exchange(back))
    near, far, cross = exchange(own)
    leaving = shape((3, P_SIZE, MIGH * BLOCK))
    current, moment_one, moment_two, outgoing, left, right = pl.pallas_call(
        bind(update_kernel, capacity),
        out_shape=state + [shape((owners, up8(9 * capacity), BLOCK)), leaving, leaving],
        in_specs=[VM] * 7 + [SM] * 3,
        out_specs=[VM] * 6,
        scratch_shapes=[cams, dense, dense, table],
    )(
        own, near, far, cross, params, first_moment, second_moment, camera, asked, migration
    )
    arrived = row_exchange(outgoing)
    below = turn(right, "row", 1)
    above = turn(left, "row", -1)
    pictures, back = second(arrived, pictures)
    own = gather(1, slots, row_exchange(back))
    near, far, cross = exchange(own)
    current, moment_one, moment_two = pl.pallas_call(
        final_kernel,
        out_shape=state,
        in_specs=[VM] * 9 + [SM],
        out_specs=[VM] * 3,
        scratch_shapes=[cams, dense, dense],
    )(own, near, far, cross, current, moment_one, moment_two, below, above, migration)
    return current, moment_one, moment_two, jnp.swapaxes(pictures, 2, 3)


def solution(mesh):
    return jax.shard_map(
        local,
        mesh=mesh,
        in_specs=(
            P(None, "row"),
            P(None, "row"),
            P(None, "row"),
            P(None, "rep", None),
            P(None, "rep", "row", None),
            P(None, "rep", "row", None),
            P(None, "rep", "row", None),
            P(None, "rep", "row", None),
            P(None, "rep", "row", None, None),
            P("row", None, None),
        ),
        out_specs=(
            P(None, "row"),
            P(None, "row"),
            P(None, "row"),
            P(None, "rep", "row", None, None),
        ),
        check_vma=False,
    )
```

```python
import jax
import jax.numpy as jnp
from jax import lax
from jax.experimental import pallas as pl
from jax.experimental.pallas import tpu as pltpu
from jax.sharding import PartitionSpec as P


P_SIZE = 59
BLOCK = 128
LISTB = 4
PIX = 256
ITERS = 2
MIGH = 2
DEPTH = 512
SIDE = 16
MIG_LANE = 64
CAM_ROWS = 16
LOG2E = 1.4426950408889634

harm_zero = 0.28209479177387814
harm_one = 0.4886025119029199
harm_two = (
    1.0925484305920792,
    -1.0925484305920792,
    0.31539156525252005,
    -1.0925484305920792,
    0.5462742152960396,
)
harm_three = (
    -0.5900435899266435,
    2.890611442640554,
    -0.4570457994644658,
    0.3731763325901154,
    -0.4570457994644658,
    1.445305721320277,
    -0.5900435899266435,
)
learn_rate = 0.01
adam_epsilon = 1e-08

f32 = jnp.float32
bf16 = jnp.bfloat16
VM = pl.BlockSpec(memory_space=pltpu.VMEM)
SM = pl.BlockSpec(memory_space=pltpu.SMEM)


def pitch(blocks):
    return blocks + 1 - blocks % 2


def up8(count):
    return -(-count // 8) * 8


def harmonics(x, y, z):
    xx, yy, zz = x * x, y * y, z * z
    return [
        harm_zero + 0.0 * x,
        -harm_one * y,
        harm_one * z,
        -harm_one * x,
        harm_two[0] * x * y,
        harm_two[1] * y * z,
        harm_two[2] * (2.0 * zz - xx - yy),
        harm_two[3] * x * z,
        harm_two[4] * (xx - yy),
        harm_three[0] * y * (3.0 * xx - yy),
        harm_three[1] * x * y * z,
        harm_three[2] * y * (4.0 * zz - xx - yy),
        harm_three[3] * z * (2.0 * zz - 3.0 * xx - 3.0 * yy),
        harm_three[4] * x * (4.0 * zz - xx - yy),
        harm_three[5] * z * (xx - yy),
        harm_three[6] * x * (xx - 3.0 * yy),
    ]


def split(value, pieces):
    out = []
    for piece in range(pieces):
        part = value.astype(bf16)
        out.append(part)
        if piece < pieces - 1:
            value = value - part.astype(f32)
    return out


def dot(left, right, dims=((1,), (0,))):
    return lax.dot_general(left, right, (dims, ((), ())), preferred_element_type=f32)


NT = ((1,), (1,))
TN = ((0,), (0,))


def rank_of(owners, index):
    rank = jnp.int32(0)
    for other in range(index):
        rank = rank + (owners[other] == owners[index]).astype(jnp.int32)
    return rank


def request_kernel(capacity, owner_ref, block_ref, migration_ref, out_ref, ranks_ref):
    owners = out_ref.shape[0]
    tiles = owner_ref.shape[2]
    lane = lax.broadcasted_iota(jnp.int32, (owners, BLOCK), 1)
    row = lax.broadcasted_iota(jnp.int32, (owners, BLOCK), 0)
    place = row * BLOCK + lane
    message = jnp.full((owners, BLOCK), -1, jnp.int32)
    for step in range(ITERS):
        names = [owner_ref[step, 0, t, j] for t in range(tiles) for j in range(LISTB)]
        for index in range(tiles * LISTB):
            rank = rank_of(names, index)
            ranks_ref[step, index] = rank
            target = names[index] * BLOCK + step * capacity + rank
            block = block_ref[step, 0, index // LISTB, index % LISTB]
            message = jnp.where(place == target, block, message)
    for side in range(2):
        for j in range(MIGH):
            message = jnp.where(
                lane == MIG_LANE + side * MIGH + j, migration_ref[0, side, j], message
            )
    for owner in range(owners):
        out_ref[owner] = message[owner : owner + 1]


def geometry(row):
    scales = [jnp.exp(row(3 + k)) for k in range(3)]
    quats = [row(6 + k) for k in range(4)]
    norm = lax.rsqrt(
        quats[0] * quats[0] + quats[1] * quats[1] + quats[2] * quats[2] + quats[3] * quats[3]
    )
    w, x, y, z = [part * norm for part in quats]
    rotation = [
        [1.0 - 2.0 * (y * y + z * z), 2.0 * (x * y - w * z), 2.0 * (x * z + w * y)],
        [2.0 * (x * y + w * z), 1.0 - 2.0 * (x * x + z * z), 2.0 * (y * z - w * x)],
        [2.0 * (x * z - w * y), 2.0 * (y * z + w * x), 1.0 - 2.0 * (x * x + y * y)],
    ]
    return scales, (w, x, y, z), norm, rotation


def conic_of(scales, rotation, affine):
    spread = [
        [
            (
                affine[3 * i] * rotation[0][k]
                + affine[3 * i + 1] * rotation[1][k]
                + affine[3 * i + 2] * rotation[2][k]
            )
            * scales[k]
            for k in range(3)
        ]
        for i in range(2)
    ]
    one, two = spread
    cov_xx = one[0] * one[0] + one[1] * one[1] + one[2] * one[2] + 0.3
    cov_yy = two[0] * two[0] + two[1] * two[1] + two[2] * two[2] + 0.3
    cov_xy = one[0] * two[0] + one[1] * two[1] + one[2] * two[2]
    inverse = 1.0 / (cov_xx * cov_yy - cov_xy * cov_xy)
    return cov_yy * inverse, -cov_xy * inverse, cov_xx * inverse


def fill_table(step, blocks, camera_ref, dense, table):
    wide = pitch(blocks)
    cam = [camera_ref[step, 0, k] for k in range(11)]
    basis = harmonics(cam[8], cam[9], cam[10])
    for group in range(blocks // 8):

        def row(p):
            return dense[p * wide + 8 * group : p * wide + 8 * group + 8, :]

        scales, _, _, rotation = geometry(row)
        conic = conic_of(scales, rotation, cam)
        means = [row(k) for k in range(3)]
        rows = [
            cam[0] * means[0] + cam[1] * means[1] + cam[2] * means[2] + cam[6],
            cam[3] * means[0] + cam[4] * means[1] + cam[5] * means[2] + cam[7],
            conic[0],
            conic[1],
            conic[2],
        ]
        for k in range(3):
            colour = basis[0] * row(11 + k)
            for j in range(1, 16):
                colour = colour + basis[j] * row(11 + 3 * j + k)
            rows.append(0.5 + colour)
        rows.append(-LOG2E * jnp.log(1.0 + jnp.exp(-row(10))))
        for k in range(9):
            table[pl.ds(72 * group + k, 8, stride=9), :] = rows[k]


def serve(step, capacity, asked_ref, table, out_ref):
    owners = out_ref.shape[0]
    for peer in range(owners):
        for slot in range(capacity):
            block = jnp.maximum(asked_ref[peer, 0, step * capacity + slot], 0)
            out_ref[peer, 8 * slot : 8 * slot + 8, :] = table[pl.ds(block * 9, 8), :]
            out_ref[peer, 8 * capacity + slot : 8 * capacity + slot + 1, :] = table[
                pl.ds(block * 9 + 8, 1), :
            ]


def row_groups():
    return [(first, min(8, P_SIZE - first)) for first in range(0, P_SIZE, 8)]


def project_kernel(params_ref, camera_ref, table, dense):
    blocks = params_ref.shape[1] // BLOCK
    wide = pitch(blocks)
    for block in range(blocks):
        for first, count in row_groups():
            dense[pl.ds(first * wide + block, count, stride=wide), :] = params_ref[
                first : first + count, block * BLOCK : (block + 1) * BLOCK
            ]
    fill_table(0, blocks, camera_ref, dense, table)


def serve_kernel(capacity, table, asked_ref, out_ref):
    serve(0, capacity, asked_ref, table, out_ref)


def pixel_features(rows, per):
    pixel = lax.broadcasted_iota(jnp.int32, (rows, PIX), 1)
    which = lax.broadcasted_iota(jnp.int32, (rows, PIX), 0) // per
    px = (pixel % SIDE).astype(f32) - (SIDE / 2 - 0.5)
    py = (pixel // SIDE).astype(f32) - (SIDE / 2 - 0.5)
    chosen = jnp.where(which == 0, 1.0, 0.0)
    for index, value in enumerate((px, py, px * px, px * py, py * py)):
        chosen = jnp.where(which == index + 1, value, chosen)
    return chosen.astype(bf16)


def lane_gather(pieces, within, source):
    got = jnp.take_along_axis(pieces[0], within, axis=1)
    for j in range(1, len(pieces)):
        got = jnp.where(source == j, jnp.take_along_axis(pieces[j], within, axis=1), got)
    return got


HEAT_PIECES = 2


def put(ref, rows, value):
    for k in range(ref.shape[0]):
        ref[k, rows, :] = value[:, k * BLOCK : (k + 1) * BLOCK]


def get(ref, first, count):
    return jnp.concatenate([ref[k, first : first + count, :] for k in range(ref.shape[0])], axis=1)


COL_ROWS = {0: (0, 9, 15), 1: (3, 12), 2: (6,)}


def render_kernel(step, capacity, slots, final, *refs):
    if final:
        (
            arrived, corner_ref, owner_ref, ranks_ref, block_ref, asked_ref, order_ref, target_ref, earlier_ref,
            picture_ref, out_ref, *scratch,
        ) = refs
        for other in range(ITERS - 1):
            picture_ref[other] = earlier_ref[other]
    else:
        arrived, corner_ref, owner_ref, ranks_ref, order_ref, target_ref, picture_ref, out_ref, *scratch = refs
    onehots, sorted_ref, coeffs, shades_ref, sums_ref, grads_ref, *per_tile = scratch
    owners = arrived.shape[0]
    tiles = owner_ref.shape[2]
    lists = DEPTH // BLOCK
    segments = 8
    steps = DEPTH // segments
    out_ref[...] = jnp.zeros_like(out_ref)
    coeffs[...] = jnp.zeros_like(coeffs)
    features = pixel_features(32, 3)
    flat = pixel_features(16, 1)

    names = [owner_ref[step, 0, t, j] for t in range(tiles) for j in range(LISTB)]
    ranks = [ranks_ref[step, index] for index in range(tiles * LISTB)]

    order = order_ref[step, 0]
    order = jnp.concatenate([order] * (8 // tiles), axis=0)
    order_pieces = [order[:, k * BLOCK : (k + 1) * BLOCK] for k in range(lists)]
    woven = []
    for k in range(lists):
        row = lax.broadcasted_iota(jnp.int32, order_pieces[0].shape, 1) + k * BLOCK
        nth = (row % segments) * steps + row // segments
        woven.append(lane_gather(order_pieces, nth & (BLOCK - 1), nth // BLOCK))
    all_within = [piece & (BLOCK - 1) for piece in woven]
    all_source = [piece // BLOCK for piece in woven]
    faint_pieces = []
    for j in range(LISTB):
        parts = [
            arrived[
                names[t * LISTB + j], pl.ds(8 * capacity + ranks[t * LISTB + j], 1), :
            ]
            for t in range(tiles)
        ]
        faint_pieces.append(jnp.concatenate(parts * (8 // tiles), axis=0))
    faint = [lane_gather(faint_pieces, all_within[k], all_source[k]) for k in range(lists)]
    faint = jnp.concatenate(faint, axis=1)[0:tiles]
    row_id = lax.broadcasted_iota(jnp.int32, (BLOCK, BLOCK), 0).astype(f32).astype(bf16)
    sub = lax.broadcasted_iota(jnp.int32, (segments, PIX), 0)

    for tile in range(tiles):
        one = slice(tile, tile + 1)
        pieces = [
            arrived[
                names[tile * LISTB + j],
                pl.ds(pl.multiple_of(ranks[tile * LISTB + j] * 8, 8), 8),
                :,
            ]
            for j in range(LISTB)
        ]
        for k in range(lists):
            within = jnp.broadcast_to(all_within[k][one], (8, BLOCK))
            source = jnp.broadcast_to(all_source[k][one], (8, BLOCK))
            sorted_ref[k, pl.ds(tile, 8, stride=9), :] = lane_gather(
                pieces, within, source
            )

    def param(k):
        return get(sorted_ref, 9 * k, tiles)

    which = lax.broadcasted_iota(jnp.int32, (tiles, DEPTH), 0)
    corner_x = jnp.zeros((tiles, DEPTH), f32)
    corner_y = jnp.zeros((tiles, DEPTH), f32)
    for tile in range(tiles):
        corner_x = jnp.where(which == tile, corner_ref[step, 0, 0, tile], corner_x)
        corner_y = jnp.where(which == tile, corner_ref[step, 0, 1, tile], corner_y)
    all_u = u = param(0) - (corner_x + SIDE / 2)
    all_v = v = param(1) - (corner_y + SIDE / 2)
    half_a, half_b, half_c = (
        (-0.5 * LOG2E) * param(2), -LOG2E * param(3), (-0.5 * LOG2E) * param(4)
    )
    values = (
        half_a * u * u + half_b * u * v + half_c * v * v + faint,
        -(2.0 * half_a * u + half_b * v),
        -(2.0 * half_c * v + half_b * u),
        half_a,
        half_b,
        half_c,
    )
    for index, value in enumerate(values):
        for piece, part in enumerate(split(value, 3)):
            put(coeffs, pl.ds(3 * index + piece, tiles, stride=33), part.astype(f32))
    for k in range(3):
        for piece, part in enumerate(split(param(5 + k), 3)):
            for at in COL_ROWS[piece]:
                put(shades_ref, pl.ds(at + k, tiles, stride=19), part.astype(f32))

    def opening(tile, ratios, locals_, weight_h, weight_m, mixed, heats):
        form = get(coeffs, 33 * tile, 32).astype(bf16)
        passed = jnp.ones((segments, PIX), f32)
        for k in range(lists):
            power = dot(form[:, k * BLOCK : (k + 1) * BLOCK], features, TN)
            for at in range(0, BLOCK, segments):
                here = slice(k * BLOCK + at, k * BLOCK + at + segments)
                alpha = jnp.exp2(power[at : at + segments])
                keep = 1.0 - alpha
                ratios[here, :] = alpha / keep
                locals_[here, :] = alpha * passed
                passed = passed * keep
        for shift in (1, 2, 4):
            passed = passed * jnp.where(sub >= shift, pltpu.roll(passed, shift, 0), 1.0)
        return jnp.where(sub >= 1, pltpu.roll(passed, 1, 0), 1.0)

    def picture(tile, passed, ratios, locals_, weight_h, weight_m, mixed, heats):
        one = slice(tile, tile + 1)
        twice = jnp.concatenate([passed, passed], axis=0)
        for at in range(0, DEPTH, 2 * segments):
            here = slice(at, at + 2 * segments)
            weight_h[here, :], weight_m[here, :] = split(locals_[here, :] * twice, 2)
        col_left = get(shades_ref, 19 * tile, 9).astype(bf16)
        shades = dot(col_left, weight_h[...]) + dot(col_left, weight_m[...])
        shades = shades[0:3] + shades[3:6] + shades[6:9]
        for k in range(3):
            picture_ref[step, 0, k, one, :] = shades[k : k + 1]
        error = shades - jnp.concatenate(
            [target_ref[step, 0, k, one, :] for k in range(3)], axis=0
        )
        err_h, err_m, err_l = [part.astype(f32) for part in split(error, 3)]
        return jnp.concatenate([err_h, err_h, err_h, err_m, err_m, err_l], axis=0).astype(bf16)

    def closing(tile, passed, errors, ratios, locals_, weight_h, weight_m, mixed, heats):
        err_left = jnp.concatenate(
            [errors.astype(f32)[0:3], errors.astype(f32)[9:12], errors.astype(f32)[15:18]], axis=0
        ).astype(bf16)
        col_grads = dot(err_left, weight_h[...], NT) + dot(err_left, weight_m[...], NT)
        put(sums_ref, pl.ds(72 + tile, 8, stride=9), col_grads[0:8])
        put(sums_ref, slice(144 + tile, 145 + tile), col_grads[8:9])
        col_right = get(shades_ref, 19 * tile, 18).astype(bf16)
        total = jnp.zeros((segments, PIX), f32)
        for k in reversed(range(lists)):
            seen = dot(col_right[:, k * BLOCK : (k + 1) * BLOCK], errors, TN)
            for at in reversed(range(0, BLOCK, segments)):
                here = slice(k * BLOCK + at, k * BLOCK + at + segments)
                flow = locals_[here, :] * passed * seen[at : at + segments]
                mixed[here, :] = flow - ratios[here, :] * total
                total = total + flow
        for shift in (1, 2, 4):
            total = total + jnp.where(
                sub < segments - shift, pltpu.roll(total, segments - shift, 0), 0.0
            )
        total = jnp.where(sub < segments - 1, pltpu.roll(total, segments - 1, 0), 0.0)
        twice = jnp.concatenate([total, total], axis=0)
        for at in range(0, DEPTH, 2 * segments):
            here = slice(at, at + 2 * segments)
            parts = split(mixed[here, :] - ratios[here, :] * twice, HEAT_PIECES)
            for ref, part in zip(heats, parts):
                ref[here, :] = part
        moments = dot(flat, heats[0][...], NT)
        for ref in heats[1:]:
            moments = moments + dot(flat, ref[...], NT)
        put(sums_ref, pl.ds(tile, 8, stride=9), moments[0:8])

    def unsort_matrix(tile):
        one = slice(tile, tile + 1)
        for k in range(lists):
            local = woven[k][one].astype(f32)
            for piece in range(lists):
                inside = jnp.where(all_source[k][one] == piece, local - piece * BLOCK, -1.0)
                onehots[
                    tile, piece * BLOCK : (piece + 1) * BLOCK, k * BLOCK : (k + 1) * BLOCK
                ] = jnp.where(row_id == inside.astype(bf16), jnp.ones((), bf16), jnp.zeros((), bf16))

    def buffers(tile):
        each = len(per_tile) // tiles
        mine = per_tile[each * tile : each * tile + each]
        return (*mine[0:5], mine[5:])

    def finish(first, count):
        def summed(row):
            return get(sums_ref, 9 * row + first, count)

        group = slice(first, first + count)
        a, b, c = [get(sorted_ref, 9 * k + first, count) for k in (2, 3, 4)]
        u, v = all_u[group], all_v[group]
        m00, m10, m01, m20, m11, m02 = [summed(k) for k in range(6)]
        x1, y1 = m10 - u * m00, m01 - v * m00
        grads = [
            a * x1 + b * y1,
            b * x1 + c * y1,
            -0.5 * (m20 - 2.0 * u * m10 + u * u * m00),
            -(m11 - u * m01 - v * m10 + u * v * m00),
            -0.5 * (m02 - 2.0 * v * m01 + v * v * m00),
            *[summed(8 + k) + summed(11 + k) + summed(14 + k) for k in range(3)],
            m00,
        ]
        for k, value in enumerate(grads):
            for piece, part in enumerate(split(value, 3)):
                put(grads_ref, pl.ds(49 * first + 16 * piece + k, count, stride=49), part.astype(f32))
        for tile in range(first, first + count):
            unsort(tile)

    def unsort(tile):
        listed = dot(get(grads_ref, 49 * tile, 48).astype(bf16), onehots[tile], NT)
        listed = listed[0:16] + listed[16:32] + listed[32:48]
        for j in range(LISTB):
            name, rank = names[tile * LISTB + j], ranks[tile * LISTB + j]
            if final:
                block = block_ref[step, 0, tile, j]
                hop = jnp.int32(0)
                for k in range(MIGH):
                    goes_left = asked_ref[name, 0, MIG_LANE + k] == block
                    goes_right = asked_ref[name, 0, MIG_LANE + MIGH + k] == block
                    rank = jnp.where(goes_left, capacity + MIGH + k, rank)
                    rank = jnp.where(goes_right, capacity + k, rank)
                    hop = hop - goes_left.astype(jnp.int32) + goes_right.astype(jnp.int32)
                name = name + hop
                name = jnp.where(name < 0, owners - 1, jnp.where(name >= owners, 0, name))
            lanes = slice(j * BLOCK, (j + 1) * BLOCK)
            main = pl.ds(pl.multiple_of(rank * 8, 8), 8)
            extra = pl.ds(8 * slots + rank, 1)
            if final:
                out_ref[name, main, :] = out_ref[name, main, :] + listed[0:8, lanes]
                out_ref[name, extra, :] = out_ref[name, extra, :] + listed[8:9, lanes]
            else:
                out_ref[name, main, :] = listed[0:8, lanes]
                out_ref[name, extra, :] = listed[8:9, lanes]


    passes, errors = {}, {}
    for tile in range(tiles):
        passes[tile] = opening(tile, *buffers(tile))
    for tile in range(tiles):
        errors[tile] = picture(tile, passes[tile], *buffers(tile))
    for tile in range(tiles):
        unsort_matrix(tile)
    for tile in range(tiles):
        closing(tile, passes[tile], errors[tile], *buffers(tile))
        if tile % 2 == 1 or tile == tiles - 1:
            finish(tile - tile % 2, 1 + tile % 2)


def gather_kernel(step, capacity, slots, returned, asked_ref, migration_ref, camera_ref, out_ref):
    owners = returned.shape[0]
    blocks = (out_ref.shape[0] - CAM_ROWS) // 9
    out_ref[...] = jnp.zeros_like(out_ref)

    def body(peer, carry):
        for slot in range(slots):
            if slot < capacity:
                block = jnp.maximum(asked_ref[peer, 0, step * capacity + slot], 0)
            else:
                block = migration_ref[0, (slot - capacity) // MIGH, (slot - capacity) % MIGH]
            main = pl.ds(block * 9, 8)
            extra = pl.ds(block * 9 + 8, 1)
            out_ref[main, :] = out_ref[main, :] + returned[peer, 8 * slot : 8 * slot + 8, :]
            out_ref[extra, :] = (
                out_ref[extra, :] + returned[peer, 8 * slots + slot : 8 * slots + slot + 1, :]
            )
        return carry

    lax.fori_loop(0, owners, body, 0)
    for index, k in enumerate((0, 1, 2, 3, 4, 5, 8, 9, 10)):
        at = 9 * blocks + index
        out_ref[at : at + 1, :] = jnp.full((1, BLOCK), camera_ref[step, 0, k], f32)


def collect(own_ref, others, scratch):
    mine = lax.axis_index("rep")
    scratch[mine] = own_ref[...]
    for offset, ref in others:
        scratch[mine ^ offset] = ref[...]


def pullback(blocks, cams, dense, grads):
    count = cams.shape[0]
    wide = pitch(blocks)
    affine, basis = [], []
    for c in range(count):
        rows = [
            jnp.broadcast_to(cams[c, 9 * blocks + k : 9 * blocks + k + 1, :], (8, BLOCK))
            for k in range(9)
        ]
        affine.append(rows[0:6])
        basis.append(harmonics(rows[6], rows[7], rows[8]))
    for group in range(blocks // 8):

        def row(p):
            return dense[p * wide + 8 * group : p * wide + 8 * group + 8, :]

        def put(p, value):
            grads[p * wide + 8 * group : p * wide + 8 * group + 8, :] = value

        given = [
            [cams[c, pl.ds(72 * group + k, 8, stride=9), :] for k in range(9)] for c in range(count)
        ]
        scales, (w, x, y, z), norm, rotation = geometry(row)
        means = [0.0, 0.0, 0.0]
        sigma = [0.0] * 6
        for c in range(count):
            m = affine[c]
            a, b, d = conic_of(scales, rotation, m)
            g_x, g_y, g_a, g_b, g_d = given[c][0:5]
            for k in range(3):
                means[k] = means[k] + m[k] * g_x + m[3 + k] * g_y
            g_b = 0.5 * g_b
            t00, t01 = a * g_a + b * g_b, a * g_b + b * g_d
            t10, t11 = b * g_a + d * g_b, b * g_b + d * g_d
            h00 = -(t00 * a + t01 * b)
            h01 = -(t00 * b + t01 * d)
            h11 = -(t10 * b + t11 * d)
            top = [h00 * m[k] + h01 * m[3 + k] for k in range(3)]
            low = [h01 * m[k] + h11 * m[3 + k] for k in range(3)]
            for index, (i, k) in enumerate(((0, 0), (0, 1), (0, 2), (1, 1), (1, 2), (2, 2))):
                sigma[index] = sigma[index] + m[i] * top[k] + m[3 + i] * low[k]
        for k in range(3):
            put(k, means[k])
        full = [
            [sigma[0], sigma[1], sigma[2]],
            [sigma[1], sigma[3], sigma[4]],
            [sigma[2], sigma[4], sigma[5]],
        ]
        turn = [[None] * 3 for _ in range(3)]
        for k in range(3):
            column = [rotation[j][k] * scales[k] for j in range(3)]
            pulled = [
                2.0 * (full[j][0] * column[0] + full[j][1] * column[1] + full[j][2] * column[2])
                for j in range(3)
            ]
            put(
                3 + k, pulled[0] * column[0] + pulled[1] * column[1] + pulled[2] * column[2]
            )
            for j in range(3):
                turn[j][k] = pulled[j] * scales[k]
        g_w = 2.0 * (
            z * (turn[1][0] - turn[0][1])
            + y * (turn[0][2] - turn[2][0])
            + x * (turn[2][1] - turn[1][2])
        )
        g_x = 2.0 * (
            y * (turn[0][1] + turn[1][0])
            + z * (turn[0][2] + turn[2][0])
            - 2.0 * x * (turn[1][1] + turn[2][2])
            + w * (turn[2][1] - turn[1][2])
        )
        g_y = 2.0 * (
            x * (turn[0][1] + turn[1][0])
            + z * (turn[1][2] + turn[2][1])
            - 2.0 * y * (turn[0][0] + turn[2][2])
            + w * (turn[0][2] - turn[2][0])
        )
        g_z = 2.0 * (
            x * (turn[0][2] + turn[2][0])
            + y * (turn[1][2] + turn[2][1])
            - 2.0 * z * (turn[0][0] + turn[1][1])
            + w * (turn[1][0] - turn[0][1])
        )
        along = w * g_w + x * g_x + y * g_y + z * g_z
        for k, (part, pull) in enumerate(((w, g_w), (x, g_x), (y, g_y), (z, g_z))):
            put(6 + k, norm * (pull - part * along))
        faint = given[0][8]
        for c in range(1, count):
            faint = faint + given[c][8]
        put(10, faint / (1.0 + jnp.exp(row(10))))
        for j in range(16):
            for k in range(3):
                value = basis[0][j] * given[0][5 + k]
                for c in range(1, count):
                    value = value + basis[c][j] * given[c][5 + k]
                put(11 + 3 * j + k, value)


def adam(value, first, second, gradient):
    first = 0.9 * first + 0.1 * gradient
    second = 0.999 * second + 0.001 * gradient * gradient
    root = second * lax.rsqrt(second)
    return value - learn_rate * first / (root + adam_epsilon), first, second


def update_kernel(capacity, *refs):
    (
        own_ref, near_ref, far_ref, cross_ref, params_ref, first_ref, second_ref, camera_ref,
        asked_ref, migration_ref, new_params, new_first, new_second, out_ref, left_ref, right_ref,
        cams, dense, grads, table,
    ) = refs
    blocks = params_ref.shape[1] // BLOCK
    wide = pitch(blocks)
    collect(own_ref, ((1, near_ref), (2, far_ref), (3, cross_ref)), cams)
    for block in range(blocks):
        for top, count in row_groups()[:2]:
            dense[pl.ds(top * wide + block, count, stride=wide), :] = params_ref[
                top : top + count, block * BLOCK : (block + 1) * BLOCK
            ]
    pullback(blocks, cams, dense, grads)
    for block in range(blocks):
        lanes = slice(block * BLOCK, (block + 1) * BLOCK)
        for top, count in row_groups():
            part = slice(top, top + count)
            where = pl.ds(top * wide + block, count, stride=wide)
            value, first, second = adam(
                params_ref[part, lanes], first_ref[part, lanes], second_ref[part, lanes],
                grads[where, :],
            )
            new_params[part, lanes] = value
            new_first[part, lanes] = first
            new_second[part, lanes] = second
            dense[where, :] = value
    fill_table(1, blocks, camera_ref, dense, table)
    serve(1, capacity, asked_ref, table, out_ref)
    for side, ref in ((0, left_ref), (1, right_ref)):
        for j in range(MIGH):
            lanes = pl.ds(pl.multiple_of(migration_ref[0, side, j] * BLOCK, BLOCK), BLOCK)
            for index, source in enumerate((new_params, new_first, new_second)):
                ref[index, :, j * BLOCK : (j + 1) * BLOCK] = source[:, lanes]


def final_kernel(*refs):
    (
        own_ref, near_ref, far_ref, cross_ref, params_ref, first_ref, second_ref, below_ref,
        above_ref, migration_ref, new_params, new_first, new_second, cams, dense, grads,
    ) = refs
    blocks = params_ref.shape[1] // BLOCK
    wide = pitch(blocks)
    collect(own_ref, ((1, near_ref), (2, far_ref), (3, cross_ref)), cams)
    for block in range(blocks):
        for top, count in row_groups()[:2]:
            dense[pl.ds(top * wide + block, count, stride=wide), :] = params_ref[
                top : top + count, block * BLOCK : (block + 1) * BLOCK
            ]
    moved = [
        (migration_ref[0, side, j], ref, j)
        for side, ref in ((0, below_ref), (1, above_ref))
        for j in range(MIGH)
    ]
    for block, ref, j in moved:
        for top, count in row_groups()[:2]:
            dense[pl.ds(top * wide + block, count, stride=wide), :] = ref[
                0, top : top + count, j * BLOCK : (j + 1) * BLOCK
            ]
    pullback(blocks, cams, dense, grads)
    for block in range(blocks):
        lanes = slice(block * BLOCK, (block + 1) * BLOCK)
        for top, count in row_groups():
            part = slice(top, top + count)
            value, first, second = adam(
                params_ref[part, lanes], first_ref[part, lanes], second_ref[part, lanes],
                grads[pl.ds(top * wide + block, count, stride=wide), :],
            )
            new_params[part, lanes] = value
            new_first[part, lanes] = first
            new_second[part, lanes] = second
    for block, ref, j in moved:
        lanes = pl.ds(pl.multiple_of(block * BLOCK, BLOCK), BLOCK)
        source = slice(j * BLOCK, (j + 1) * BLOCK)
        for top, count in row_groups():
            part = slice(top, top + count)
            value, first, second = adam(
                ref[0, part, source], ref[1, part, source], ref[2, part, source],
                grads[pl.ds(top * wide + block, count, stride=wide), :],
            )
            new_params[part, lanes] = value
            new_first[part, lanes] = first
            new_second[part, lanes] = second


def shape(dims, dtype=f32):
    return jax.ShapeDtypeStruct(dims, dtype)


def bind(kernel, *static):
    def run(*refs):
        kernel(*static, *refs)

    return run


def grant(mebibytes):
    return pltpu.CompilerParams(vmem_limit_bytes=mebibytes << 20)


def near_core(*values):
    return [pltpu.with_memory_space_constraint(value, pltpu.VMEM) for value in values]


def swap(value, axis, offset):
    count = lax.axis_size(axis)
    return lax.ppermute(value, axis, [(i, i ^ offset) for i in range(count)])


def turn(value, axis, offset):
    count = lax.axis_size(axis)
    return lax.ppermute(value, axis, [(i, (i + offset) % count) for i in range(count)])


def exchange(value):
    far = swap(value, "rep", 2)
    near = swap(value, "rep", 1)
    cross = swap(far, "rep", 1)
    return near, far, cross


def row_exchange(value):
    return lax.all_to_all(value, "row", split_axis=0, concat_axis=0, tiled=True)


def local(
    params,
    first_moment,
    second_moment,
    camera,
    tile_corner,
    tile_owner,
    tile_block,
    depth_order,
    targets,
    migration,
):
    owners = lax.axis_size("row")
    replicas = lax.axis_size("rep")
    blocks = params.shape[1] // BLOCK
    tiles = tile_owner.shape[2]
    requests = tiles * LISTB
    capacity = max(2, 2 * ((requests + owners - 1) // owners))
    slots = capacity + 2 * MIGH
    dense = pltpu.VMEM((64 * pitch(blocks), BLOCK), f32)
    table = pltpu.VMEM((9 * blocks, BLOCK), f32)
    payload = 9 * blocks + CAM_ROWS
    cams = pltpu.VMEM((replicas, payload, BLOCK), f32)
    state = [shape(params.shape)] * 3
    kept = [pltpu.VMEM(params.shape, f32)] * 3

    lists, ranks = pl.pallas_call(
        bind(request_kernel, capacity),
        out_shape=[
            shape((owners, 1, BLOCK), jnp.int32), shape((ITERS, requests), jnp.int32)
        ],
        in_specs=[SM, SM, SM],
        out_specs=[VM, SM],
        compiler_params=grant(8),
    )(tile_owner, tile_block, migration)
    asked = row_exchange(lists)
    projected = pl.pallas_call(
        project_kernel,
        out_shape=shape((9 * blocks, BLOCK)),
        in_specs=[VM, SM],
        out_specs=VM,
        scratch_shapes=[dense],
        compiler_params=grant(8),
    )(params, camera)
    message = shape((owners, up8(9 * capacity), BLOCK))
    outgoing = pl.pallas_call(
        bind(serve_kernel, capacity), out_shape=message, in_specs=[VM, SM], out_specs=VM,
        compiler_params=grant(8),
    )(projected, asked)

    deep = pltpu.VMEM((DEPTH, PIX), f32)
    packed = pltpu.VMEM((DEPTH, PIX), bf16)
    render_scratch = [
        pltpu.VMEM((tiles, DEPTH, DEPTH), bf16),
        pltpu.VMEM((DEPTH // BLOCK, 80, BLOCK), f32),
        pltpu.VMEM((DEPTH // BLOCK, 33 * tiles, BLOCK), f32),
        pltpu.VMEM((DEPTH // BLOCK, 19 * tiles, BLOCK), f32),
        pltpu.VMEM((DEPTH // BLOCK, 160, BLOCK), f32),
        pltpu.VMEM((DEPTH // BLOCK, 49 * tiles, BLOCK), f32),
    ] + [deep, deep, packed, packed, deep, *[packed] * HEAT_PIECES] * tiles
    corners = jnp.swapaxes(tile_corner, 2, 3)
    photos = jnp.swapaxes(targets, 2, 3)
    pictures_shape = shape(photos.shape)

    def gather(step, count, returned):
        return pl.pallas_call(
            bind(gather_kernel, step, capacity, count),
            out_shape=pltpu.VMEM((payload, BLOCK), f32),
            compiler_params=grant(8),
            in_specs=[VM, SM, SM, SM],
            out_specs=VM,
        )(*near_core(returned), asked, migration, camera)

    def second(arrived, pictures):
        return pl.pallas_call(
            bind(render_kernel, 1, capacity, slots, True),
            out_shape=[pictures_shape, shape((owners, up8(9 * slots), BLOCK))],
            in_specs=[VM, SM, SM, SM, SM, SM, VM, VM, VM],
            out_specs=[VM, VM],
            scratch_shapes=render_scratch,
            compiler_params=grant(24),
        )(
            *near_core(arrived), corners, tile_owner, ranks, tile_block, asked, depth_order, photos,
            pictures,
        )

    arrived = row_exchange(outgoing)
    pictures, back = pl.pallas_call(
        bind(render_kernel, 0, capacity, capacity, False),
        out_shape=[pictures_shape, shape((owners, up8(9 * capacity), BLOCK))],
        in_specs=[VM, SM, SM, SM, VM, VM],
        out_specs=[VM, VM],
        scratch_shapes=render_scratch,
        compiler_params=grant(24),
    )(*near_core(arrived), corners, tile_owner, ranks, depth_order, photos)
    own = gather(0, capacity, row_exchange(back))
    near, far, cross = exchange(own)
    leaving = pltpu.VMEM((3, P_SIZE, MIGH * BLOCK), f32)
    current, moment_one, moment_two, outgoing, left, right = pl.pallas_call(
        bind(update_kernel, capacity),
        out_shape=kept + [shape((owners, up8(9 * capacity), BLOCK)), leaving, leaving],
        in_specs=[VM] * 7 + [SM] * 3,
        out_specs=[VM] * 6,
        scratch_shapes=[cams, dense, dense, table],
        compiler_params=grant(16),
    )(
        *near_core(own, near, far, cross, params, first_moment, second_moment),
        camera, asked, migration,
    )
    arrived = row_exchange(outgoing)
    below = turn(right, "row", 1)
    above = turn(left, "row", -1)
    pictures, back = second(arrived, pictures)
    own = gather(1, slots, row_exchange(back))
    near, far, cross = exchange(own)
    current, moment_one, moment_two = pl.pallas_call(
        final_kernel,
        out_shape=state,
        in_specs=[VM] * 9 + [SM],
        out_specs=[VM] * 3,
        scratch_shapes=[cams, dense, dense],
        compiler_params=grant(16),
    )(
        *near_core(own, near, far, cross, current, moment_one, moment_two, below, above), migration
    )
    return current, moment_one, moment_two, jnp.swapaxes(pictures, 2, 3)


def solution(mesh):
    return jax.shard_map(
        local,
        mesh=mesh,
        in_specs=(
            P(None, "row"),
            P(None, "row"),
            P(None, "row"),
            P(None, "rep", None),
            P(None, "rep", "row", None),
            P(None, "rep", "row", None),
            P(None, "rep", "row", None),
            P(None, "rep", "row", None),
            P(None, "rep", "row", None, None),
            P("row", None, None),
        ),
        out_specs=(
            P(None, "row"),
            P(None, "row"),
            P(None, "row"),
            P(None, "rep", "row", None, None),
        ),
        check_vma=False,
    )
```

```python
import jax
import jax.numpy as jnp
from jax import lax
from jax.experimental import pallas as pl
from jax.experimental.pallas import tpu as pltpu
from jax.sharding import PartitionSpec as P


P_SIZE = 59
BLOCK = 128
LISTB = 4
PIX = 256
ITERS = 2
MIGH = 2
DEPTH = 512
SIDE = 16
MIG_LANE = 64
PLAN_LANE = 72
CAM_ROWS = 16
LOG2E = 1.4426950408889634

harm_zero = 0.28209479177387814
harm_one = 0.4886025119029199
harm_two = (
    1.0925484305920792,
    -1.0925484305920792,
    0.31539156525252005,
    -1.0925484305920792,
    0.5462742152960396,
)
harm_three = (
    -0.5900435899266435,
    2.890611442640554,
    -0.4570457994644658,
    0.3731763325901154,
    -0.4570457994644658,
    1.445305721320277,
    -0.5900435899266435,
)
learn_rate = 0.01
adam_epsilon = 1e-08

f32 = jnp.float32
bf16 = jnp.bfloat16
VM = pl.BlockSpec(memory_space=pltpu.VMEM)
SM = pl.BlockSpec(memory_space=pltpu.SMEM)
ANY = pl.BlockSpec(memory_space=pl.ANY)


def pitch(blocks):
    return blocks + 1 - blocks % 2


def up8(count):
    return -(-count // 8) * 8


def harmonics(x, y, z):
    xx, yy, zz = x * x, y * y, z * z
    return [
        harm_zero + 0.0 * x,
        -harm_one * y,
        harm_one * z,
        -harm_one * x,
        harm_two[0] * x * y,
        harm_two[1] * y * z,
        harm_two[2] * (2.0 * zz - xx - yy),
        harm_two[3] * x * z,
        harm_two[4] * (xx - yy),
        harm_three[0] * y * (3.0 * xx - yy),
        harm_three[1] * x * y * z,
        harm_three[2] * y * (4.0 * zz - xx - yy),
        harm_three[3] * z * (2.0 * zz - 3.0 * xx - 3.0 * yy),
        harm_three[4] * x * (4.0 * zz - xx - yy),
        harm_three[5] * z * (xx - yy),
        harm_three[6] * x * (xx - 3.0 * yy),
    ]


def split(value, pieces):
    out = []
    for piece in range(pieces):
        part = value.astype(bf16)
        out.append(part)
        if piece < pieces - 1:
            value = value - part.astype(f32)
    return out


def dot(left, right, dims=((1,), (0,))):
    return lax.dot_general(left, right, (dims, ((), ())), preferred_element_type=f32)


NT = ((1,), (1,))
TN = ((0,), (0,))


def rank_of(owners, index):
    rank = jnp.int32(0)
    for other in range(index):
        rank = rank + (owners[other] == owners[index]).astype(jnp.int32)
    return rank


def request_kernel(capacity, blocks, owner_ref, block_ref, migration_ref, out_ref):
    owners = out_ref.shape[0]
    tiles = owner_ref.shape[2]
    lane = lax.broadcasted_iota(jnp.int32, (owners, BLOCK), 1)
    row = lax.broadcasted_iota(jnp.int32, (owners, BLOCK), 0)
    place = row * BLOCK + lane
    message = jnp.full((owners, BLOCK), -1, jnp.int32)
    for step in range(ITERS):
        names = [owner_ref[step, 0, t, j] for t in range(tiles) for j in range(LISTB)]
        for index in range(tiles * LISTB):
            rank = rank_of(names, index)
            target = names[index] * BLOCK + step * capacity + rank
            block = block_ref[step, 0, index // LISTB, index % LISTB]
            message = jnp.where(place == target, block, message)
            plan = (names[index] * capacity + rank) * blocks + block
            message = jnp.where(
                lane == PLAN_LANE + step * tiles * LISTB + index, plan, message
            )
    for side in range(2):
        for j in range(MIGH):
            message = jnp.where(
                lane == MIG_LANE + side * MIGH + j, migration_ref[0, side, j], message
            )
    for owner in range(owners):
        out_ref[owner] = message[owner : owner + 1]


def geometry(row):
    scales = [jnp.exp(row(3 + k)) for k in range(3)]
    quats = [row(6 + k) for k in range(4)]
    norm = lax.rsqrt(
        quats[0] * quats[0] + quats[1] * quats[1] + quats[2] * quats[2] + quats[3] * quats[3]
    )
    w, x, y, z = [part * norm for part in quats]
    rotation = [
        [1.0 - 2.0 * (y * y + z * z), 2.0 * (x * y - w * z), 2.0 * (x * z + w * y)],
        [2.0 * (x * y + w * z), 1.0 - 2.0 * (x * x + z * z), 2.0 * (y * z - w * x)],
        [2.0 * (x * z - w * y), 2.0 * (y * z + w * x), 1.0 - 2.0 * (x * x + y * y)],
    ]
    return scales, (w, x, y, z), norm, rotation


def conic_of(scales, rotation, affine):
    spread = [
        [
            (
                affine[3 * i] * rotation[0][k]
                + affine[3 * i + 1] * rotation[1][k]
                + affine[3 * i + 2] * rotation[2][k]
            )
            * scales[k]
            for k in range(3)
        ]
        for i in range(2)
    ]
    one, two = spread
    cov_xx = one[0] * one[0] + one[1] * one[1] + one[2] * one[2] + 0.3
    cov_yy = two[0] * two[0] + two[1] * two[1] + two[2] * two[2] + 0.3
    cov_xy = one[0] * two[0] + one[1] * two[1] + one[2] * two[2]
    inverse = 1.0 / (cov_xx * cov_yy - cov_xy * cov_xy)
    return cov_yy * inverse, -cov_xy * inverse, cov_xx * inverse


def fill_table(step, blocks, camera_ref, dense, table):
    wide = pitch(blocks)
    cam = [camera_ref[step, 0, k] for k in range(11)]
    basis = harmonics(cam[8], cam[9], cam[10])
    for group in range(blocks // 8):

        def row(p):
            return dense[p * wide + 8 * group : p * wide + 8 * group + 8, :]

        scales, _, _, rotation = geometry(row)
        conic = conic_of(scales, rotation, cam)
        means = [row(k) for k in range(3)]
        rows = [
            cam[0] * means[0] + cam[1] * means[1] + cam[2] * means[2] + cam[6],
            cam[3] * means[0] + cam[4] * means[1] + cam[5] * means[2] + cam[7],
            conic[0],
            conic[1],
            conic[2],
        ]
        for k in range(3):
            colour = basis[0] * row(11 + k)
            for j in range(1, 16):
                colour = colour + basis[j] * row(11 + 3 * j + k)
            rows.append(0.5 + colour)
        rows.append(-LOG2E * jnp.log(1.0 + jnp.exp(-row(10))))
        for k in range(9):
            table[pl.ds(72 * group + k, 8, stride=9), :] = rows[k]


def serve(step, capacity, asked_ref, table, out_ref):
    owners = out_ref.shape[0]
    for peer in range(owners):
        for slot in range(capacity):
            block = jnp.maximum(asked_ref[peer, 0, step * capacity + slot], 0)
            out_ref[peer, 8 * slot : 8 * slot + 8, :] = table[pl.ds(block * 9, 8), :]
            out_ref[peer, 8 * capacity + slot : 8 * capacity + slot + 1, :] = table[
                pl.ds(block * 9 + 8, 1), :
            ]


def row_groups():
    return [(first, min(8, P_SIZE - first)) for first in range(0, P_SIZE, 8)]


def project_kernel(params_ref, camera_ref, table, dense):
    blocks = params_ref.shape[1] // BLOCK
    wide = pitch(blocks)
    for block in range(blocks):
        for first, count in row_groups():
            dense[pl.ds(first * wide + block, count, stride=wide), :] = params_ref[
                first : first + count, block * BLOCK : (block + 1) * BLOCK
            ]
    fill_table(0, blocks, camera_ref, dense, table)


def serve_kernel(capacity, table, asked_ref, out_ref):
    serve(0, capacity, asked_ref, table, out_ref)


def pixel_features(rows, per):
    pixel = lax.broadcasted_iota(jnp.int32, (rows, PIX), 1)
    which = lax.broadcasted_iota(jnp.int32, (rows, PIX), 0) // per
    px = (pixel % SIDE).astype(f32) - (SIDE / 2 - 0.5)
    py = (pixel // SIDE).astype(f32) - (SIDE / 2 - 0.5)
    chosen = jnp.where(which == 0, 1.0, 0.0)
    for index, value in enumerate((px, py, px * px, px * py, py * py)):
        chosen = jnp.where(which == index + 1, value, chosen)
    return chosen.astype(bf16)


def lane_gather(pieces, within, source):
    got = jnp.take_along_axis(pieces[0], within, axis=1)
    for j in range(1, len(pieces)):
        got = jnp.where(source == j, jnp.take_along_axis(pieces[j], within, axis=1), got)
    return got


HEAT_PIECES = 2


def put(ref, rows, value):
    for k in range(ref.shape[0]):
        ref[k, rows, :] = value[:, k * BLOCK : (k + 1) * BLOCK]


def get(ref, first, count):
    return jnp.concatenate([ref[k, first : first + count, :] for k in range(ref.shape[0])], axis=1)


COL_ROWS = {0: (0, 9, 15), 1: (3, 12), 2: (6,)}


def render_kernel(step, capacity, slots, blocks, final, *refs):
    if final:
        (
            arrived, corner_ref, asked_ref, order_ref, target_ref, earlier_ref,
            rendered_ref, out_ref, picture_ref, leaving, *scratch,
        ) = refs
        store = pltpu.make_async_copy(picture_ref, rendered_ref.at[step, 0], leaving)
    else:
        (
            arrived, corner_ref, asked_ref, order_ref, target_ref,
            rendered_ref, out_ref, *scratch,
        ) = refs
        picture_ref = rendered_ref.at[step, 0]
    onehots, sorted_ref, coeffs, shades_ref, sums_ref, grads_ref, *per_tile = scratch
    owners = arrived.shape[0]
    tiles = order_ref.shape[2]
    lists = DEPTH // BLOCK
    segments = 8
    steps = DEPTH // segments
    out_ref[...] = jnp.zeros_like(out_ref)
    coeffs[...] = jnp.zeros_like(coeffs)
    features = pixel_features(32, 3)
    flat = pixel_features(16, 1)

    mine = lax.axis_index("row")
    plans = [
        asked_ref[mine, 0, PLAN_LANE + step * tiles * LISTB + index]
        for index in range(tiles * LISTB)
    ]
    numbers = [lax.rem(plan, blocks) for plan in plans]
    places = [lax.div(plan, blocks) for plan in plans]
    ranks = [lax.rem(place, capacity) for place in places]
    names = [lax.div(place, capacity) for place in places]

    order = order_ref[step, 0]
    order = jnp.concatenate([order] * (8 // tiles), axis=0)
    order_pieces = [order[:, k * BLOCK : (k + 1) * BLOCK] for k in range(lists)]
    woven = []
    for k in range(lists):
        row = lax.broadcasted_iota(jnp.int32, order_pieces[0].shape, 1) + k * BLOCK
        nth = (row % segments) * steps + row // segments
        woven.append(lane_gather(order_pieces, nth & (BLOCK - 1), nth // BLOCK))
    all_within = [piece & (BLOCK - 1) for piece in woven]
    all_source = [piece // BLOCK for piece in woven]
    faint_pieces = []
    for j in range(LISTB):
        parts = [
            arrived[
                names[t * LISTB + j], pl.ds(8 * capacity + ranks[t * LISTB + j], 1), :
            ]
            for t in range(tiles)
        ]
        faint_pieces.append(jnp.concatenate(parts * (8 // tiles), axis=0))
    faint = [lane_gather(faint_pieces, all_within[k], all_source[k]) for k in range(lists)]
    faint = jnp.concatenate(faint, axis=1)[0:tiles]
    row_id = lax.broadcasted_iota(jnp.int32, (BLOCK, BLOCK), 0).astype(f32).astype(bf16)
    sub = lax.broadcasted_iota(jnp.int32, (segments, PIX), 0)

    for tile in range(tiles):
        one = slice(tile, tile + 1)
        pieces = [
            arrived[
                names[tile * LISTB + j],
                pl.ds(pl.multiple_of(ranks[tile * LISTB + j] * 8, 8), 8),
                :,
            ]
            for j in range(LISTB)
        ]
        for k in range(lists):
            within = jnp.broadcast_to(all_within[k][one], (8, BLOCK))
            source = jnp.broadcast_to(all_source[k][one], (8, BLOCK))
            sorted_ref[k, pl.ds(tile, 8, stride=9), :] = lane_gather(
                pieces, within, source
            )

    def param(k):
        return get(sorted_ref, 9 * k, tiles)

    which = lax.broadcasted_iota(jnp.int32, (tiles, DEPTH), 0)
    corner_x = jnp.zeros((tiles, DEPTH), f32)
    corner_y = jnp.zeros((tiles, DEPTH), f32)
    for tile in range(tiles):
        corner_x = jnp.where(which == tile, corner_ref[step, 0, 0, tile], corner_x)
        corner_y = jnp.where(which == tile, corner_ref[step, 0, 1, tile], corner_y)
    all_u = u = param(0) - (corner_x + SIDE / 2)
    all_v = v = param(1) - (corner_y + SIDE / 2)
    half_a, half_b, half_c = (
        (-0.5 * LOG2E) * param(2), -LOG2E * param(3), (-0.5 * LOG2E) * param(4)
    )
    values = (
        half_a * u * u + half_b * u * v + half_c * v * v + faint,
        -(2.0 * half_a * u + half_b * v),
        -(2.0 * half_c * v + half_b * u),
        half_a,
        half_b,
        half_c,
    )
    for index, value in enumerate(values):
        for piece, part in enumerate(split(value, 3)):
            put(coeffs, pl.ds(3 * index + piece, tiles, stride=33), part.astype(f32))
    for k in range(3):
        for piece, part in enumerate(split(param(5 + k), 3)):
            for at in COL_ROWS[piece]:
                put(shades_ref, pl.ds(at + k, tiles, stride=19), part.astype(f32))

    def opening(tile, ratios, locals_, weight_h, weight_m, mixed, heats):
        form = get(coeffs, 33 * tile, 32).astype(bf16)
        passed = jnp.ones((segments, PIX), f32)
        for k in range(lists):
            power = dot(form[:, k * BLOCK : (k + 1) * BLOCK], features, TN)
            for at in range(0, BLOCK, segments):
                here = slice(k * BLOCK + at, k * BLOCK + at + segments)
                alpha = jnp.exp2(power[at : at + segments])
                keep = 1.0 - alpha
                ratios[here, :] = alpha / keep
                locals_[here, :] = alpha * passed
                passed = passed * keep
        for shift in (1, 2, 4):
            passed = passed * jnp.where(sub >= shift, pltpu.roll(passed, shift, 0), 1.0)
        return jnp.where(sub >= 1, pltpu.roll(passed, 1, 0), 1.0)

    def picture(tile, passed, ratios, locals_, weight_h, weight_m, mixed, heats):
        one = slice(tile, tile + 1)
        twice = jnp.concatenate([passed, passed], axis=0)
        for at in range(0, DEPTH, 2 * segments):
            here = slice(at, at + 2 * segments)
            weight_h[here, :], weight_m[here, :] = split(locals_[here, :] * twice, 2)
        col_left = get(shades_ref, 19 * tile, 9).astype(bf16)
        shades = dot(col_left, weight_h[...]) + dot(col_left, weight_m[...])
        shades = shades[0:3] + shades[3:6] + shades[6:9]
        for k in range(3):
            picture_ref[k, one, :] = shades[k : k + 1]
        error = shades - jnp.concatenate(
            [target_ref[step, 0, k, one, :] for k in range(3)], axis=0
        )
        err_h, err_m, err_l = [part.astype(f32) for part in split(error, 3)]
        return jnp.concatenate([err_h, err_h, err_h, err_m, err_m, err_l], axis=0).astype(bf16)

    def closing(tile, passed, errors, ratios, locals_, weight_h, weight_m, mixed, heats):
        err_left = jnp.concatenate(
            [errors.astype(f32)[0:3], errors.astype(f32)[9:12], errors.astype(f32)[15:18]], axis=0
        ).astype(bf16)
        col_grads = dot(err_left, weight_h[...], NT) + dot(err_left, weight_m[...], NT)
        put(sums_ref, pl.ds(72 + tile, 8, stride=9), col_grads[0:8])
        put(sums_ref, slice(144 + tile, 145 + tile), col_grads[8:9])
        col_right = get(shades_ref, 19 * tile, 18).astype(bf16)
        total = jnp.zeros((segments, PIX), f32)
        for k in reversed(range(lists)):
            seen = dot(col_right[:, k * BLOCK : (k + 1) * BLOCK], errors, TN)
            for at in reversed(range(0, BLOCK, segments)):
                here = slice(k * BLOCK + at, k * BLOCK + at + segments)
                flow = locals_[here, :] * passed * seen[at : at + segments]
                mixed[here, :] = flow - ratios[here, :] * total
                total = total + flow
        for shift in (1, 2, 4):
            total = total + jnp.where(
                sub < segments - shift, pltpu.roll(total, segments - shift, 0), 0.0
            )
        total = jnp.where(sub < segments - 1, pltpu.roll(total, segments - 1, 0), 0.0)
        twice = jnp.concatenate([total, total], axis=0)
        for at in range(0, DEPTH, 2 * segments):
            here = slice(at, at + 2 * segments)
            parts = split(mixed[here, :] - ratios[here, :] * twice, HEAT_PIECES)
            for ref, part in zip(heats, parts):
                ref[here, :] = part
        moments = dot(flat, heats[0][...], NT)
        for ref in heats[1:]:
            moments = moments + dot(flat, ref[...], NT)
        put(sums_ref, pl.ds(tile, 8, stride=9), moments[0:8])

    def unsort_matrix(tile):
        one = slice(tile, tile + 1)
        for k in range(lists):
            local = woven[k][one].astype(f32)
            for piece in range(lists):
                inside = jnp.where(all_source[k][one] == piece, local - piece * BLOCK, -1.0)
                onehots[
                    tile, piece * BLOCK : (piece + 1) * BLOCK, k * BLOCK : (k + 1) * BLOCK
                ] = jnp.where(row_id == inside.astype(bf16), jnp.ones((), bf16), jnp.zeros((), bf16))

    def buffers(tile):
        each = len(per_tile) // tiles
        mine = per_tile[each * tile : each * tile + each]
        return (*mine[0:5], mine[5:])

    def finish(first, count):
        def summed(row):
            return get(sums_ref, 9 * row + first, count)

        group = slice(first, first + count)
        a, b, c = [get(sorted_ref, 9 * k + first, count) for k in (2, 3, 4)]
        u, v = all_u[group], all_v[group]
        m00, m10, m01, m20, m11, m02 = [summed(k) for k in range(6)]
        x1, y1 = m10 - u * m00, m01 - v * m00
        grads = [
            a * x1 + b * y1,
            b * x1 + c * y1,
            -0.5 * (m20 - 2.0 * u * m10 + u * u * m00),
            -(m11 - u * m01 - v * m10 + u * v * m00),
            -0.5 * (m02 - 2.0 * v * m01 + v * v * m00),
            *[summed(8 + k) + summed(11 + k) + summed(14 + k) for k in range(3)],
            m00,
        ]
        for k, value in enumerate(grads):
            for piece, part in enumerate(split(value, 3)):
                put(grads_ref, pl.ds(49 * first + 16 * piece + k, count, stride=49), part.astype(f32))
        for tile in range(first, first + count):
            unsort(tile)

    def unsort(tile):
        listed = dot(get(grads_ref, 49 * tile, 48).astype(bf16), onehots[tile], NT)
        listed = listed[0:16] + listed[16:32] + listed[32:48]
        for j in range(LISTB):
            name, rank = names[tile * LISTB + j], ranks[tile * LISTB + j]
            if final:
                block = numbers[tile * LISTB + j]
                hop = jnp.int32(0)
                for k in range(MIGH):
                    goes_left = asked_ref[name, 0, MIG_LANE + k] == block
                    goes_right = asked_ref[name, 0, MIG_LANE + MIGH + k] == block
                    rank = jnp.where(goes_left, capacity + MIGH + k, rank)
                    rank = jnp.where(goes_right, capacity + k, rank)
                    hop = hop - goes_left.astype(jnp.int32) + goes_right.astype(jnp.int32)
                name = name + hop
                name = jnp.where(name < 0, owners - 1, jnp.where(name >= owners, 0, name))
            lanes = slice(j * BLOCK, (j + 1) * BLOCK)
            main = pl.ds(pl.multiple_of(rank * 8, 8), 8)
            extra = pl.ds(8 * slots + rank, 1)
            if final:
                out_ref[name, main, :] = out_ref[name, main, :] + listed[0:8, lanes]
                out_ref[name, extra, :] = out_ref[name, extra, :] + listed[8:9, lanes]
            else:
                out_ref[name, main, :] = listed[0:8, lanes]
                out_ref[name, extra, :] = listed[8:9, lanes]


    passes, errors = {}, {}
    for tile in range(tiles):
        passes[tile] = opening(tile, *buffers(tile))
    for tile in range(tiles):
        errors[tile] = picture(tile, passes[tile], *buffers(tile))
    if final:
        store.start()
    for tile in range(tiles):
        unsort_matrix(tile)
    for tile in range(tiles):
        closing(tile, passes[tile], errors[tile], *buffers(tile))
        if tile % 2 == 1 or tile == tiles - 1:
            finish(tile - tile % 2, 1 + tile % 2)
    if final:
        store.wait()


def gather_kernel(step, capacity, slots, returned, asked_ref, migration_ref, camera_ref, out_ref):
    owners = returned.shape[0]
    blocks = (out_ref.shape[0] - CAM_ROWS) // 9
    out_ref[...] = jnp.zeros_like(out_ref)

    def body(peer, carry):
        for slot in range(slots):
            if slot < capacity:
                block = jnp.maximum(asked_ref[peer, 0, step * capacity + slot], 0)
            else:
                block = migration_ref[0, (slot - capacity) // MIGH, (slot - capacity) % MIGH]
            main = pl.ds(block * 9, 8)
            extra = pl.ds(block * 9 + 8, 1)
            out_ref[main, :] = out_ref[main, :] + returned[peer, 8 * slot : 8 * slot + 8, :]
            out_ref[extra, :] = (
                out_ref[extra, :] + returned[peer, 8 * slots + slot : 8 * slots + slot + 1, :]
            )
        return carry

    lax.fori_loop(0, owners, body, 0)
    for index, k in enumerate((0, 1, 2, 3, 4, 5, 8, 9, 10)):
        at = 9 * blocks + index
        out_ref[at : at + 1, :] = jnp.full((1, BLOCK), camera_ref[step, 0, k], f32)


def collect(own_ref, others, scratch):
    mine = lax.axis_index("rep")
    scratch[mine] = own_ref[...]
    for offset, ref in others:
        scratch[mine ^ offset] = ref[...]


def pullback(blocks, cams, dense, grads):
    count = cams.shape[0]
    wide = pitch(blocks)
    affine, basis = [], []
    for c in range(count):
        rows = [
            jnp.broadcast_to(cams[c, 9 * blocks + k : 9 * blocks + k + 1, :], (8, BLOCK))
            for k in range(9)
        ]
        affine.append(rows[0:6])
        basis.append(harmonics(rows[6], rows[7], rows[8]))
    for group in range(blocks // 8):

        def row(p):
            return dense[p * wide + 8 * group : p * wide + 8 * group + 8, :]

        def put(p, value):
            grads[p * wide + 8 * group : p * wide + 8 * group + 8, :] = value

        given = [
            [cams[c, pl.ds(72 * group + k, 8, stride=9), :] for k in range(9)] for c in range(count)
        ]
        scales, (w, x, y, z), norm, rotation = geometry(row)
        means = [0.0, 0.0, 0.0]
        sigma = [0.0] * 6
        for c in range(count):
            m = affine[c]
            a, b, d = conic_of(scales, rotation, m)
            g_x, g_y, g_a, g_b, g_d = given[c][0:5]
            for k in range(3):
                means[k] = means[k] + m[k] * g_x + m[3 + k] * g_y
            g_b = 0.5 * g_b
            t00, t01 = a * g_a + b * g_b, a * g_b + b * g_d
            t10, t11 = b * g_a + d * g_b, b * g_b + d * g_d
            h00 = -(t00 * a + t01 * b)
            h01 = -(t00 * b + t01 * d)
            h11 = -(t10 * b + t11 * d)
            top = [h00 * m[k] + h01 * m[3 + k] for k in range(3)]
            low = [h01 * m[k] + h11 * m[3 + k] for k in range(3)]
            for index, (i, k) in enumerate(((0, 0), (0, 1), (0, 2), (1, 1), (1, 2), (2, 2))):
                sigma[index] = sigma[index] + m[i] * top[k] + m[3 + i] * low[k]
        for k in range(3):
            put(k, means[k])
        full = [
            [sigma[0], sigma[1], sigma[2]],
            [sigma[1], sigma[3], sigma[4]],
            [sigma[2], sigma[4], sigma[5]],
        ]
        turn = [[None] * 3 for _ in range(3)]
        for k in range(3):
            column = [rotation[j][k] * scales[k] for j in range(3)]
            pulled = [
                2.0 * (full[j][0] * column[0] + full[j][1] * column[1] + full[j][2] * column[2])
                for j in range(3)
            ]
            put(
                3 + k, pulled[0] * column[0] + pulled[1] * column[1] + pulled[2] * column[2]
            )
            for j in range(3):
                turn[j][k] = pulled[j] * scales[k]
        g_w = 2.0 * (
            z * (turn[1][0] - turn[0][1])
            + y * (turn[0][2] - turn[2][0])
            + x * (turn[2][1] - turn[1][2])
        )
        g_x = 2.0 * (
            y * (turn[0][1] + turn[1][0])
            + z * (turn[0][2] + turn[2][0])
            - 2.0 * x * (turn[1][1] + turn[2][2])
            + w * (turn[2][1] - turn[1][2])
        )
        g_y = 2.0 * (
            x * (turn[0][1] + turn[1][0])
            + z * (turn[1][2] + turn[2][1])
            - 2.0 * y * (turn[0][0] + turn[2][2])
            + w * (turn[0][2] - turn[2][0])
        )
        g_z = 2.0 * (
            x * (turn[0][2] + turn[2][0])
            + y * (turn[1][2] + turn[2][1])
            - 2.0 * z * (turn[0][0] + turn[1][1])
            + w * (turn[1][0] - turn[0][1])
        )
        along = w * g_w + x * g_x + y * g_y + z * g_z
        for k, (part, pull) in enumerate(((w, g_w), (x, g_x), (y, g_y), (z, g_z))):
            put(6 + k, norm * (pull - part * along))
        faint = given[0][8]
        for c in range(1, count):
            faint = faint + given[c][8]
        put(10, faint / (1.0 + jnp.exp(row(10))))
        for j in range(16):
            for k in range(3):
                value = basis[0][j] * given[0][5 + k]
                for c in range(1, count):
                    value = value + basis[c][j] * given[c][5 + k]
                put(11 + 3 * j + k, value)


def adam(value, first, second, gradient):
    first = 0.9 * first + 0.1 * gradient
    second = 0.999 * second + 0.001 * gradient * gradient
    root = second * lax.rsqrt(second)
    return value - learn_rate * first / (root + adam_epsilon), first, second


def update_kernel(capacity, *refs):
    (
        own_ref, near_ref, far_ref, cross_ref, params_ref, first_ref, second_ref, camera_ref,
        asked_ref, migration_ref, new_params, new_first, new_second, out_ref, left_ref, right_ref,
        cams, dense, grads, table,
    ) = refs
    blocks = params_ref.shape[1] // BLOCK
    wide = pitch(blocks)
    collect(own_ref, ((1, near_ref), (2, far_ref), (3, cross_ref)), cams)
    for block in range(blocks):
        for top, count in row_groups()[:2]:
            dense[pl.ds(top * wide + block, count, stride=wide), :] = params_ref[
                top : top + count, block * BLOCK : (block + 1) * BLOCK
            ]
    pullback(blocks, cams, dense, grads)
    for block in range(blocks):
        lanes = slice(block * BLOCK, (block + 1) * BLOCK)
        for top, count in row_groups():
            part = slice(top, top + count)
            where = pl.ds(top * wide + block, count, stride=wide)
            value, first, second = adam(
                params_ref[part, lanes], first_ref[part, lanes], second_ref[part, lanes],
                grads[where, :],
            )
            new_params[part, lanes] = value
            new_first[part, lanes] = first
            new_second[part, lanes] = second
            dense[where, :] = value
    fill_table(1, blocks, camera_ref, dense, table)
    serve(1, capacity, asked_ref, table, out_ref)
    for side, ref in ((0, left_ref), (1, right_ref)):
        for j in range(MIGH):
            lanes = pl.ds(pl.multiple_of(migration_ref[0, side, j] * BLOCK, BLOCK), BLOCK)
            for index, source in enumerate((new_params, new_first, new_second)):
                ref[index, :, j * BLOCK : (j + 1) * BLOCK] = source[:, lanes]


def final_kernel(*refs):
    (
        own_ref, near_ref, far_ref, cross_ref, params_ref, first_ref, second_ref, below_ref,
        above_ref, migration_ref, new_params, new_first, new_second, cams, dense, grads,
    ) = refs
    blocks = params_ref.shape[1] // BLOCK
    wide = pitch(blocks)
    collect(own_ref, ((1, near_ref), (2, far_ref), (3, cross_ref)), cams)
    for block in range(blocks):
        for top, count in row_groups()[:2]:
            dense[pl.ds(top * wide + block, count, stride=wide), :] = params_ref[
                top : top + count, block * BLOCK : (block + 1) * BLOCK
            ]
    moved = [
        (migration_ref[0, side, j], ref, j)
        for side, ref in ((0, below_ref), (1, above_ref))
        for j in range(MIGH)
    ]
    for block, ref, j in moved:
        for top, count in row_groups()[:2]:
            dense[pl.ds(top * wide + block, count, stride=wide), :] = ref[
                0, top : top + count, j * BLOCK : (j + 1) * BLOCK
            ]
    pullback(blocks, cams, dense, grads)
    for block in range(blocks):
        lanes = slice(block * BLOCK, (block + 1) * BLOCK)
        for top, count in row_groups():
            part = slice(top, top + count)
            value, first, second = adam(
                params_ref[part, lanes], first_ref[part, lanes], second_ref[part, lanes],
                grads[pl.ds(top * wide + block, count, stride=wide), :],
            )
            new_params[part, lanes] = value
            new_first[part, lanes] = first
            new_second[part, lanes] = second
    for block, ref, j in moved:
        lanes = pl.ds(pl.multiple_of(block * BLOCK, BLOCK), BLOCK)
        source = slice(j * BLOCK, (j + 1) * BLOCK)
        for top, count in row_groups():
            part = slice(top, top + count)
            value, first, second = adam(
                ref[0, part, source], ref[1, part, source], ref[2, part, source],
                grads[pl.ds(top * wide + block, count, stride=wide), :],
            )
            new_params[part, lanes] = value
            new_first[part, lanes] = first
            new_second[part, lanes] = second


def shape(dims, dtype=f32):
    return jax.ShapeDtypeStruct(dims, dtype)


def bind(kernel, *static):
    def run(*refs):
        kernel(*static, *refs)

    return run


def grant(mebibytes):
    return pltpu.CompilerParams(vmem_limit_bytes=mebibytes << 20)


def near_core(*values):
    return [pltpu.with_memory_space_constraint(value, pltpu.VMEM) for value in values]


def in_hbm(*values):
    return [pltpu.with_memory_space_constraint(value, pltpu.HBM) for value in values]


def swap(value, axis, offset):
    count = lax.axis_size(axis)
    return lax.ppermute(value, axis, [(i, i ^ offset) for i in range(count)])


def turn(value, axis, offset):
    count = lax.axis_size(axis)
    return lax.ppermute(value, axis, [(i, (i + offset) % count) for i in range(count)])


def exchange(value):
    far = swap(value, "rep", 2)
    near = swap(value, "rep", 1)
    cross = swap(far, "rep", 1)
    return near, far, cross


def row_exchange(value):
    return lax.all_to_all(value, "row", split_axis=0, concat_axis=0, tiled=True)


def local(
    params,
    first_moment,
    second_moment,
    camera,
    tile_corner,
    tile_owner,
    tile_block,
    depth_order,
    targets,
    migration,
):
    owners = lax.axis_size("row")
    replicas = lax.axis_size("rep")
    blocks = params.shape[1] // BLOCK
    tiles = tile_owner.shape[2]
    requests = tiles * LISTB
    capacity = max(2, 2 * ((requests + owners - 1) // owners))
    slots = capacity + 2 * MIGH
    dense = pltpu.VMEM((64 * pitch(blocks), BLOCK), f32)
    table = pltpu.VMEM((9 * blocks, BLOCK), f32)
    payload = 9 * blocks + CAM_ROWS
    cams = pltpu.VMEM((replicas, payload, BLOCK), f32)
    state = [shape(params.shape)] * 3
    kept = [pltpu.VMEM(params.shape, f32)] * 2 + [pltpu.HBM(params.shape, f32)]

    lists = pl.pallas_call(
        bind(request_kernel, capacity, blocks),
        out_shape=shape((owners, 1, BLOCK), jnp.int32),
        in_specs=[SM, SM, SM],
        out_specs=VM,
    )(tile_owner, tile_block, migration)
    asked = row_exchange(lists)
    projected = pl.pallas_call(
        project_kernel,
        out_shape=shape((9 * blocks, BLOCK)),
        in_specs=[VM, SM],
        out_specs=VM,
        scratch_shapes=[dense],
        compiler_params=grant(4),
    )(params, camera)
    message = shape((owners, up8(9 * capacity), BLOCK))
    outgoing = pl.pallas_call(
        bind(serve_kernel, capacity), out_shape=message, in_specs=[VM, SM], out_specs=VM,
        compiler_params=grant(4),
    )(projected, asked)

    deep = pltpu.VMEM((DEPTH, PIX), f32)
    packed = pltpu.VMEM((DEPTH, PIX), bf16)
    render_scratch = [
        pltpu.VMEM((tiles, DEPTH, DEPTH), bf16),
        pltpu.VMEM((DEPTH // BLOCK, 80, BLOCK), f32),
        pltpu.VMEM((DEPTH // BLOCK, 33 * tiles, BLOCK), f32),
        pltpu.VMEM((DEPTH // BLOCK, 19 * tiles, BLOCK), f32),
        pltpu.VMEM((DEPTH // BLOCK, 160, BLOCK), f32),
        pltpu.VMEM((DEPTH // BLOCK, 49 * tiles, BLOCK), f32),
    ] + [deep, deep, packed, packed, deep, *[packed] * HEAT_PIECES] * tiles
    corners = jnp.swapaxes(tile_corner, 2, 3)
    photos = jnp.swapaxes(targets, 2, 3)
    pictures_shape = shape(photos.shape)

    def gather(step, count, returned):
        return pl.pallas_call(
            bind(gather_kernel, step, capacity, count),
            out_shape=pltpu.VMEM((payload, BLOCK), f32),
            compiler_params=grant(4),
            in_specs=[VM, SM, SM, SM],
            out_specs=VM,
        )(*near_core(returned), asked, migration, camera)

    def second(arrived, pictures):
        return pl.pallas_call(
            bind(render_kernel, 1, capacity, slots, blocks, True),
            out_shape=[pictures_shape, shape((owners, up8(9 * slots), BLOCK))],
            in_specs=[VM, SM, SM, VM, VM, ANY],
            out_specs=[ANY, VM],
            input_output_aliases={5: 0},
            scratch_shapes=[
                pltpu.VMEM(photos.shape[2:], f32), pltpu.SemaphoreType.DMA, *render_scratch
            ],
            compiler_params=grant(17),
        )(
            *near_core(arrived), *in_hbm(corners), asked, depth_order, photos, pictures
        )

    arrived = row_exchange(outgoing)
    pictures, back = pl.pallas_call(
        bind(render_kernel, 0, capacity, capacity, blocks, False),
        out_shape=[pictures_shape, shape((owners, up8(9 * capacity), BLOCK))],
        in_specs=[VM, SM, SM, VM, VM],
        out_specs=[VM, VM],
        scratch_shapes=render_scratch,
        compiler_params=grant(17),
    )(*near_core(arrived), corners, asked, depth_order, photos)
    own = gather(0, capacity, row_exchange(back))
    near, far, cross = exchange(own)
    leaving = pltpu.HBM((3, P_SIZE, MIGH * BLOCK), f32)
    current, moment_one, moment_two, outgoing, left, right = pl.pallas_call(
        bind(update_kernel, capacity),
        out_shape=kept + [shape((owners, up8(9 * capacity), BLOCK)), leaving, leaving],
        in_specs=[VM] * 7 + [SM] * 3,
        out_specs=[VM] * 6,
        scratch_shapes=[cams, dense, dense, table],
        compiler_params=grant(12),
    )(
        *near_core(own, near, far, cross, params), *in_hbm(first_moment, second_moment), camera, asked, migration,
    )
    arrived = row_exchange(outgoing)
    below = turn(right, "row", 1)
    above = turn(left, "row", -1)
    pictures, back = second(arrived, pictures)
    own = gather(1, slots, row_exchange(back))
    near, far, cross = exchange(own)
    current, moment_one, moment_two = pl.pallas_call(
        final_kernel,
        out_shape=state,
        in_specs=[VM] * 9 + [SM],
        out_specs=[VM] * 3,
        scratch_shapes=[cams, dense, dense],
        compiler_params=grant(16),
    )(
        *near_core(own, near, far, cross, current, moment_one), *in_hbm(moment_two, below, above),
        *in_hbm(migration),
    )
    return current, moment_one, moment_two, jnp.swapaxes(pictures, 2, 3)


def solution(mesh):
    return jax.shard_map(
        local,
        mesh=mesh,
        in_specs=(
            P(None, "row"),
            P(None, "row"),
            P(None, "row"),
            P(None, "rep", None),
            P(None, "rep", "row", None),
            P(None, "rep", "row", None),
            P(None, "rep", "row", None),
            P(None, "rep", "row", None),
            P(None, "rep", "row", None, None),
            P("row", None, None),
        ),
        out_specs=(
            P(None, "row"),
            P(None, "row"),
            P(None, "row"),
            P(None, "rep", "row", None, None),
        ),
        check_vma=False,
    )
```

```python
import jax
import jax.numpy as jnp
from jax import lax
from jax.experimental import pallas as pl
from jax.experimental.pallas import tpu as pltpu
from jax.sharding import PartitionSpec as P


P_SIZE = 59
BLOCK = 128
LISTB = 4
PIX = 256
ITERS = 2
MIGH = 2
DEPTH = 512
SIDE = 16
MIG_LANE = 64
PLAN_LANE = 72
RANK_BIT = 12
OWNER_BIT = 20
CAM_ROWS = 16
LOG2E = 1.4426950408889634

harm_zero = 0.28209479177387814
harm_one = 0.4886025119029199
harm_two = (
    1.0925484305920792,
    -1.0925484305920792,
    0.31539156525252005,
    -1.0925484305920792,
    0.5462742152960396,
)
harm_three = (
    -0.5900435899266435,
    2.890611442640554,
    -0.4570457994644658,
    0.3731763325901154,
    -0.4570457994644658,
    1.445305721320277,
    -0.5900435899266435,
)
learn_rate = 0.01
adam_epsilon = 1e-08

f32 = jnp.float32
bf16 = jnp.bfloat16
VM = pl.BlockSpec(memory_space=pltpu.VMEM)
SM = pl.BlockSpec(memory_space=pltpu.SMEM)
ANY = pl.BlockSpec(memory_space=pl.ANY)


def pitch(blocks):
    return blocks + 1 - blocks % 2


def up8(count):
    return -(-count // 8) * 8


def harmonics(x, y, z):
    xx, yy, zz = x * x, y * y, z * z
    return [
        harm_zero + 0.0 * x,
        -harm_one * y,
        harm_one * z,
        -harm_one * x,
        harm_two[0] * x * y,
        harm_two[1] * y * z,
        harm_two[2] * (2.0 * zz - xx - yy),
        harm_two[3] * x * z,
        harm_two[4] * (xx - yy),
        harm_three[0] * y * (3.0 * xx - yy),
        harm_three[1] * x * y * z,
        harm_three[2] * y * (4.0 * zz - xx - yy),
        harm_three[3] * z * (2.0 * zz - 3.0 * xx - 3.0 * yy),
        harm_three[4] * x * (4.0 * zz - xx - yy),
        harm_three[5] * z * (xx - yy),
        harm_three[6] * x * (xx - 3.0 * yy),
    ]


def split(value, pieces):
    out = []
    for piece in range(pieces):
        part = value.astype(bf16)
        out.append(part)
        if piece < pieces - 1:
            value = value - part.astype(f32)
    return out


def dot(left, right, dims=((1,), (0,))):
    return lax.dot_general(left, right, (dims, ((), ())), preferred_element_type=f32)


NT = ((1,), (1,))
TN = ((0,), (0,))


def request_kernel(capacity, owner_ref, block_ref, migration_ref, out_ref, counts):
    owners = out_ref.shape[0]
    tiles = owner_ref.shape[2]
    lane = lax.broadcasted_iota(jnp.int32, (owners, BLOCK), 1)
    row = lax.broadcasted_iota(jnp.int32, (owners, BLOCK), 0)
    place = row * BLOCK + lane
    message = jnp.full((owners, BLOCK), -1, jnp.int32)
    for step in range(ITERS):
        for owner in range(owners):
            counts[step, owner] = 0
    for step in range(ITERS):
        names = [owner_ref[step, 0, t, j] for t in range(tiles) for j in range(LISTB)]
        for index in range(tiles * LISTB):
            rank = counts[step, names[index]]
            counts[step, names[index]] = rank + 1
            target = names[index] * BLOCK + step * capacity + rank
            block = block_ref[step, 0, index // LISTB, index % LISTB]
            message = jnp.where(place == target, block, message)
            plan = (names[index] << OWNER_BIT) | (rank << RANK_BIT) | block
            message = jnp.where(
                lane == PLAN_LANE + step * tiles * LISTB + index, plan, message
            )
    for side in range(2):
        for j in range(MIGH):
            message = jnp.where(
                lane == MIG_LANE + side * MIGH + j, migration_ref[0, side, j], message
            )
    for owner in range(owners):
        out_ref[owner] = message[owner : owner + 1]


def geometry(row):
    scales = [jnp.exp(row(3 + k)) for k in range(3)]
    quats = [row(6 + k) for k in range(4)]
    norm = lax.rsqrt(
        quats[0] * quats[0] + quats[1] * quats[1] + quats[2] * quats[2] + quats[3] * quats[3]
    )
    w, x, y, z = [part * norm for part in quats]
    rotation = [
        [1.0 - 2.0 * (y * y + z * z), 2.0 * (x * y - w * z), 2.0 * (x * z + w * y)],
        [2.0 * (x * y + w * z), 1.0 - 2.0 * (x * x + z * z), 2.0 * (y * z - w * x)],
        [2.0 * (x * z - w * y), 2.0 * (y * z + w * x), 1.0 - 2.0 * (x * x + y * y)],
    ]
    return scales, (w, x, y, z), norm, rotation


def conic_of(scales, rotation, affine):
    spread = [
        [
            (
                affine[3 * i] * rotation[0][k]
                + affine[3 * i + 1] * rotation[1][k]
                + affine[3 * i + 2] * rotation[2][k]
            )
            * scales[k]
            for k in range(3)
        ]
        for i in range(2)
    ]
    one, two = spread
    cov_xx = one[0] * one[0] + one[1] * one[1] + one[2] * one[2] + 0.3
    cov_yy = two[0] * two[0] + two[1] * two[1] + two[2] * two[2] + 0.3
    cov_xy = one[0] * two[0] + one[1] * two[1] + one[2] * two[2]
    inverse = 1.0 / (cov_xx * cov_yy - cov_xy * cov_xy)
    return cov_yy * inverse, -cov_xy * inverse, cov_xx * inverse


def fill_table(step, blocks, camera_ref, dense, table):
    wide = pitch(blocks)
    cam = [camera_ref[step, 0, k] for k in range(11)]
    basis = harmonics(cam[8], cam[9], cam[10])
    for group in range(blocks // 8):

        def row(p):
            return dense[p * wide + 8 * group : p * wide + 8 * group + 8, :]

        scales, _, _, rotation = geometry(row)
        conic = conic_of(scales, rotation, cam)
        means = [row(k) for k in range(3)]
        rows = [
            cam[0] * means[0] + cam[1] * means[1] + cam[2] * means[2] + cam[6],
            cam[3] * means[0] + cam[4] * means[1] + cam[5] * means[2] + cam[7],
            conic[0],
            conic[1],
            conic[2],
        ]
        for k in range(3):
            colour = basis[0] * row(11 + k)
            for j in range(1, 16):
                colour = colour + basis[j] * row(11 + 3 * j + k)
            rows.append(0.5 + colour)
        rows.append(-LOG2E * jnp.log(1.0 + jnp.exp(-row(10))))
        for k in range(9):
            table[pl.ds(72 * group + k, 8, stride=9), :] = rows[k]


def serve(step, capacity, asked_ref, table, out_ref):
    owners = out_ref.shape[0]
    for peer in range(owners):
        for slot in range(capacity):
            block = jnp.maximum(asked_ref[peer, 0, step * capacity + slot], 0)
            out_ref[peer, 8 * slot : 8 * slot + 8, :] = table[pl.ds(block * 9, 8), :]
            out_ref[peer, 8 * capacity + slot : 8 * capacity + slot + 1, :] = table[
                pl.ds(block * 9 + 8, 1), :
            ]


def row_groups():
    return [(first, min(8, P_SIZE - first)) for first in range(0, P_SIZE, 8)]


def project_kernel(params_ref, camera_ref, table, dense):
    blocks = params_ref.shape[1] // BLOCK
    wide = pitch(blocks)
    for block in range(blocks):
        for first, count in row_groups():
            dense[pl.ds(first * wide + block, count, stride=wide), :] = params_ref[
                first : first + count, block * BLOCK : (block + 1) * BLOCK
            ]
    fill_table(0, blocks, camera_ref, dense, table)


def serve_kernel(capacity, table, asked_ref, out_ref):
    serve(0, capacity, asked_ref, table, out_ref)


def pixel_features(rows, per):
    pixel = lax.broadcasted_iota(jnp.int32, (rows, PIX), 1)
    which = lax.broadcasted_iota(jnp.int32, (rows, PIX), 0) // per
    px = (pixel % SIDE).astype(f32) - (SIDE / 2 - 0.5)
    py = (pixel // SIDE).astype(f32) - (SIDE / 2 - 0.5)
    chosen = jnp.where(which == 0, 1.0, 0.0)
    for index, value in enumerate((px, py, px * px, px * py, py * py)):
        chosen = jnp.where(which == index + 1, value, chosen)
    return chosen.astype(bf16)


def lane_gather(pieces, within, source):
    got = jnp.take_along_axis(pieces[0], within, axis=1)
    for j in range(1, len(pieces)):
        got = jnp.where(source == j, jnp.take_along_axis(pieces[j], within, axis=1), got)
    return got


HEAT_PIECES = 2


def put(ref, rows, value):
    for k in range(ref.shape[0]):
        ref[k, rows, :] = value[:, k * BLOCK : (k + 1) * BLOCK]


def get(ref, first, count):
    return jnp.concatenate([ref[k, first : first + count, :] for k in range(ref.shape[0])], axis=1)


COL_ROWS = {0: (0, 9, 15), 1: (3, 12), 2: (6,)}


def render_kernel(step, capacity, slots, final, *refs):
    if final:
        (
            arrived, corner_ref, asked_ref, order_ref, target_ref, earlier_ref,
            rendered_ref, out_ref, picture_ref, leaving, *scratch,
        ) = refs
        store = pltpu.make_async_copy(picture_ref, rendered_ref.at[step, 0], leaving)
    else:
        (
            arrived, corner_ref, asked_ref, order_ref, target_ref,
            rendered_ref, out_ref, *scratch,
        ) = refs
        picture_ref = rendered_ref.at[step, 0]
    onehots, sorted_ref, coeffs, shades_ref, sums_ref, grads_ref, *per_tile = scratch
    owners = arrived.shape[0]
    tiles = order_ref.shape[2]
    lists = DEPTH // BLOCK
    segments = 8
    steps = DEPTH // segments
    out_ref[...] = jnp.zeros_like(out_ref)
    coeffs[...] = jnp.zeros_like(coeffs)
    features = pixel_features(32, 3)
    flat = pixel_features(16, 1)

    mine = lax.axis_index("row")
    plans = [
        asked_ref[mine, 0, PLAN_LANE + step * tiles * LISTB + index]
        for index in range(tiles * LISTB)
    ]
    numbers = [plan & ((1 << RANK_BIT) - 1) for plan in plans]
    ranks = [(plan >> RANK_BIT) & ((1 << (OWNER_BIT - RANK_BIT)) - 1) for plan in plans]
    names = [plan >> OWNER_BIT for plan in plans]

    order = order_ref[step, 0]
    order = jnp.concatenate([order] * (8 // tiles), axis=0)
    order_pieces = [order[:, k * BLOCK : (k + 1) * BLOCK] for k in range(lists)]
    woven = []
    for k in range(lists):
        row = lax.broadcasted_iota(jnp.int32, order_pieces[0].shape, 1) + k * BLOCK
        nth = (row % segments) * steps + row // segments
        woven.append(lane_gather(order_pieces, nth & (BLOCK - 1), nth // BLOCK))
    all_within = [piece & (BLOCK - 1) for piece in woven]
    all_source = [piece // BLOCK for piece in woven]
    faint_pieces = []
    for j in range(LISTB):
        parts = [
            arrived[
                names[t * LISTB + j], pl.ds(8 * capacity + ranks[t * LISTB + j], 1), :
            ]
            for t in range(tiles)
        ]
        faint_pieces.append(jnp.concatenate(parts * (8 // tiles), axis=0))
    faint = [lane_gather(faint_pieces, all_within[k], all_source[k]) for k in range(lists)]
    faint = jnp.concatenate(faint, axis=1)[0:tiles]
    row_id = lax.broadcasted_iota(jnp.int32, (BLOCK, BLOCK), 0).astype(f32).astype(bf16)
    sub = lax.broadcasted_iota(jnp.int32, (segments, PIX), 0)

    for tile in range(tiles):
        one = slice(tile, tile + 1)
        pieces = [
            arrived[
                names[tile * LISTB + j],
                pl.ds(pl.multiple_of(ranks[tile * LISTB + j] * 8, 8), 8),
                :,
            ]
            for j in range(LISTB)
        ]
        for k in range(lists):
            within = jnp.broadcast_to(all_within[k][one], (8, BLOCK))
            source = jnp.broadcast_to(all_source[k][one], (8, BLOCK))
            sorted_ref[k, pl.ds(tile, 8, stride=9), :] = lane_gather(
                pieces, within, source
            )

    def param(k):
        return get(sorted_ref, 9 * k, tiles)

    which = lax.broadcasted_iota(jnp.int32, (tiles, DEPTH), 0)
    corner_x = jnp.zeros((tiles, DEPTH), f32)
    corner_y = jnp.zeros((tiles, DEPTH), f32)
    for tile in range(tiles):
        corner_x = jnp.where(which == tile, corner_ref[step, 0, 0, tile], corner_x)
        corner_y = jnp.where(which == tile, corner_ref[step, 0, 1, tile], corner_y)
    all_u = u = param(0) - (corner_x + SIDE / 2)
    all_v = v = param(1) - (corner_y + SIDE / 2)
    half_a, half_b, half_c = (
        (-0.5 * LOG2E) * param(2), -LOG2E * param(3), (-0.5 * LOG2E) * param(4)
    )
    values = (
        half_a * u * u + half_b * u * v + half_c * v * v + faint,
        -(2.0 * half_a * u + half_b * v),
        -(2.0 * half_c * v + half_b * u),
        half_a,
        half_b,
        half_c,
    )
    for index, value in enumerate(values):
        for piece, part in enumerate(split(value, 3)):
            put(coeffs, pl.ds(3 * index + piece, tiles, stride=33), part.astype(f32))
    for k in range(3):
        for piece, part in enumerate(split(param(5 + k), 3)):
            for at in COL_ROWS[piece]:
                put(shades_ref, pl.ds(at + k, tiles, stride=19), part.astype(f32))

    def opening(tile, ratios, locals_, weight_h, weight_m, mixed, heats):
        form = get(coeffs, 33 * tile, 32).astype(bf16)
        passed = jnp.ones((segments, PIX), f32)
        for k in range(lists):
            power = dot(form[:, k * BLOCK : (k + 1) * BLOCK], features, TN)
            for at in range(0, BLOCK, segments):
                here = slice(k * BLOCK + at, k * BLOCK + at + segments)
                alpha = jnp.exp2(power[at : at + segments])
                keep = 1.0 - alpha
                ratios[here, :] = alpha / keep
                locals_[here, :] = alpha * passed
                passed = passed * keep
        for shift in (1, 2, 4):
            passed = passed * jnp.where(sub >= shift, pltpu.roll(passed, shift, 0), 1.0)
        return jnp.where(sub >= 1, pltpu.roll(passed, 1, 0), 1.0)

    def picture(tile, passed, ratios, locals_, weight_h, weight_m, mixed, heats):
        one = slice(tile, tile + 1)
        twice = jnp.concatenate([passed, passed], axis=0)
        for at in range(0, DEPTH, 2 * segments):
            here = slice(at, at + 2 * segments)
            weight_h[here, :], weight_m[here, :] = split(locals_[here, :] * twice, 2)
        col_left = get(shades_ref, 19 * tile, 9).astype(bf16)
        shades = dot(col_left, weight_h[...]) + dot(col_left, weight_m[...])
        shades = shades[0:3] + shades[3:6] + shades[6:9]
        for k in range(3):
            picture_ref[k, one, :] = shades[k : k + 1]
        error = shades - jnp.concatenate(
            [target_ref[step, 0, k, one, :] for k in range(3)], axis=0
        )
        err_h, err_m, err_l = [part.astype(f32) for part in split(error, 3)]
        return jnp.concatenate([err_h, err_h, err_h, err_m, err_m, err_l], axis=0).astype(bf16)

    def closing(tile, passed, errors, ratios, locals_, weight_h, weight_m, mixed, heats):
        err_left = jnp.concatenate(
            [errors.astype(f32)[0:3], errors.astype(f32)[9:12], errors.astype(f32)[15:18]], axis=0
        ).astype(bf16)
        col_grads = dot(err_left, weight_h[...], NT) + dot(err_left, weight_m[...], NT)
        put(sums_ref, pl.ds(72 + tile, 8, stride=9), col_grads[0:8])
        put(sums_ref, slice(144 + tile, 145 + tile), col_grads[8:9])
        col_right = get(shades_ref, 19 * tile, 18).astype(bf16)
        total = jnp.zeros((segments, PIX), f32)
        for k in reversed(range(lists)):
            seen = dot(col_right[:, k * BLOCK : (k + 1) * BLOCK], errors, TN)
            for at in reversed(range(0, BLOCK, segments)):
                here = slice(k * BLOCK + at, k * BLOCK + at + segments)
                flow = locals_[here, :] * passed * seen[at : at + segments]
                mixed[here, :] = flow - ratios[here, :] * total
                total = total + flow
        for shift in (1, 2, 4):
            total = total + jnp.where(
                sub < segments - shift, pltpu.roll(total, segments - shift, 0), 0.0
            )
        total = jnp.where(sub < segments - 1, pltpu.roll(total, segments - 1, 0), 0.0)
        twice = jnp.concatenate([total, total], axis=0)
        for at in range(0, DEPTH, 2 * segments):
            here = slice(at, at + 2 * segments)
            parts = split(mixed[here, :] - ratios[here, :] * twice, HEAT_PIECES)
            for ref, part in zip(heats, parts):
                ref[here, :] = part
        moments = dot(flat, heats[0][...], NT)
        for ref in heats[1:]:
            moments = moments + dot(flat, ref[...], NT)
        put(sums_ref, pl.ds(tile, 8, stride=9), moments[0:8])

    def unsort_matrix(tile):
        one = slice(tile, tile + 1)
        for k in range(lists):
            local = woven[k][one].astype(f32)
            for piece in range(lists):
                inside = jnp.where(all_source[k][one] == piece, local - piece * BLOCK, -1.0)
                onehots[
                    tile, piece * BLOCK : (piece + 1) * BLOCK, k * BLOCK : (k + 1) * BLOCK
                ] = jnp.where(row_id == inside.astype(bf16), jnp.ones((), bf16), jnp.zeros((), bf16))

    def buffers(tile):
        each = len(per_tile) // tiles
        mine = per_tile[each * tile : each * tile + each]
        return (*mine[0:5], mine[5:])

    def finish(first, count):
        def summed(row):
            return get(sums_ref, 9 * row + first, count)

        group = slice(first, first + count)
        a, b, c = [get(sorted_ref, 9 * k + first, count) for k in (2, 3, 4)]
        u, v = all_u[group], all_v[group]
        m00, m10, m01, m20, m11, m02 = [summed(k) for k in range(6)]
        x1, y1 = m10 - u * m00, m01 - v * m00
        grads = [
            a * x1 + b * y1,
            b * x1 + c * y1,
            -0.5 * (m20 - 2.0 * u * m10 + u * u * m00),
            -(m11 - u * m01 - v * m10 + u * v * m00),
            -0.5 * (m02 - 2.0 * v * m01 + v * v * m00),
            *[summed(8 + k) + summed(11 + k) + summed(14 + k) for k in range(3)],
            m00,
        ]
        for k, value in enumerate(grads):
            for piece, part in enumerate(split(value, 3)):
                put(grads_ref, pl.ds(49 * first + 16 * piece + k, count, stride=49), part.astype(f32))
        for tile in range(first, first + count):
            unsort(tile)

    def unsort(tile):
        listed = dot(get(grads_ref, 49 * tile, 48).astype(bf16), onehots[tile], NT)
        listed = listed[0:16] + listed[16:32] + listed[32:48]
        for j in range(LISTB):
            name, rank = names[tile * LISTB + j], ranks[tile * LISTB + j]
            if final:
                block = numbers[tile * LISTB + j]
                hop = jnp.int32(0)
                for k in range(MIGH):
                    goes_left = asked_ref[name, 0, MIG_LANE + k] == block
                    goes_right = asked_ref[name, 0, MIG_LANE + MIGH + k] == block
                    rank = jnp.where(goes_left, capacity + MIGH + k, rank)
                    rank = jnp.where(goes_right, capacity + k, rank)
                    hop = hop - goes_left.astype(jnp.int32) + goes_right.astype(jnp.int32)
                name = name + hop
                name = jnp.where(name < 0, owners - 1, jnp.where(name >= owners, 0, name))
            lanes = slice(j * BLOCK, (j + 1) * BLOCK)
            main = pl.ds(pl.multiple_of(rank * 8, 8), 8)
            extra = pl.ds(8 * slots + rank, 1)
            if final:
                out_ref[name, main, :] = out_ref[name, main, :] + listed[0:8, lanes]
                out_ref[name, extra, :] = out_ref[name, extra, :] + listed[8:9, lanes]
            else:
                out_ref[name, main, :] = listed[0:8, lanes]
                out_ref[name, extra, :] = listed[8:9, lanes]


    passes, errors = {}, {}
    for tile in range(tiles):
        passes[tile] = opening(tile, *buffers(tile))
    for tile in range(tiles):
        errors[tile] = picture(tile, passes[tile], *buffers(tile))
    if final:
        store.start()
    for tile in range(tiles):
        unsort_matrix(tile)
    for tile in range(tiles):
        closing(tile, passes[tile], errors[tile], *buffers(tile))
        if tile % 2 == 1 or tile == tiles - 1:
            finish(tile - tile % 2, 1 + tile % 2)
    if final:
        store.wait()


def gather_kernel(step, capacity, slots, returned, asked_ref, migration_ref, camera_ref, out_ref):
    owners = returned.shape[0]
    blocks = (out_ref.shape[0] - CAM_ROWS) // 9
    out_ref[...] = jnp.zeros_like(out_ref)

    def body(peer, carry):
        for slot in range(slots):
            if slot < capacity:
                block = jnp.maximum(asked_ref[peer, 0, step * capacity + slot], 0)
            else:
                block = migration_ref[0, (slot - capacity) // MIGH, (slot - capacity) % MIGH]
            main = pl.ds(block * 9, 8)
            extra = pl.ds(block * 9 + 8, 1)
            out_ref[main, :] = out_ref[main, :] + returned[peer, 8 * slot : 8 * slot + 8, :]
            out_ref[extra, :] = (
                out_ref[extra, :] + returned[peer, 8 * slots + slot : 8 * slots + slot + 1, :]
            )
        return carry

    lax.fori_loop(0, owners, body, 0)
    for index, k in enumerate((0, 1, 2, 3, 4, 5, 8, 9, 10)):
        at = 9 * blocks + index
        out_ref[at : at + 1, :] = jnp.full((1, BLOCK), camera_ref[step, 0, k], f32)


def collect(own_ref, others, scratch):
    mine = lax.axis_index("rep")
    scratch[mine] = own_ref[...]
    for offset, ref in others:
        scratch[mine ^ offset] = ref[...]


def pullback(blocks, cams, dense, grads):
    count = cams.shape[0]
    wide = pitch(blocks)
    affine, basis = [], []
    for c in range(count):
        rows = [
            jnp.broadcast_to(cams[c, 9 * blocks + k : 9 * blocks + k + 1, :], (8, BLOCK))
            for k in range(9)
        ]
        affine.append(rows[0:6])
        basis.append(harmonics(rows[6], rows[7], rows[8]))
    for group in range(blocks // 8):

        def row(p):
            return dense[p * wide + 8 * group : p * wide + 8 * group + 8, :]

        def put(p, value):
            grads[p * wide + 8 * group : p * wide + 8 * group + 8, :] = value

        given = [
            [cams[c, pl.ds(72 * group + k, 8, stride=9), :] for k in range(9)] for c in range(count)
        ]
        scales, (w, x, y, z), norm, rotation = geometry(row)
        means = [0.0, 0.0, 0.0]
        sigma = [0.0] * 6
        for c in range(count):
            m = affine[c]
            a, b, d = conic_of(scales, rotation, m)
            g_x, g_y, g_a, g_b, g_d = given[c][0:5]
            for k in range(3):
                means[k] = means[k] + m[k] * g_x + m[3 + k] * g_y
            g_b = 0.5 * g_b
            t00, t01 = a * g_a + b * g_b, a * g_b + b * g_d
            t10, t11 = b * g_a + d * g_b, b * g_b + d * g_d
            h00 = -(t00 * a + t01 * b)
            h01 = -(t00 * b + t01 * d)
            h11 = -(t10 * b + t11 * d)
            top = [h00 * m[k] + h01 * m[3 + k] for k in range(3)]
            low = [h01 * m[k] + h11 * m[3 + k] for k in range(3)]
            for index, (i, k) in enumerate(((0, 0), (0, 1), (0, 2), (1, 1), (1, 2), (2, 2))):
                sigma[index] = sigma[index] + m[i] * top[k] + m[3 + i] * low[k]
        for k in range(3):
            put(k, means[k])
        full = [
            [sigma[0], sigma[1], sigma[2]],
            [sigma[1], sigma[3], sigma[4]],
            [sigma[2], sigma[4], sigma[5]],
        ]
        turn = [[None] * 3 for _ in range(3)]
        for k in range(3):
            column = [rotation[j][k] * scales[k] for j in range(3)]
            pulled = [
                2.0 * (full[j][0] * column[0] + full[j][1] * column[1] + full[j][2] * column[2])
                for j in range(3)
            ]
            put(
                3 + k, pulled[0] * column[0] + pulled[1] * column[1] + pulled[2] * column[2]
            )
            for j in range(3):
                turn[j][k] = pulled[j] * scales[k]
        g_w = 2.0 * (
            z * (turn[1][0] - turn[0][1])
            + y * (turn[0][2] - turn[2][0])
            + x * (turn[2][1] - turn[1][2])
        )
        g_x = 2.0 * (
            y * (turn[0][1] + turn[1][0])
            + z * (turn[0][2] + turn[2][0])
            - 2.0 * x * (turn[1][1] + turn[2][2])
            + w * (turn[2][1] - turn[1][2])
        )
        g_y = 2.0 * (
            x * (turn[0][1] + turn[1][0])
            + z * (turn[1][2] + turn[2][1])
            - 2.0 * y * (turn[0][0] + turn[2][2])
            + w * (turn[0][2] - turn[2][0])
        )
        g_z = 2.0 * (
            x * (turn[0][2] + turn[2][0])
            + y * (turn[1][2] + turn[2][1])
            - 2.0 * z * (turn[0][0] + turn[1][1])
            + w * (turn[1][0] - turn[0][1])
        )
        along = w * g_w + x * g_x + y * g_y + z * g_z
        for k, (part, pull) in enumerate(((w, g_w), (x, g_x), (y, g_y), (z, g_z))):
            put(6 + k, norm * (pull - part * along))
        faint = given[0][8]
        for c in range(1, count):
            faint = faint + given[c][8]
        put(10, faint / (1.0 + jnp.exp(row(10))))
        for j in range(16):
            for k in range(3):
                value = basis[0][j] * given[0][5 + k]
                for c in range(1, count):
                    value = value + basis[c][j] * given[c][5 + k]
                put(11 + 3 * j + k, value)


def adam(value, first, second, gradient):
    first = 0.9 * first + 0.1 * gradient
    second = 0.999 * second + 0.001 * gradient * gradient
    root = second * lax.rsqrt(second)
    return value - learn_rate * first / (root + adam_epsilon), first, second


def update_kernel(capacity, *refs):
    (
        own_ref, near_ref, far_ref, cross_ref, params_ref, first_ref, second_ref, camera_ref,
        asked_ref, migration_ref, new_params, new_first, new_second, out_ref, left_ref, right_ref,
        cams, dense, grads, table,
    ) = refs
    blocks = params_ref.shape[1] // BLOCK
    wide = pitch(blocks)
    collect(own_ref, ((1, near_ref), (2, far_ref), (3, cross_ref)), cams)
    for block in range(blocks):
        for top, count in row_groups()[:2]:
            dense[pl.ds(top * wide + block, count, stride=wide), :] = params_ref[
                top : top + count, block * BLOCK : (block + 1) * BLOCK
            ]
    pullback(blocks, cams, dense, grads)
    for block in range(blocks):
        lanes = slice(block * BLOCK, (block + 1) * BLOCK)
        for top, count in row_groups():
            part = slice(top, top + count)
            where = pl.ds(top * wide + block, count, stride=wide)
            value, first, second = adam(
                params_ref[part, lanes], first_ref[part, lanes], second_ref[part, lanes],
                grads[where, :],
            )
            new_params[part, lanes] = value
            new_first[part, lanes] = first
            new_second[part, lanes] = second
            dense[where, :] = value
    fill_table(1, blocks, camera_ref, dense, table)
    serve(1, capacity, asked_ref, table, out_ref)
    for side, ref in ((0, left_ref), (1, right_ref)):
        for j in range(MIGH):
            lanes = pl.ds(pl.multiple_of(migration_ref[0, side, j] * BLOCK, BLOCK), BLOCK)
            for index, source in enumerate((new_params, new_first, new_second)):
                ref[index, :, j * BLOCK : (j + 1) * BLOCK] = source[:, lanes]


def final_kernel(*refs):
    (
        own_ref, near_ref, far_ref, cross_ref, params_ref, first_ref, second_ref, below_ref,
        above_ref, migration_ref, new_params, new_first, new_second, cams, dense, grads,
        params, first_moment, second_moment, sems,
    ) = refs
    blocks = params_ref.shape[1] // BLOCK
    wide = pitch(blocks)
    collect(own_ref, ((1, near_ref), (2, far_ref), (3, cross_ref)), cams)
    for block in range(blocks):
        for top, count in row_groups()[:2]:
            dense[pl.ds(top * wide + block, count, stride=wide), :] = params_ref[
                top : top + count, block * BLOCK : (block + 1) * BLOCK
            ]
    moved = [
        (migration_ref[0, side, j], ref, j)
        for side, ref in ((0, below_ref), (1, above_ref))
        for j in range(MIGH)
    ]
    for block, ref, j in moved:
        for top, count in row_groups()[:2]:
            dense[pl.ds(top * wide + block, count, stride=wide), :] = ref[
                0, top : top + count, j * BLOCK : (j + 1) * BLOCK
            ]
    pullback(blocks, cams, dense, grads)
    targets = (params, first_moment, second_moment)
    copies = []
    for group, (top, count) in enumerate(row_groups()):
        part = slice(top, top + count)
        for block in range(blocks):
            lanes = slice(block * BLOCK, (block + 1) * BLOCK)
            values = adam(
                params_ref[part, lanes], first_ref[part, lanes], second_ref[part, lanes],
                grads[pl.ds(top * wide + block, count, stride=wide), :],
            )
            for target, value in zip(targets, values):
                target[part, lanes] = value
        for block, ref, j in moved:
            lanes = pl.ds(pl.multiple_of(block * BLOCK, BLOCK), BLOCK)
            source = slice(j * BLOCK, (j + 1) * BLOCK)
            values = adam(
                ref[0, part, source], ref[1, part, source], ref[2, part, source],
                grads[pl.ds(top * wide + block, count, stride=wide), :],
            )
            for target, value in zip(targets, values):
                target[part, lanes] = value
        for index, (target, result) in enumerate(zip(targets, (new_params, new_first, new_second))):
            copy = pltpu.make_async_copy(
                target.at[part, :], result.at[part, :], sems.at[index, group]
            )
            copy.start()
            copies.append(copy)
    for copy in copies:
        copy.wait()


def shape(dims, dtype=f32):
    return jax.ShapeDtypeStruct(dims, dtype)


def bind(kernel, *static):
    def run(*refs):
        kernel(*static, *refs)

    return run


def grant(mebibytes):
    return pltpu.CompilerParams(vmem_limit_bytes=mebibytes << 20)


def near_core(*values):
    return [pltpu.with_memory_space_constraint(value, pltpu.VMEM) for value in values]


def in_hbm(*values):
    return [pltpu.with_memory_space_constraint(value, pltpu.HBM) for value in values]


def swap(value, axis, offset):
    count = lax.axis_size(axis)
    return lax.ppermute(value, axis, [(i, i ^ offset) for i in range(count)])


def turn(value, axis, offset):
    count = lax.axis_size(axis)
    return lax.ppermute(value, axis, [(i, (i + offset) % count) for i in range(count)])


def exchange(value):
    far = swap(value, "rep", 2)
    near = swap(value, "rep", 1)
    cross = swap(far, "rep", 1)
    return near, far, cross


def row_exchange(value):
    return lax.all_to_all(value, "row", split_axis=0, concat_axis=0, tiled=True)


def local(
    params,
    first_moment,
    second_moment,
    camera,
    tile_corner,
    tile_owner,
    tile_block,
    depth_order,
    targets,
    migration,
):
    owners = lax.axis_size("row")
    replicas = lax.axis_size("rep")
    blocks = params.shape[1] // BLOCK
    tiles = tile_owner.shape[2]
    requests = tiles * LISTB
    capacity = max(2, 2 * ((requests + owners - 1) // owners))
    slots = capacity + 2 * MIGH
    dense = pltpu.VMEM((64 * pitch(blocks), BLOCK), f32)
    table = pltpu.VMEM((9 * blocks, BLOCK), f32)
    payload = 9 * blocks + CAM_ROWS
    cams = pltpu.VMEM((replicas, payload, BLOCK), f32)
    state = [shape(params.shape)] * 3
    kept = [pltpu.VMEM(params.shape, f32)] * 2 + [pltpu.HBM(params.shape, f32)]

    lists = pl.pallas_call(
        bind(request_kernel, capacity),
        out_shape=shape((owners, 1, BLOCK), jnp.int32),
        in_specs=[SM, SM, SM],
        out_specs=VM,
        scratch_shapes=[pltpu.SMEM((ITERS, owners), jnp.int32)],
    )(tile_owner, tile_block, migration)
    asked = row_exchange(lists)
    projected = pl.pallas_call(
        project_kernel,
        out_shape=shape((9 * blocks, BLOCK)),
        in_specs=[VM, SM],
        out_specs=VM,
        scratch_shapes=[dense],
        compiler_params=grant(4),
    )(params, camera)
    message = shape((owners, up8(9 * capacity), BLOCK))
    outgoing = pl.pallas_call(
        bind(serve_kernel, capacity), out_shape=message, in_specs=[VM, SM], out_specs=VM,
        compiler_params=grant(4),
    )(projected, asked)

    deep = pltpu.VMEM((DEPTH, PIX), f32)
    packed = pltpu.VMEM((DEPTH, PIX), bf16)
    render_scratch = [
        pltpu.VMEM((tiles, DEPTH, DEPTH), bf16),
        pltpu.VMEM((DEPTH // BLOCK, 80, BLOCK), f32),
        pltpu.VMEM((DEPTH // BLOCK, 33 * tiles, BLOCK), f32),
        pltpu.VMEM((DEPTH // BLOCK, 19 * tiles, BLOCK), f32),
        pltpu.VMEM((DEPTH // BLOCK, 160, BLOCK), f32),
        pltpu.VMEM((DEPTH // BLOCK, 49 * tiles, BLOCK), f32),
    ] + [deep, deep, packed, packed, deep, *[packed] * HEAT_PIECES] * tiles
    corners = jnp.swapaxes(tile_corner, 2, 3)
    photos = jnp.swapaxes(targets, 2, 3)
    pictures_shape = shape(photos.shape)

    def gather(step, count, returned):
        return pl.pallas_call(
            bind(gather_kernel, step, capacity, count),
            out_shape=pltpu.VMEM((payload, BLOCK), f32),
            compiler_params=grant(4),
            in_specs=[VM, SM, SM, SM],
            out_specs=VM,
        )(*near_core(returned), asked, migration, camera)

    def second(arrived, pictures):
        return pl.pallas_call(
            bind(render_kernel, 1, capacity, slots, True),
            out_shape=[pictures_shape, shape((owners, up8(9 * slots), BLOCK))],
            in_specs=[VM, SM, SM, VM, VM, ANY],
            out_specs=[ANY, VM],
            input_output_aliases={5: 0},
            scratch_shapes=[
                pltpu.VMEM(photos.shape[2:], f32), pltpu.SemaphoreType.DMA, *render_scratch
            ],
            compiler_params=grant(17),
        )(
            *near_core(arrived), *in_hbm(corners), asked, depth_order, photos, pictures
        )

    arrived = row_exchange(outgoing)
    pictures, back = pl.pallas_call(
        bind(render_kernel, 0, capacity, capacity, False),
        out_shape=[pltpu.VMEM(photos.shape, f32), shape((owners, up8(9 * capacity), BLOCK))],
        in_specs=[VM, SM, SM, VM, VM],
        out_specs=[VM, VM],
        scratch_shapes=render_scratch,
        compiler_params=grant(17),
    )(*near_core(arrived), corners, asked, depth_order, photos)
    own = gather(0, capacity, row_exchange(back))
    near, far, cross = exchange(own)
    leaving = pltpu.HBM((3, P_SIZE, MIGH * BLOCK), f32)
    current, moment_one, moment_two, outgoing, left, right = pl.pallas_call(
        bind(update_kernel, capacity),
        out_shape=kept + [shape((owners, up8(9 * capacity), BLOCK)), leaving, leaving],
        in_specs=[VM] * 7 + [SM] * 3,
        out_specs=[VM] * 6,
        scratch_shapes=[cams, dense, dense, table],
        compiler_params=grant(12),
    )(
        *near_core(own, near, far, cross, params), *in_hbm(first_moment, second_moment), camera, asked, migration,
    )
    arrived = row_exchange(outgoing)
    below = turn(right, "row", 1)
    above = turn(left, "row", -1)
    pictures, back = second(arrived, pictures)
    own = gather(1, slots, row_exchange(back))
    near, far, cross = exchange(own)
    current, moment_one, moment_two = pl.pallas_call(
        final_kernel,
        out_shape=state,
        in_specs=[VM] * 9 + [SM],
        out_specs=[ANY] * 3,
        scratch_shapes=[
            cams, dense, dense, *[pltpu.VMEM(params.shape, f32)] * 3,
            pltpu.SemaphoreType.DMA((3, len(row_groups()))),
        ],
        compiler_params=grant(16),
    )(
        *near_core(own, near, far, cross, current, moment_one), *in_hbm(moment_two, below, above),
        *in_hbm(migration),
    )
    return current, moment_one, moment_two, jnp.swapaxes(pictures, 2, 3)


def solution(mesh):
    return jax.shard_map(
        local,
        mesh=mesh,
        in_specs=(
            P(None, "row"),
            P(None, "row"),
            P(None, "row"),
            P(None, "rep", None),
            P(None, "rep", "row", None),
            P(None, "rep", "row", None),
            P(None, "rep", "row", None),
            P(None, "rep", "row", None),
            P(None, "rep", "row", None, None),
            P("row", None, None),
        ),
        out_specs=(
            P(None, "row"),
            P(None, "row"),
            P(None, "row"),
            P(None, "rep", "row", None, None),
        ),
        check_vma=False,
    )
```
